32 devices in a mesh: shard: 4 (over z), ctx: 4 (over x, core), tp: 2 (over y).
Axes of the slice: x: 2, y: 2, z: 4, core: 2. Of those that a mesh axis runs over, the one named last changes fastest.
Arguments:
- tokens: bfloat16 [4, 2048, 768], P('shard', 'ctx'), may hold values from -6 to 6
- cotangent: bfloat16 [4, 2048, 768], P('shard', 'ctx'), may hold values from -6 to 6
- neighbours: bfloat16 [4, 64, 128, 768], P('shard', 'ctx'), may hold values from -6 to 6
- neighbour_ids: int32 [4, 32, 2], P('shard', 'ctx'), may hold values from 0 to 15
- norm_gains: float32 [3, 768], replicated, may hold values from 0.1 to 1.9
- norm_shifts: float32 [3, 768], replicated, may hold values from -3 to 3
- head_bias: float32 [4, 768], P(None, 'tp'), may hold values from -3 to 3
- out_bias: float32 [3, 768], replicated, may hold values from -3 to 3
- up_bias: float32 [3072], P('tp'), may hold values from -3 to 3
- self_input: bfloat16 [768, 3, 768], P('shard', None, 'tp'), may hold values from -0.3125 to 0.3125
- self_output: bfloat16 [768, 768], P('tp', 'shard'), may hold values from -0.625 to 0.625
- cross_query: bfloat16 [768, 768], P('shard', 'tp'), may hold values from -0.3125 to 0.3125
- cross_memory: bfloat16 [768, 2, 768], P('shard', None, 'tp'), may hold values from -0.3125 to 0.3125
- cross_output: bfloat16 [768, 768], P('tp', 'shard'), may hold values from -0.3125 to 0.3125
- hidden_up: bfloat16 [768, 3072], P('shard', 'tp'), may hold values from -0.21875 to 0.21875
- hidden_down: bfloat16 [3072, 768], P('tp', 'shard'), may hold values from -0.15625 to 0.15625
Outputs:
- layer_output: bfloat16 [4, 2048, 768], P('shard', 'ctx')
- grad_tokens: float32 [4, 2048, 768], P('shard', 'ctx')
- grad_neighbours: float32 [4, 64, 128, 768], P('shard', 'ctx', None, 'tp')
- grad_norm_gains: float32 [3, 768], replicated
- grad_norm_shifts: float32 [3, 768], replicated
- grad_head_bias: float32 [4, 768], P(None, 'tp')
- grad_out_bias: float32 [3, 768], replicated
- grad_up_bias: float32 [3072], P('tp')
- grad_self_input: float32 [768, 3, 768], P('shard', None, 'tp')
- grad_self_output: float32 [768, 768], P('tp', 'shard')
- grad_cross_query: float32 [768, 768], P('shard', 'tp')
- grad_cross_memory: float32 [768, 2, 768], P('shard', None, 'tp')
- grad_cross_output: float32 [768, 768], P('tp', 'shard')
- grad_hidden_up: float32 [768, 3072], P('shard', 'tp')
- grad_hidden_down: float32 [3072, 768], P('tp', 'shard')
The draws below stay inside these ranges and needn't reach their ends.
Inputs may be any that keep to these rules, and one draw needn't show every extreme that they name: Stretch c of a sequence reads bank stretches floor(c / 8) * 16 + neighbour_ids[c, p]: the 16 bank stretches that lie beside its own block of 512 positions.
All inputs are finite; a program needn't handle non-finite values.
Results may differ from the reference program's by a relative error of at most 0.025.
Values may be sent and summed in bfloat16 or wider, within the bound.
A program may use at most 192 MiB of HBM per device.

```python
import jax
import jax.numpy as jnp
from jax import lax

D = 768
HEADS = 12
HEAD_DIM = 64
FF = 3072
STRETCH = 64
NBR_LEN = 128
PICKS = 2
BLOCK = 256
LENGTH = 2048
SEQ_ALL = 4
STRETCHES = 32
CH_DEV = 8
NB_DEV = 16
NB_ALL = 64


def place_ends(array, stream_key, smallest, largest):
    longest = array.shape.index(max(array.shape))
    spots = []
    for shift in (0, 1):
        where = [jax.random.randint(jax.random.fold_in(stream_key, axis), (), 0, length) for axis, length in enumerate(array.shape)]
        where[longest] = (where[longest] + shift) % array.shape[longest]
        spots.append(tuple(where))
    return array.at[spots[0]].set(smallest).at[spots[1]].set(largest)


def levels(key, extent, shards, low, largest):
    def one(position, shards_of):
        steps = jax.random.uniform(jax.random.fold_in(jax.random.fold_in(key, 6), position), (shards_of,), jnp.float32, low / len(shards), largest / len(shards))
        return jnp.repeat(jnp.exp(steps), extent[position] // shards_of).reshape((-1,) + (1,) * (len(extent) - position - 1))

    loudness = one(*shards[0])
    for cut in shards[1:]:
        loudness = loudness * one(*cut)
    return loudness


def normal_values(stream_key, extent, width, bound, shards=(), kind=jnp.bfloat16):
    result = jax.random.normal(stream_key, extent, jnp.float32) * width
    if len(shards) > 0:
        result = levels(stream_key, extent, shards, -0.22, 0.18) * result
    return jnp.clip(result, min=-bound, max=bound).astype(kind)


def setup_inputs(seed: int = 0) -> dict:
    arg_keys = jax.random.split(jax.random.key(seed), 17)
    tokens = normal_values(arg_keys[0], (SEQ_ALL, LENGTH, D), 1.0, 6.0, ((0, 4), (1, 4)))
    cotangent = normal_values(arg_keys[1], (SEQ_ALL, LENGTH, D), 1.0, 6.0, ((0, 4), (1, 4)))
    neighbours = normal_values(arg_keys[2], (SEQ_ALL, NB_ALL, NBR_LEN, D), 1.0, 6.0, ((0, 4), (1, 4)))
    neighbour_ids = place_ends(jax.random.randint(arg_keys[3], (SEQ_ALL, STRETCHES, PICKS), 0, NB_DEV), jax.random.fold_in(arg_keys[3], 1), 0, NB_DEV - 1).astype(jnp.int32)
    norm_gains = jnp.clip(1.0 + 0.18 * jax.random.normal(arg_keys[4], (3, D), jnp.float32), 0.1, 1.9)
    norm_shifts = normal_values(arg_keys[5], (3, D), 0.5, 3.0, (), jnp.float32)
    head_bias = normal_values(arg_keys[6], (4, D), 0.5, 3.0, ((1, 2),), jnp.float32)
    out_bias = normal_values(arg_keys[7], (3, D), 0.5, 3.0, (), jnp.float32)
    up_bias = normal_values(arg_keys[8], (FF,), 0.5, 3.0, ((0, 2),), jnp.float32)
    self_input = normal_values(arg_keys[9], (D, 3, D), (D // 2) ** -0.5, 0.3125, ((0, 4), (2, 2)))
    self_output = normal_values(arg_keys[10], (D, D), (D // 8) ** -0.5, 0.625, ((0, 2), (1, 4)))
    cross_query = normal_values(arg_keys[11], (D, D), (D // 2) ** -0.5, 0.3125, ((0, 4), (1, 2)))
    cross_memory = normal_values(arg_keys[12], (D, 2, D), (D // 2) ** -0.5, 0.3125, ((0, 4), (2, 2)))
    cross_output = normal_values(arg_keys[13], (D, D), (D // 2) ** -0.5, 0.3125, ((0, 2), (1, 4)))
    hidden_up = normal_values(arg_keys[14], (D, FF), D ** -0.5, 0.21875, ((0, 4), (1, 2)))
    hidden_down = normal_values(arg_keys[15], (FF, D), (FF // 2) ** -0.5, 0.15625, ((0, 2), (1, 4)))
    return {"tokens": tokens, "cotangent": cotangent, "neighbours": neighbours, "neighbour_ids": neighbour_ids, "norm_gains": norm_gains, "norm_shifts": norm_shifts, "head_bias": head_bias, "out_bias": out_bias, "up_bias": up_bias, "self_input": self_input, "self_output": self_output, "cross_query": cross_query, "cross_memory": cross_memory, "cross_output": cross_output, "hidden_up": hidden_up, "hidden_down": hidden_down}


@jax.custom_vjp
def low(v):
    return lax.optimization_barrier(v.astype(jnp.bfloat16)).astype(jnp.float32)

@jax.custom_vjp
def low_back(v):
    return v

def low_keep(v):
    return (low(v), None)

def low_pass(kept, grad):
    return (grad,)

def back_keep(v):
    return (v, None)

def back_low(kept, grad):
    return (low(grad),)
low.defvjp(low_keep, low_pass)
low_back.defvjp(back_keep, back_low)
EPSILON = 1e-05
NEGATIVE = -1e+30
HIGHEST = lax.Precision.HIGHEST

def layer_norm(values, gain, shift):
    centre = values - lax.optimization_barrier(jnp.mean(values, axis=-1, keepdims=True))
    spread = lax.optimization_barrier(jnp.mean(centre * centre, axis=-1, keepdims=True))
    return centre * lax.rsqrt(spread + EPSILON) * gain + shift

def product(left, right):
    return jnp.dot(left, right, precision=HIGHEST)

def self_block(key_heads, value_heads, item):
    queries, start = item
    count = queries.shape[0]
    scores = jnp.einsum('qhe,khe->hqk', queries, key_heads, precision=HIGHEST) * HEAD_DIM ** (-0.5)
    query_pos = start + jnp.arange(count, dtype=jnp.int32)
    key_pos = jnp.arange(key_heads.shape[0], dtype=jnp.int32)
    allowed = (key_pos // BLOCK)[None, :] <= (query_pos // BLOCK)[:, None]
    scores = low_back(jnp.where(allowed[None], scores, NEGATIVE))
    weights = jax.nn.softmax(scores, axis=-1)
    return jnp.einsum('hqk,khe->qhe', low(weights), value_heads, precision=HIGHEST)

def layer(params, stream, memory, chosen_ids):
    gains, shifts, head_bias, out_bias, up_bias, self_input, self_output, cross_query, cross_memory, cross_output, hidden_up, hidden_down = params
    scale = HEAD_DIM ** (-0.5)
    normed_one = low(layer_norm(stream, gains[0], shifts[0]))
    queries = low_back(low(product(normed_one, self_input[:, 0, :]) + head_bias[0]))
    keys = low_back(low(product(normed_one, self_input[:, 1, :])))
    values = low_back(low(product(normed_one, self_input[:, 2, :]) + head_bias[1]))
    count = min(512, LENGTH)
    blocks = queries.reshape(LENGTH // count, count, HEADS, HEAD_DIM)
    starts = jnp.arange(LENGTH // count, dtype=jnp.int32) * count
    key_heads = keys.reshape(LENGTH, HEADS, HEAD_DIM)
    value_heads = values.reshape(LENGTH, HEADS, HEAD_DIM)
    block_fn = jax.checkpoint(self_block)
    attended = lax.map(lambda item: block_fn(key_heads, value_heads, item), (blocks, starts))
    attended = low_back(low(attended.reshape(LENGTH, D)))
    first = stream + low_back(product(attended, self_output)) + out_bias[0]
    normed_two = low(layer_norm(first, gains[1], shifts[1]))
    cross_queries = low_back(low(product(normed_two, cross_query) + head_bias[2]))
    memory_rows = memory.reshape(NB_ALL * NBR_LEN, D)
    memory_keys = low_back(low(product(memory_rows, cross_memory[:, 0, :])))
    memory_values = low_back(low(product(memory_rows, cross_memory[:, 1, :]) + head_bias[3]))
    chooser = (chosen_ids.reshape(STRETCHES * PICKS, 1) == jnp.arange(NB_ALL, dtype=jnp.int32)[None, :]).astype(jnp.float32)
    chosen_keys = product(chooser, memory_keys.reshape(NB_ALL, NBR_LEN * D)).reshape(STRETCHES, PICKS * NBR_LEN, HEADS, HEAD_DIM)
    chosen_values = product(chooser, memory_values.reshape(NB_ALL, NBR_LEN * D)).reshape(STRETCHES, PICKS * NBR_LEN, HEADS, HEAD_DIM)
    cross_heads = cross_queries.reshape(STRETCHES, STRETCH, HEADS, HEAD_DIM)
    cross_scores = low_back(jnp.einsum('cqhe,ckhe->chqk', cross_heads, chosen_keys, precision=HIGHEST) * scale)
    cross_weights = jax.nn.softmax(cross_scores, axis=-1)
    cross_mixed = jnp.einsum('chqk,ckhe->cqhe', low(cross_weights), chosen_values, precision=HIGHEST)
    cross_mixed = low_back(low(cross_mixed.reshape(LENGTH, D)))
    second = first + low_back(product(cross_mixed, cross_output)) + out_bias[1]
    normed_three = low(layer_norm(second, gains[2], shifts[2]))
    hidden = low_back(product(normed_three, hidden_up) + up_bias)
    active = low(jax.nn.gelu(hidden, approximate=True))
    return second + low_back(product(active, hidden_down)) + out_bias[2]

def reference(tokens, cotangent, neighbours, neighbour_ids, norm_gains, norm_shifts, head_bias, out_bias, up_bias, self_input, self_output, cross_query, cross_memory, cross_output, hidden_up, hidden_down):
    params = tuple((entry.astype(jnp.float32) for entry in (norm_gains, norm_shifts, head_bias, out_bias, up_bias, self_input, self_output, cross_query, cross_memory, cross_output, hidden_up, hidden_down)))
    offsets = (jnp.arange(STRETCHES, dtype=jnp.int32) // CH_DEV * NB_DEV)[:, None]

    def one_sequence(totals, item):
        stream, upstream, memory, picked = item
        chosen_ids = offsets + picked
        output, pull = jax.vjp(lambda weights, inputs, banked: layer(weights, inputs, banked, chosen_ids), params, stream.astype(jnp.float32), memory.astype(jnp.float32))
        grad_params, grad_stream, grad_memory = pull(upstream.astype(jnp.float32))
        totals = jax.tree.map(jnp.add, totals, grad_params)
        return (totals, (output.astype(jnp.bfloat16), grad_stream, grad_memory))
    zeros = jax.tree.map(jnp.zeros_like, params)
    totals, stacked = lax.scan(one_sequence, zeros, (tokens, cotangent, neighbours, neighbour_ids))
    outputs, grad_tokens, grad_neighbours = stacked
    grad_gains, grad_shifts, grad_head, grad_out, grad_up_bias, grad_self_in, grad_self_out, grad_cross_q, grad_cross_mem, grad_cross_out, grad_up, grad_down = totals
    return (outputs, grad_tokens, grad_neighbours, grad_gains, grad_shifts, grad_head, grad_out, grad_up_bias, grad_self_in, grad_self_out, grad_cross_q, grad_cross_mem, grad_cross_out, grad_up, grad_down)
```

```python
from functools import partial

import jax
import jax.numpy as jnp
from jax import lax
from jax.experimental import pallas as pl
from jax.experimental.pallas import tpu as pltpu
from jax.sharding import PartitionSpec as P

HEAD_DIM = 64
BLOCK = 256


EPSILON = 1e-05
NEGATIVE = -1e30
HIGHEST = lax.Precision.HIGHEST


GROUP = 8
MESH = pl.DeviceIdType.MESH


def aligned(index, size):
    return pl.multiple_of(index * size, size)


def remote(src, dst, send, recv, where):
    return pltpu.make_async_remote_copy(
        src_ref=src, dst_ref=dst, send_sem=send, recv_sem=recv, device_id=where, device_id_type=MESH
    )


def greet(n_s, n_x, s, x, core, extra=()):
    barrier = pltpu.get_barrier_semaphore()

    def hello(where):
        pl.semaphore_signal(barrier, inc=1, device_id=where, device_id_type=MESH)

    for step in range(1, n_x):
        hello({"ctx": lax.rem(x + step, n_x) * 2 + core})
    hello({"ctx": x * 2 + 1 - core})
    for where in extra:
        hello(where)
    for step in range(1, n_s):
        hello({"shard": lax.rem(s + step, n_s)})
    pl.semaphore_wait(barrier, n_x + len(extra) + n_s - 1)


LOG2E = 1.4426950408889634
TILE = 128


def dot_nn(left, right):
    return lax.dot_general(left, right, (((1,), (0,)), ((), ())), preferred_element_type=jnp.float32)


def dot_nt(left, right):
    return lax.dot_general(left, right, (((1,), (1,)), ((), ())), preferred_element_type=jnp.float32)


def dot_tn(left, right):
    return lax.dot_general(left, right, (((0,), (0,)), ((), ())), preferred_element_type=jnp.float32)


def joined(ref, low, high):
    return jnp.concatenate([ref[index] for index in range(low, high)], axis=1)


def norm_parts(values):
    centre = values - jnp.mean(values, axis=-1, keepdims=True)
    spread = jnp.mean(centre * centre, axis=-1, keepdims=True)
    rate = lax.rsqrt(spread + EPSILON)
    return centre * rate, rate


def norm_rows(values, gain, shift):
    return (norm_parts(values)[0] * gain + shift).astype(jnp.bfloat16)


def half_masks(shape):
    lane = lax.broadcasted_iota(jnp.int32, shape, len(shape) - 1)
    return lane < HEAD_DIM


def keep_half(values, low, half):
    zero = jnp.zeros_like(values)
    return jnp.where(low, values, zero) if half == 0 else jnp.where(low, zero, values)


def attend(c, q, k, v, att, lse, scores, after):
    slabs, length, unused = q.shape
    scale = HEAD_DIM ** (-0.5) * LOG2E
    low = half_masks((BLOCK, TILE))
    lane = lax.broadcasted_iota(jnp.int32, (BLOCK, TILE), 1)
    per = length // BLOCK
    lse[...] = jnp.zeros_like(lse)

    def one(step, carry):
        p, qb = lax.div(step, per), lax.rem(step, per)
        rows = pl.ds(pl.multiple_of(qb * BLOCK, BLOCK), BLOCK)
        block_q = q[p, rows, :]
        parts = [keep_half(block_q, low, half) for half in (0, 1)]
        count = c * per + qb + 1

        def first(j, peaks):
            keys = k[p, pl.ds(pl.multiple_of(j * BLOCK, BLOCK), BLOCK), :]
            out = []
            for half in (0, 1):
                s = dot_nt(parts[half], keys) * scale
                scores[half, j] = s
                best = peaks[half]
                for at in range(0, BLOCK, TILE):
                    best = jnp.maximum(best, s[:, at : at + TILE])
                out.append(best)
            return tuple(out)

        start = jnp.full((BLOCK, TILE), NEGATIVE, jnp.float32)
        peaks = lax.fori_loop(0, count, first, (start, start))
        tops = [jnp.max(peak, axis=1, keepdims=True) for peak in peaks]

        def second(j, state):
            values = v[p, pl.ds(pl.multiple_of(j * BLOCK, BLOCK), BLOCK), :]
            out = []
            for half in (0, 1):
                total, mixed = state[half]
                raised = jnp.exp2(scores[half, j] - tops[half])
                for at in range(0, BLOCK, TILE):
                    total = total + raised[:, at : at + TILE]
                mixed = mixed + dot_nn(raised.astype(jnp.bfloat16), values)
                out.append((total, mixed))
            return tuple(out)

        zero = jnp.zeros((BLOCK, TILE), jnp.float32)
        state = lax.fori_loop(0, count, second, ((zero, zero), (zero, zero)))
        outs = []
        logs = lse[rows, :]
        for half in (0, 1):
            total = jnp.sum(state[half][0], axis=1, keepdims=True)
            outs.append(state[half][1] / total)
            logs = jnp.where(lane == p * 2 + half, tops[half] + jnp.log2(total), logs)
        lse[rows, :] = logs
        att[p, rows, :] = jnp.where(low, outs[0], outs[1]).astype(jnp.bfloat16)
        after(step)
        return carry

    lax.fori_loop(0, slabs * per, one, 0)


def front_kernel(
    n_s, n_c, shard_ref, tok_ref, gains, shifts, bias, w_ref, q, k_out, v_out, att, lse,
    t_ref, normed, scores, own_sem, zs, zr, xs, xr, cs, cr, txs, txr, tcs, tcr,
):
    s, c = lax.axis_index("shard"), lax.axis_index("ctx")
    n_x = n_c // 2
    x, core = lax.div(c, 2), lax.rem(c, 2)
    sibling_index = x * 2 + 1 - core
    sibling = {"ctx": sibling_index}
    total, rows, unused = shard_ref.shape
    length, width = tok_ref.shape
    chunks, part = total // GROUP, GROUP // n_c
    slabs = q.shape[0]
    greet(n_s, n_x, s, x, core)

    def token_rows(index):
        return t_ref.at[pl.ds(aligned(index, length), length), :]

    own_shard = pltpu.make_async_copy(shard_ref, w_ref.at[:, pl.ds(aligned(s, rows), rows), :], own_sem.at[0])
    own_shard.start()

    def token_x(d):
        peer = lax.rem(x + d, n_x)
        return remote(tok_ref, token_rows(c), txs.at[d - 1], txr.at[d - 1], {"ctx": peer * 2 + core}), peer > x

    def token_x_in(d):
        src = lax.rem(x - d + n_x, n_x)
        rows_in = token_rows(src * 2 + core)
        return remote(rows_in, rows_in, txs.at[d - 1], txr.at[d - 1], sibling), src < x

    def token_relay(d):
        src = lax.rem(x - d + n_x, n_x)
        rows_in = token_rows(src * 2 + core)
        return remote(rows_in, rows_in, tcs.at[d], tcr.at[d], sibling), src < x

    def token_relay_in(d):
        src = lax.rem(x - d + n_x, n_x)
        rows_in = token_rows(src * 2 + 1 - core)
        return remote(rows_in, rows_in, tcs.at[d], tcr.at[d], sibling), src < x

    token_core = remote(tok_ref, token_rows(c), tcs.at[0], tcr.at[0], sibling)

    def run(pair, method):
        copy, valid = pair
        pl.when(valid)(lambda: getattr(copy, method)())

    for d in range(1, n_x):
        run(token_x(d), "start")
    run((token_core, core == 0), "start")

    def block(origin, k, quarter):
        return w_ref.at[pl.ds((k * n_c + quarter) * part, part), pl.ds(aligned(origin, rows), rows), :]

    def own_block(k):
        return shard_ref.at[pl.ds((k * n_c + c) * part, part)]

    def origin_of(way, t):
        return s - 1 - t if way == 0 else s + 1 + t

    def arrives(way, t):
        return s - 1 - t >= 0 if way == 0 else s + 1 + t <= n_s - 1

    def onward(way):
        return s + 1 <= n_s - 1 if way == 0 else s >= 1

    def target(way):
        return {"shard": lax.min(s + 1, n_s - 1)} if way == 0 else {"shard": lax.max(s - 1, 0)}

    slots = [(way, t) for t in range(n_s - 1) for way in (0, 1)]

    def send_own(k):
        for way in (0, 1):
            copy = remote(own_block(k), block(s, k, c), zs.at[way, k, 0], zr.at[way, k, 0], target(way))
            pl.when(onward(way))(copy.start)

    def z_in(way, t, k):
        here = block(origin_of(way, t), k, c)
        return remote(here, here, zs.at[way, k, t], zr.at[way, k, t], target(way))

    def z_out(way, t, k):
        here = block(origin_of(way, t), k, c)
        return remote(here, here, zs.at[way, k, t + 1], zr.at[way, k, t + 1], target(way))

    def x_out(slot, way, t, k, d):
        here = block(origin_of(way, t), k, c)
        peer = lax.rem(x + d, n_x) * 2 + core
        return remote(here, here, xs.at[k, slot, d - 1], xr.at[k, slot, d - 1], {"ctx": peer})

    def x_in(slot, way, t, k, d):
        here = block(origin_of(way, t), k, lax.rem(x - d + n_x, n_x) * 2 + core)
        return remote(here, here, xs.at[k, slot, d - 1], xr.at[k, slot, d - 1], sibling)

    def core_out(slot, way, t, k, d):
        here = block(origin_of(way, t), k, lax.rem(x - d + n_x, n_x) * 2 + core)
        return remote(here, here, cs.at[k, slot, d], cr.at[k, slot, d], sibling)

    def core_in(slot, way, t, k, d):
        here = block(origin_of(way, t), k, lax.rem(x - d + n_x, n_x) * 2 + 1 - core)
        return remote(here, here, cs.at[k, slot, d], cr.at[k, slot, d], sibling)

    send_own(0)

    def norm_block(source, j):
        def tile(i, carry):
            at = pl.ds(pl.multiple_of(i * TILE, TILE), TILE)
            normed[j, at, :] = norm_rows(source(at).astype(jnp.float32), gains[0:1, :], shifts[0:1, :])
            return carry

        lax.fori_loop(0, length // TILE, tile, 0)

    def advance(i):
        @pl.when(i + 1 < chunks)
        def _():
            send_own(i + 1)

        for slot, (way, t) in enumerate(slots):
            now = i - t

            @pl.when(arrives(way, t) & (now < chunks) & (now >= 0))
            def _():
                z_in(way, t, now).wait_recv()
                if t + 1 < n_s - 1:
                    pl.when(onward(way))(z_out(way, t, now).start)
                for d in range(1, n_x):
                    x_out(slot, way, t, now, d).start()
                core_out(slot, way, t, now, 0).start()

            @pl.when(arrives(way, t) & (now > 0) & (now <= chunks))
            def _():
                for d in range(1, n_x):
                    x_in(slot, way, t, now - 1, d).wait_recv()
                    core_out(slot, way, t, now - 1, d).start()

    def advance_loop(i, carry):
        advance(i)
        return carry

    def complete(k, carry):
        for slot, (way, t) in enumerate(slots):

            @pl.when(arrives(way, t))
            def _():
                for d in range(n_x):
                    core_in(slot, way, t, k, d).wait_recv()

        return carry

    norm_block(lambda at: tok_ref[at, :], c)
    lax.fori_loop(0, 2, advance_loop, 0)
    for d in range(1, n_x):
        run(token_x_in(d), "wait_recv")
        run(token_relay(d), "start")
    lax.fori_loop(2, n_s, advance_loop, 0)
    for d in range(1, n_x):
        run(token_relay_in(d), "wait_recv")
    incoming = token_rows(sibling_index)
    run((remote(incoming, incoming, tcs.at[0], tcr.at[0], sibling), core == 1), "wait_recv")

    def norm_other(j, carry):
        norm_block(lambda at: t_ref[pl.ds(pl.multiple_of(j * length + at.start, TILE), TILE), :], j)
        return carry

    lax.fori_loop(0, c, norm_other, 0)
    advance(n_s)
    own_shard.wait()
    first_chunks = -(-3 * slabs // GROUP)
    lax.fori_loop(0, first_chunks, complete, 0)

    def project(j, which, row_bias):
        weight = joined(w_ref, which * slabs, (which + 1) * slabs)
        result = dot_nn(normed[j], weight)
        if row_bias is not None:
            result = result + row_bias
        return result.astype(jnp.bfloat16)

    def project_keys(j, carry):
        spot = pl.ds(pl.multiple_of(j * length, length), length)
        for which, target, row_bias in ((1, k_out, None), (2, v_out, bias[1:2, :])):
            result = project(j, which, row_bias)
            for p in range(slabs):
                target[p, spot, :] = result[:, p * TILE : (p + 1) * TILE]
        return carry

    lax.fori_loop(0, c + 1, project_keys, 0)
    queries = project(c, 0, bias[0:1, :])
    for p in range(slabs):
        q[p] = queries[:, p * TILE : (p + 1) * TILE]
    last = chunks + n_s - 1
    pieces = slabs * (length // BLOCK)

    def after(step):
        pl.when(n_s + 1 + step < last)(lambda: advance(n_s + 1 + step))

    attend(c, q, k_out, v_out, att, lse, scores, after)
    lax.fori_loop(min(n_s + 1 + pieces, last), last, advance_loop, 0)
    lax.fori_loop(first_chunks, chunks, complete, 0)

    def finish(k, carry):
        for way in (0, 1):
            pl.when(onward(way))(
                remote(own_block(k), block(s, k, c), zs.at[way, k, 0], zr.at[way, k, 0], target(way)).wait_send
            )
        for slot, (way, t) in enumerate(slots):

            @pl.when(arrives(way, t))
            def _():
                if t + 1 < n_s - 1:
                    pl.when(onward(way))(z_out(way, t, k).wait_send)
                for d in range(1, n_x):
                    x_out(slot, way, t, k, d).wait_send()
                for d in range(n_x):
                    core_out(slot, way, t, k, d).wait_send()

        return carry

    lax.fori_loop(0, chunks, finish, 0)
    for d in range(1, n_x):
        run(token_x(d), "wait_send")
        run(token_relay(d), "wait_send")
    run((token_core, core == 0), "wait_send")


def front(shard, tok, gains, shifts, bias, n_s, n_c):
    total, rows, unused = shard.shape
    length, width = tok.shape
    slabs = bias.shape[1] // TILE
    chunks, n_x, slots = total // GROUP, n_c // 2, 2 * (n_s - 1)
    dma, shape, scratch = pltpu.SemaphoreType.DMA, jax.ShapeDtypeStruct, pltpu.VMEM
    vmem = pl.BlockSpec(memory_space=pltpu.VMEM)
    bf16, f32 = jnp.bfloat16, jnp.float32
    return pl.pallas_call(
        partial(front_kernel, n_s, n_c),
        out_shape=(
            shape((total, rows * n_s, TILE), bf16),
            shape((slabs, length, TILE), bf16),
            shape((slabs, length * n_c, TILE), bf16),
            shape((slabs, length * n_c, TILE), bf16),
            shape((slabs, length, TILE), bf16),
            shape((length, TILE), f32),
        ),
        in_specs=[vmem] * 5,
        out_specs=(vmem,) * 6,
        scratch_shapes=[
            scratch((length * n_c, width), bf16), scratch((n_c, length, width), bf16),
            scratch((2, length * n_c // BLOCK, BLOCK, BLOCK), f32),
            dma((1,)),
            dma((2, chunks, n_s - 1)), dma((2, chunks, n_s - 1)),
            dma((chunks, slots, n_x - 1)), dma((chunks, slots, n_x - 1)),
            dma((chunks, slots, n_x)), dma((chunks, slots, n_x)),
            dma((n_x - 1,)), dma((n_x - 1,)), dma((n_x,)), dma((n_x,)),
        ],
        compiler_params=pltpu.CompilerParams(collective_id=0, has_side_effects=True, vmem_limit_bytes=60 << 20),
        name="front",
    )(shard, tok, gains, shifts, bias)


def rows_at(index, size):
    return pl.ds(pl.multiple_of(index * size, size), size)


def chain_kernel(
    at, chunk, banks, ids, att, tok, cot, bank, w, gains, shifts, bias, out_bias, up_bias,
    n2, n3, sl, fl, act, gh, mx, gcq, ga, dks, dvs, gfirst, result, sums, up_sums, head_sums,
    mem_k, mem_v, first, second, gsecond, weights, gmix, cq, tx, rx, ss, rs,
):
    tp = lax.axis_index("tp")
    peer = {"tp": 1 - tp}
    barrier = pltpu.get_barrier_semaphore()
    pl.semaphore_signal(barrier, inc=1, device_id=peer, device_id_type=MESH)
    pl.semaphore_wait(barrier, 1)
    f32, bf16 = jnp.float32, jnp.bfloat16
    length, width = tok.shape
    slabs = att.shape[0]
    units = act.shape[0]
    span = bank.shape[0] // banks
    stretches, picks = ids.shape
    stretch = length // stretches
    keys_each = picks * span
    scale = HEAD_DIM ** (-0.5)
    count = length // chunk
    tiles = chunk // TILE
    low = half_masks((stretch, TILE))
    sums[...] = jnp.zeros_like(sums)
    up_sums[...] = jnp.zeros_like(up_sums)
    head_sums[...] = jnp.zeros_like(head_sums)

    def exchange(phase, r):
        rows = rows_at(r, chunk)
        return remote(tx.at[phase, rows, :], rx.at[phase, rows, :], ss.at[phase, r], rs.at[phase, r], peer)

    def every(stage):
        def run(r, carry):
            stage(r)
            return carry

        lax.fori_loop(0, count, run, 0)

    def per_tile(r, body):
        def run(i, carry):
            body(pl.ds(pl.multiple_of(r * chunk + i * TILE, TILE), TILE))
            return carry

        lax.fori_loop(0, tiles, run, 0)

    def out_product(phase, r, left, name, total):
        rows = rows_at(r, chunk)
        low_slab = at[name]
        step = 256

        def run(n, carry):
            cols = pl.ds(pl.multiple_of(n * step, step), step)
            weight = jnp.concatenate([w[low_slab + i, cols, :] for i in range(total)], axis=1)
            product = dot_nt(jnp.concatenate([left[i, rows, :] for i in range(total)], axis=1), weight)
            tx[phase, rows, cols] = product.astype(bf16)
            return carry

        lax.fori_loop(0, width // step, run, 0)

    def send_attended(r):
        out_product(0, r, att, "self_out", slabs)
        exchange(0, r).start()

    every(send_attended)

    def memory(i, carry):
        rows = rows_at(i, 4 * span)
        for which, target, row_bias in ((0, mem_k, None), (1, mem_v, bias[3:4, :])):
            base = at["memory"] + which * slabs
            product = dot_nn(bank[rows, :], joined(w, base, base + slabs))
            if row_bias is not None:
                product = product + row_bias
            product = product.astype(bf16)
            for p in range(slabs):
                for e in range(4):
                    target[p, i * 4 + e] = product[e * span : (e + 1) * span, p * TILE : (p + 1) * TILE]
        return carry

    lax.fori_loop(0, banks // 4, memory, 0)

    def narrow(source, r, base, row_bias, target):
        rows = rows_at(r, chunk)
        product = dot_nn(source[rows, :], joined(w, base, base + slabs))
        if row_bias is not None:
            product = product + row_bias
        product = product.astype(bf16)
        for p in range(slabs):
            target[p, rows, :] = product[:, p * TILE : (p + 1) * TILE]

    def picked(source, p, st):
        return jnp.concatenate(
            [source[p, ids[st, n]] for n in range(picks)], axis=0
        )

    def stacked(source, p, st):
        block = source[p, rows_at(st, stretch), :]
        return jnp.concatenate([keep_half(block, low, 0), keep_half(block, low, 1)], axis=0)

    def unstacked(both):
        return jnp.where(low, both[:stretch], both[stretch:])

    def total_of(phase, rows):
        return tx[phase, rows, :].astype(f32) + rx[phase, rows, :].astype(f32)

    def per_stretch(r, body):
        each = chunk // stretch

        def run(i, carry):
            p, inner = lax.div(i, each), lax.rem(i, each)
            body(p, r * each + inner)
            return carry

        lax.fori_loop(0, slabs * each, run, 0)

    def cross_forward(r):
        exchange(0, r).wait_recv()

        def tile(rows):
            value = tok[rows, :].astype(f32) + total_of(0, rows) + out_bias[0:1, :]
            first[rows, :] = value
            n2[rows, :] = norm_rows(value, gains[1:2, :], shifts[1:2, :])

        per_tile(r, tile)
        narrow(n2, r, at["cross_q"], bias[2:3, :], cq)

        def one(p, st):
            keys, values = picked(mem_k, p, st), picked(mem_v, p, st)
            s = dot_nt(stacked(cq, p, st), keys) * (scale * LOG2E)
            raised = jnp.exp2(s - jnp.max(s, axis=1, keepdims=True))
            probs = raised / jnp.sum(raised, axis=1, keepdims=True)
            weights[p, st] = probs
            mixed = dot_nn(probs.astype(bf16), values)
            mx[p, rows_at(st, stretch), :] = unstacked(mixed).astype(bf16)

        per_stretch(r, one)
        out_product(1, r, mx, "cross_out", slabs)
        exchange(1, r).start()

    every(cross_forward)
    curve = 0.7978845608028654
    cubic = 0.044715

    def feed(r):
        exchange(1, r).wait_recv()
        rows_all = rows_at(r, chunk)

        def tile(rows):
            value = first[rows, :] + total_of(1, rows) + out_bias[1:2, :]
            second[rows, :] = value
            n3[rows, :] = norm_rows(value, gains[2:3, :], shifts[2:3, :])

        per_tile(r, tile)

        def unit(j, carry):
            up = jnp.concatenate([w[at["up"] + 2 * j], w[at["up"] + 2 * j + 1]], axis=1)
            down = jnp.concatenate([w[at["down"] + 2 * j], w[at["down"] + 2 * j + 1]], axis=1)
            hidden = dot_nn(n3[rows_all, :], up) + up_bias[j]
            back = dot_nn(cot[rows_all, :], down)
            square = hidden * hidden
            bent = jnp.tanh(curve * hidden * (1.0 + cubic * square))
            half = 0.5 * (1.0 + bent)
            active = (hidden * half).astype(bf16)
            slope = half + 0.5 * hidden * (1.0 - bent * bent) * (curve * (1.0 + 3.0 * cubic * square))
            grad = (slope * back).astype(bf16)
            up_sums[j] = up_sums[j] + jnp.sum(grad.astype(f32), axis=0, keepdims=True)
            for i in range(2):
                lanes = slice(i * TILE, (i + 1) * TILE)
                act[2 * j + i, rows_all, :] = active[:, lanes]
                gh[2 * j + i, rows_all, :] = grad[:, lanes]
            return carry

        lax.fori_loop(0, units // 2, unit, 0)
        out_product(2, r, gh, "up", units)
        exchange(2, r).start()

    every(feed)

    def result_product(r):
        out_product(4, r, act, "down", units)

    every(result_product)

    def norm_back_rows(value, gain, upstream, row):
        spot, rate = norm_parts(value)
        scaled = upstream * gain
        sums[row : row + 1, :] = sums[row : row + 1, :] + jnp.sum(upstream * spot, axis=0, keepdims=True)
        sums[row + 3 : row + 4, :] = sums[row + 3 : row + 4, :] + jnp.sum(upstream, axis=0, keepdims=True)
        return rate * (
            scaled - jnp.mean(scaled, axis=-1, keepdims=True)
            - spot * jnp.mean(scaled * spot, axis=-1, keepdims=True)
        )

    def add_sum(row, values):
        sums[row : row + 1, :] = sums[row : row + 1, :] + jnp.sum(values, axis=0, keepdims=True)

    def cross_back(r):
        exchange(2, r).wait_recv()

        def tile(rows):
            upstream = cot[rows, :].astype(f32)
            grad = upstream + norm_back_rows(second[rows, :], gains[2:3, :], total_of(2, rows), 2)
            add_sum(8, upstream)
            add_sum(7, grad)
            gsecond[rows, :] = grad
            sl[rows, :] = grad.astype(bf16)

        per_tile(r, tile)
        narrow(sl, r, at["cross_out"], None, gmix)

        def one(p, st):
            keys, values = picked(mem_k, p, st), picked(mem_v, p, st)
            grads, queries = stacked(gmix, p, st), stacked(cq, p, st)
            probs = weights[p, st]
            spread = dot_nt(grads, values)
            ds = (probs * (spread - jnp.sum(probs * spread, axis=1, keepdims=True))).astype(bf16)
            back = unstacked(dot_nn(ds, keys)) * scale
            gcq[p, rows_at(st, stretch), :] = back.astype(bf16)
            dks[p, rows_at(st, keys_each), :] = (dot_tn(ds, queries) * scale).astype(bf16)
            dvs[p, rows_at(st, keys_each), :] = dot_tn(probs.astype(bf16), grads).astype(bf16)

        per_stretch(r, one)
        out_product(3, r, gcq, "cross_q", slabs)
        exchange(3, r).start()
        exchange(4, r).start()

    every(cross_back)

    def finish(r):
        exchange(3, r).wait_recv()

        def tile(rows):
            grad = gsecond[rows, :] + norm_back_rows(first[rows, :], gains[1:2, :], total_of(3, rows), 1)
            add_sum(6, grad)
            gfirst[rows, :] = grad
            fl[rows, :] = grad.astype(bf16)

        per_tile(r, tile)
        narrow(fl, r, at["self_out"], None, ga)

    every(finish)
    for p in range(slabs):
        head_sums[p] = jnp.sum(gcq[p].astype(f32), axis=0, keepdims=True)

    def output(r):
        exchange(4, r).wait_recv()

        def tile(rows):
            value = second[rows, :] + total_of(4, rows) + out_bias[2:3, :]
            result[rows, :] = value.astype(bf16)

        per_tile(r, tile)
        for phase in range(5):
            exchange(phase, r).wait_send()

    every(output)


def chain(at, ids, att, tok, cot, bank, w, gains, shifts, bias, out_bias, up_bias, banks, chunk):
    length, width = tok.shape
    slabs = att.shape[0]
    units = up_bias.shape[0] // TILE
    stretches, picks = ids.shape
    stretch, span = length // stretches, bank.shape[0] // banks
    keys_each = picks * span
    bf16, f32 = jnp.bfloat16, jnp.float32
    vmem, smem = pl.BlockSpec(memory_space=pltpu.VMEM), pl.BlockSpec(memory_space=pltpu.SMEM)
    shape = jax.ShapeDtypeStruct
    scratch = pltpu.VMEM
    row_slabs = shape((slabs, length, TILE), bf16)
    rows = shape((length, width), bf16)
    return pl.pallas_call(
        partial(chain_kernel, at, chunk, banks),
        out_shape=(
            rows, rows, rows, rows,
            shape((units, length, TILE), bf16), shape((units, length, TILE), bf16),
            row_slabs, row_slabs, row_slabs,
            shape((slabs, stretches * keys_each, TILE), bf16), shape((slabs, stretches * keys_each, TILE), bf16),
            shape((length, width), f32), rows,
            shape((16, width), f32), shape((units // 2, 1, 2 * TILE), f32), shape((slabs, 1, TILE), f32),
        ),
        in_specs=[smem] + [vmem] * 10,
        out_specs=(vmem,) * 16,
        scratch_shapes=[
            scratch((slabs, banks, span, TILE), bf16), scratch((slabs, banks, span, TILE), bf16),
            scratch((length, width), f32), scratch((length, width), f32), scratch((length, width), f32),
            scratch((slabs, stretches, 2 * stretch, keys_each), f32),
            scratch((slabs, length, TILE), bf16), scratch((slabs, length, TILE), bf16),
            scratch((5, length, width), bf16), scratch((5, length, width), bf16),
            pltpu.SemaphoreType.DMA((5, length // chunk)), pltpu.SemaphoreType.DMA((5, length // chunk)),
        ],
        compiler_params=pltpu.CompilerParams(collective_id=2, has_side_effects=True, vmem_limit_bytes=63 << 20),
        name="chain",
    )(ids, att, tok, cot, bank, w, gains, shifts, bias, out_bias, up_bias.reshape(units // 2, 1, 2 * TILE))


def bank_kernel(span, ids, dks, dvs, w, mg, mine, send, head_sums, acc):
    t = lax.axis_index("tp")
    f32, bf16 = jnp.float32, jnp.bfloat16
    slabs = dks.shape[0]
    stretches, picks = ids.shape
    acc[...] = jnp.zeros_like(acc)

    def add(i, carry):
        st, n = lax.div(i, picks), lax.rem(i, picks)
        rows = rows_at(ids[st, n], span)
        source = rows_at(i, span)
        for p in range(slabs):
            acc[p, rows, :] = acc[p, rows, :] + dks[p, source, :].astype(f32)
            acc[slabs + p, rows, :] = acc[slabs + p, rows, :] + dvs[p, source, :].astype(f32)
        return carry

    lax.fori_loop(0, stretches * picks, add, 0)
    half = mine.shape[1]
    total = jnp.zeros((1, slabs * TILE), f32)

    def one(i, sums):
        rows = rows_at(i, BLOCK)
        for p in range(2 * slabs):
            mg[p, rows, :] = acc[p, rows, :].astype(bf16)
        left = jnp.concatenate([mg[p, rows, :] for p in range(2 * slabs)], axis=1)
        for which, target in ((t, mine), (1 - t, send)):
            cols = pl.ds(pl.multiple_of(which * half, half), half)
            weight = jnp.concatenate([w[p, cols, :] for p in range(2 * slabs)], axis=1)
            target[rows, :] = dot_nt(left, weight).astype(target.dtype)
        return sums + jnp.sum(left[:, slabs * TILE :].astype(f32), axis=0, keepdims=True)

    total = lax.fori_loop(0, mine.shape[0] // BLOCK, one, total)
    for p in range(slabs):
        head_sums[p] = total[:, p * TILE : (p + 1) * TILE]


def bank_back(ids, dks, dvs, w, banks, span):
    slabs = dks.shape[0]
    rows, half = banks * span, w.shape[1] // 2
    bf16, f32 = jnp.bfloat16, jnp.float32
    vmem, smem = pl.BlockSpec(memory_space=pltpu.VMEM), pl.BlockSpec(memory_space=pltpu.SMEM)
    shape = jax.ShapeDtypeStruct
    return pl.pallas_call(
        partial(bank_kernel, span),
        out_shape=(
            shape((2 * slabs, rows, TILE), bf16), shape((rows, half), f32),
            shape((rows, half), bf16), shape((slabs, 1, TILE), f32),
        ),
        in_specs=[smem, vmem, vmem, vmem],
        out_specs=(vmem,) * 4,
        scratch_shapes=[pltpu.VMEM((2 * slabs, rows, TILE), f32)],
        compiler_params=pltpu.CompilerParams(vmem_limit_bytes=40 << 20),
        name="bank_back",
    )(ids, dks, dvs, w)


def tail_kernel(
    n_s, n_c, groups, early,
    q, k, v, up, att, lse, tok, norms, w, gfirst, small_in, bank, fl, n2, sl, n3, cot, mg, gcq, mx, gh, act,
    gtok, res, small_out,
    dk, dv, qm, um, lse_t, delta_t, dq_acc, dq, gk, gv, n1, core_in, x_in, tx, rx,
    xt, stage, gbuf, a_buf, b_buf, p_buf, zbuf_in, zbuf_out, sm_mine, sm_core, sm_x, sm_z,
    cs, cr, xs, xr, ts, tr, ds_, as_, ar, bs, br, zs, zr, fs, fr, hs, hr, ms, mr,
):
    f32, bf16 = jnp.float32, jnp.bfloat16
    s, c, t = lax.axis_index("shard"), lax.axis_index("ctx"), lax.axis_index("tp")
    n_x = n_c // 2
    x, core = lax.div(c, 2), lax.rem(c, 2)
    sibling, peer = {"ctx": x * 2 + 1 - core}, {"tp": 1 - t}
    slabs, length, unused = q.shape
    width = tok.shape[1]
    per = length // BLOCK
    scale = HEAD_DIM ** (-0.5)
    rows = width // n_s
    ring = gbuf.shape[0]
    p_ring = p_buf.shape[0]
    chunks = a_buf.shape[0]
    barrier = pltpu.get_barrier_semaphore()
    hellos = [{"ctx": lax.rem(x + step, n_x) * 2 + core} for step in range(1, n_x)]
    hellos += [{"shard": lax.rem(s + step, n_s)} for step in range(1, n_s)]
    hellos += [sibling, peer]
    for where in hellos:
        pl.semaphore_signal(barrier, inc=1, device_id=where, device_id_type=MESH)
    pl.semaphore_wait(barrier, len(hellos))

    def owner_rows(index):
        return pl.ds(pl.multiple_of(index * length, length), length)

    sources = {"self_in": n1, "memory": bank, "self_out": fl, "cross_q": n2, "cross_out": sl, "up": n3, "down": cot}

    def slab_of(name, index):
        if name == "self_in":
            return (dq, gk, gv)[index // slabs][index % slabs]
        return {"memory": mg, "self_out": att, "cross_q": gcq, "cross_out": mx, "up": gh, "down": act}[name][index]

    def turn(name):
        source = sources[name]
        if name == "self_in":

            def piece(i, carry):
                xt[:, rows_at(i, BLOCK)] = source[rows_at(i, BLOCK), :].T
                return carry

            lax.fori_loop(0, per, piece, 0)
            return
        total = source.shape[0] // BLOCK

        def fetch(i):
            slot = lax.rem(i, 2)
            return pltpu.make_async_copy(source.at[rows_at(i, BLOCK), :], stage.at[slot], ds_.at[slot])

        fetch(0).start()

        def piece(i, carry):
            fetch(i).wait()
            pl.when(i + 1 < total)(lambda: fetch(i + 1).start())
            xt[:, rows_at(i, BLOCK)] = stage[lax.rem(i, 2)].T
            return carry

        lax.fori_loop(0, total, piece, 0)

    order = [(name, index) for name, count in groups for index in range(count)]

    def produce(kk):
        slot = kk % ring
        if kk >= ring:
            for e in range(n_x):
                a_out(kk - ring, e).wait_send()
        at = 0
        while at < n_c:
            name, index = order[kk * n_c + at]
            if index == 0:
                turn(name)
            both = at + 1 < n_c and order[kk * n_c + at + 1][0] == name
            depth = bank.shape[0] if name == "memory" else length
            right = slab_of(name, index)
            if both:
                right = jnp.concatenate([right, slab_of(name, index + 1)], axis=1)
            product = dot_nn(xt[:, :depth], right).astype(bf16)
            gbuf[slot, at] = product[:, :TILE]
            if both:
                gbuf[slot, at + 1] = product[:, TILE:]
            at += 2 if both else 1
        for e in range(n_x):
            a_out(kk, e).start()

    def a_out(kk, e):
        slot = lax.rem(kk, ring)
        return remote(gbuf.at[slot, e * 2 + 1 - core], a_buf.at[kk, e], as_.at[kk, e], ar.at[kk, e], sibling)

    def b_out(kk, d):
        to = lax.rem(x + d, n_x)
        return remote(a_buf.at[kk, to], b_buf.at[kk, d - 1], bs.at[kk, d - 1], br.at[kk, d - 1], {"ctx": to * 2 + core})

    def stage_b(kk):
        slot = lax.rem(kk, ring)
        for d in range(1, n_x):
            e = lax.rem(x + d, n_x)
            a_out(kk, e).wait_recv()
            a_buf[kk, e] = (gbuf[slot, e * 2 + core].astype(f32) + a_buf[kk, e].astype(f32)).astype(bf16)
            b_out(kk, d).start()
        a_out(kk, x).wait_recv()
        p_buf[lax.rem(kk, p_ring)] = gbuf[slot, c].astype(f32) + a_buf[kk, x].astype(f32)

    def stage_sum(kk):
        slot = lax.rem(kk, p_ring)
        for d in range(1, n_x):
            b_out(kk, d).wait_recv()
            p_buf[slot] = p_buf[slot] + b_buf[kk, d - 1].astype(f32)

    def dest(way, m):
        return n_s - 1 - m if way == 0 else m

    def z_copy(way, m, kk):
        neighbour = lax.min(s + 1, n_s - 1) if way == 0 else lax.max(s - 1, 0)
        return remote(
            zbuf_out.at[way, kk, m], zbuf_in.at[way, kk, m], zs.at[way, kk, m], zr.at[way, kk, m], {"shard": neighbour}
        )

    def sends(way, m):
        return dest(way, m) > s if way == 0 else dest(way, m) < s

    def stage_z(way, kk):
        slot = lax.rem(kk, p_ring)
        inner = s > 0 if way == 0 else s < n_s - 1
        for m in range(n_s - 1):
            o = dest(way, m)

            @pl.when(sends(way, m))
            def _():
                piece = p_buf[slot, o * rows : (o + 1) * rows, :]

                @pl.when(inner)
                def _():
                    z_copy(way, m, kk).wait_recv()
                    zbuf_out[way, kk, m] = (piece + zbuf_in[way, kk, m].astype(f32)).astype(bf16)

                @pl.when(jnp.logical_not(inner))
                def _():
                    zbuf_out[way, kk, m] = piece.astype(bf16)

                z_copy(way, m, kk).start()

    def res_block(kk, quarter):
        return res.at[:, pl.ds(pl.multiple_of((kk * n_c + quarter) * TILE, TILE), TILE)]

    def f_out(kk, d):
        here = res_block(kk, c)
        return remote(here, here, fs.at[kk, d - 1], fr.at[kk, d - 1], {"ctx": lax.rem(x + d, n_x) * 2 + core})

    def f_in(kk, d):
        here = res_block(kk, lax.rem(x - d + n_x, n_x) * 2 + core)
        return remote(here, here, fs.at[kk, d - 1], fr.at[kk, d - 1], sibling)

    def h_out(kk, d):
        here = res_block(kk, lax.rem(x - d + n_x, n_x) * 2 + core)
        return remote(here, here, hs.at[kk, d], hr.at[kk, d], sibling)

    def h_in(kk, d):
        here = res_block(kk, lax.rem(x - d + n_x, n_x) * 2 + 1 - core)
        return remote(here, here, hs.at[kk, d], hr.at[kk, d], sibling)

    def stage_d(kk):
        own = pl.ds(aligned(s, rows), rows)
        slot = lax.rem(kk, p_ring)

        @pl.when(s > 0)
        def _():
            m = n_s - 1 - s
            z_copy(0, m, kk).wait_recv()
            p_buf[slot, own, :] = p_buf[slot, own, :] + zbuf_in[0, kk, m].astype(f32)

        @pl.when(s < n_s - 1)
        def _():
            z_copy(1, s, kk).wait_recv()
            p_buf[slot, own, :] = p_buf[slot, own, :] + zbuf_in[1, kk, s].astype(f32)

        res[:, pl.ds(pl.multiple_of((kk * n_c + c) * TILE, TILE), TILE)] = p_buf[slot, own, :].astype(bf16)
        for d in range(1, n_x):
            f_out(kk, d).start()
        h_out(kk, 0).start()

    def stage_e(kk):
        for d in range(1, n_x):
            f_in(kk, d).wait_recv()
            h_out(kk, d).start()

    def stage_f(kk):
        for d in range(n_x):
            h_in(kk, d).wait_recv()

    def during(i, lag, action):
        kk = i - lag

        @pl.when((kk >= 0) & (kk < chunks))
        def _():
            action(kk)

    def reduce_step(i, low, high):
        for kk in range(low, high):
            pl.when(i == kk)(partial(produce, kk))
        during(i, 1, stage_b)
        during(i, 2, stage_sum)
        during(i, 2 + s, partial(stage_z, 0))
        during(i, n_s + 1 - s, partial(stage_z, 1))
        during(i, 2 + n_s, stage_d)
        during(i, 3 + n_s, stage_e)
        during(i, 4 + n_s, stage_f)

    low_all = half_masks((length, TILE))
    low = half_masks((BLOCK, TILE))
    lse_t[...] = lse[...].T
    dq_acc[...] = jnp.zeros_like(dq_acc)

    def prepare(p, carry):
        for half in (0, 1):
            qm[p, half] = keep_half(q[p], low_all, half)
            um[p, half] = keep_half(up[p], low_all, half)
        prod = (up[p].astype(f32) * att[p].astype(f32)).T
        for half in (0, 1):
            delta_t[p, half] = jnp.sum(prod[half * HEAD_DIM : (half + 1) * HEAD_DIM, :], axis=0, keepdims=True)
        return carry

    lax.fori_loop(0, slabs, prepare, 0)

    def to_core(xo, part):
        theirs = owner_rows(xo * 2 + 1 - core)
        source = (dk if part == 0 else dv).at[:, theirs, :]
        return remote(source, core_in.at[xo, part], cs.at[xo, part], cr.at[xo, part], sibling)

    def to_owner(xo):
        d = x - xo
        return remote(core_in.at[xo], x_in.at[d - 1], xs.at[xo], xr.at[d - 1], {"ctx": xo * 2 + core})

    def from_higher(d):
        return remote(x_in.at[d - 1], x_in.at[d - 1], xs.at[0], xr.at[d - 1], sibling)

    def relay(xo):
        mine = owner_rows(xo * 2 + core)
        for part, source in ((0, dk), (1, dv)):
            to_core(xo, part).wait_recv()
            core_in[xo, part] = (source[:, mine, :].astype(f32) + core_in[xo, part].astype(f32)).astype(bf16)
        to_owner(xo).start()

    points = (x + 1) * slabs

    def chip(xo, carry):
        first = xo * 2 * per
        last = lax.min(first + 2 * per, (c + 1) * per)

        def one(p, inner):
            def keys_loop(j, deeper):
                spot = pl.ds(pl.multiple_of(j * BLOCK, BLOCK), BLOCK)
                keys, values = k[p, spot, :], v[p, spot, :]
                kept = [keep_half(keys, low, half) for half in (0, 1)]

                def body(qb, sums_in):
                    dk_sum, dv_sum = sums_in
                    at = pl.ds(pl.multiple_of(qb * BLOCK, BLOCK), BLOCK)
                    back = jnp.zeros((BLOCK, TILE), f32)
                    for half in (0, 1):
                        q_half, u_half = qm[p, half, at, :], um[p, half, at, :]
                        score = dot_nt(keys, q_half) * (scale * LOG2E)
                        probs = jnp.exp2(score - lse_t[pl.ds(p * 2 + half, 1), at])
                        grad = dot_nt(values, u_half)
                        slope = (probs * (grad - delta_t[p, half, :, at])).astype(bf16)
                        dv_sum = dv_sum + dot_nn(probs.astype(bf16), u_half)
                        dk_sum = dk_sum + dot_nn(slope, q_half)
                        back = back + dot_tn(slope, kept[half])
                    dq_acc[p, at, :] = dq_acc[p, at, :] + back
                    return dk_sum, dv_sum

                zero = jnp.zeros((BLOCK, TILE), f32)
                start = lax.max(j - c * per, 0)
                dk_sum, dv_sum = lax.fori_loop(start, per, body, (zero, zero))
                dk[p, spot, :] = (dk_sum * scale).astype(bf16)
                dv[p, spot, :] = dv_sum.astype(bf16)
                return deeper

            lax.fori_loop(first, last, keys_loop, 0)

            @pl.when((p == 0) & (xo > 0))
            def _():
                relay(xo - 1)

            point = xo * slabs + p

            def between(i, deeper):
                reduce_step(i, 0, early)
                return deeper

            lax.fori_loop(lax.div(point * early, points), lax.div((point + 1) * early, points), between, 0)
            return inner

        lax.fori_loop(0, slabs, one, 0)

        @pl.when(xo < x)
        def _():
            to_core(xo, 0).start()
            to_core(xo, 1).start()

        return carry

    lax.fori_loop(0, x + 1, chip, 0)

    @pl.when(core == 1)
    def _():
        to_core(x, 0).start()
        to_core(x, 1).start()

    for p in range(slabs):
        dq[p] = (dq_acc[p] * scale).astype(bf16)

    def norm_tile(i, carry):
        at = rows_at(i, TILE)
        n1[at, :] = norm_rows(tok[at, :].astype(f32), norms[0:1, :], norms[3:4, :])
        return carry

    lax.fori_loop(0, length // TILE, norm_tile, 0)
    own = owner_rows(c)

    @pl.when(core == 0)
    def _():
        to_core(x, 0).wait_recv()
        to_core(x, 1).wait_recv()

    for d in range(1, n_x):
        pl.when(x + d < n_x)(from_higher(d).wait_recv)
    for part, target in ((0, gk), (1, gv)):
        dq_acc[...] = (dk if part == 0 else dv)[:, own, :].astype(f32)

        @pl.when(core == 0)
        def _():
            dq_acc[...] = dq_acc[...] + core_in[x, part].astype(f32)

        for d in range(1, n_x):

            @pl.when(x + d < n_x)
            def _():
                dq_acc[...] = dq_acc[...] + x_in[d - 1, part].astype(f32)

        target[...] = dq_acc[...].astype(bf16)

    def exchange(r):
        at = rows_at(r, BLOCK)
        return remote(tx.at[at, :], rx.at[at, :], ts.at[r], tr.at[r], peer)

    def product(r, carry):
        at = rows_at(r, BLOCK)
        left = jnp.concatenate([ref[i, at, :] for ref in (dq, gk, gv) for i in range(slabs)], axis=1)

        def run(n, inner):
            cols = pl.ds(pl.multiple_of(n * 256, 256), 256)
            weight = jnp.concatenate([w[i, cols, :] for i in range(3 * slabs)], axis=1)
            tx[at, cols] = dot_nt(left, weight).astype(bf16)
            return inner

        lax.fori_loop(0, width // 256, run, 0)
        exchange(r).start()
        return carry

    lax.fori_loop(0, per, product, 0)

    def late(i, carry):
        reduce_step(i, early, chunks)
        return carry

    pause = lax.min(early + 4, chunks)
    lax.fori_loop(early, pause, late, 0)
    sm_mine[...] = small_in[...]
    for index, source in ((0, dq), (1, gv)):
        for p in range(slabs):
            lanes = slice((index * slabs + p) * TILE, (index * slabs + p + 1) * TILE)
            sm_mine[9:10, lanes] = jnp.sum(source[p].astype(f32), axis=0, keepdims=True)

    def last_rows(r, carry):
        exchange(r).wait_recv()

        def tile(i, inner):
            at = pl.ds(pl.multiple_of(r * BLOCK + i * TILE, TILE), TILE)
            spot, rate = norm_parts(tok[at, :].astype(f32))
            upstream = tx[at, :].astype(f32) + rx[at, :].astype(f32)
            scaled = upstream * norms[0:1, :]
            sm_mine[0:1, :] = sm_mine[0:1, :] + jnp.sum(upstream * spot, axis=0, keepdims=True)
            sm_mine[3:4, :] = sm_mine[3:4, :] + jnp.sum(upstream, axis=0, keepdims=True)
            gtok[at, :] = gfirst[at, :] + rate * (
                scaled - jnp.mean(scaled, axis=-1, keepdims=True)
                - spot * jnp.mean(scaled * spot, axis=-1, keepdims=True)
            )
            return inner

        lax.fori_loop(0, BLOCK // TILE, tile, 0)
        return carry

    lax.fori_loop(0, per, last_rows, 0)
    sm_send = remote(sm_mine, sm_core, ms.at[0], mr.at[0], sibling)

    def sm_x_copy(d):
        return remote(sm_x.at[x], sm_x.at[x], ms.at[d], mr.at[d], {"ctx": lax.rem(x + d, n_x) * 2 + core})

    def sm_x_in(d):
        here = sm_x.at[lax.rem(x - d + n_x, n_x)]
        return remote(here, here, ms.at[d], mr.at[d], sibling)

    def sm_z_copy(d):
        return remote(sm_z.at[s], sm_z.at[s], ms.at[n_x + d - 1], mr.at[n_x + d - 1], {"shard": lax.rem(s + d, n_s)})

    def sm_z_in(d):
        here = sm_z.at[lax.rem(s - d + n_s, n_s)]
        return remote(here, here, ms.at[n_x + d - 1], mr.at[n_x + d - 1], peer)

    sm_send.start()

    def rest(i, carry):
        reduce_step(i, early, chunks)

        @pl.when(i == pause)
        def _():
            sm_send.wait_recv()
            sm_x[x] = sm_mine[...] + sm_core[...]
            for d in range(1, n_x):
                sm_x_copy(d).start()

        @pl.when(i == pause + 1)
        def _():
            for d in range(1, n_x):
                sm_x_in(d).wait_recv()
            both = sm_x[0]
            for e in range(1, n_x):
                both = both + sm_x[e]
            sm_z[s] = both
            for d in range(1, n_s):
                sm_z_copy(d).start()

        return carry

    lax.fori_loop(pause, chunks + 5 + n_s, rest, 0)
    for d in range(1, n_s):
        sm_z_in(d).wait_recv()
    both = sm_z[0]
    for e in range(1, n_s):
        both = both + sm_z[e]
    small_out[...] = both
    sm_send.wait_send()
    for d in range(1, n_x):
        sm_x_copy(d).wait_send()
    for d in range(1, n_s):
        sm_z_copy(d).wait_send()

    def settle(xo, carry):
        @pl.when(xo < x)
        def _():
            to_core(xo, 0).wait_send()
            to_core(xo, 1).wait_send()
            to_owner(xo).wait_send()

        @pl.when((xo == x) & (core == 1))
        def _():
            to_core(xo, 0).wait_send()
            to_core(xo, 1).wait_send()

        return carry

    lax.fori_loop(0, x + 1, settle, 0)

    def settle_tp(r, carry):
        exchange(r).wait_send()
        return carry

    lax.fori_loop(0, per, settle_tp, 0)

    def finish(kk, carry):
        @pl.when(kk >= max(chunks - ring, 0))
        def _():
            for e in range(n_x):
                a_out(kk, e).wait_send()

        for d in range(1, n_x):
            b_out(kk, d).wait_send()
            f_out(kk, d).wait_send()
        for d in range(n_x):
            h_out(kk, d).wait_send()
        for way in (0, 1):
            for m in range(n_s - 1):
                pl.when(sends(way, m))(z_copy(way, m, kk).wait_send)
        return carry

    lax.fori_loop(0, chunks, finish, 0)


def tail(groups, n_s, n_c, q, k, v, up, att, lse, tok, norms, w, gfirst, small, bank, *grad_inputs):
    slabs, length, unused = q.shape
    width = tok.shape[1]
    n_x = n_c // 2
    bf16, f32 = jnp.bfloat16, jnp.float32
    vmem, anywhere = pl.BlockSpec(memory_space=pltpu.VMEM), pl.BlockSpec(memory_space=pl.ANY)
    shape, scratch, dma = jax.ShapeDtypeStruct, pltpu.VMEM, pltpu.SemaphoreType.DMA
    pair = (2, slabs, length, TILE)
    total = sum(count for name, count in groups)
    chunks, rows = total // n_c, width // n_s
    early = (total - groups[-1][1]) // n_c
    ring = min(4, chunks)
    return pl.pallas_call(
        partial(tail_kernel, n_s, n_c, groups, early),
        out_shape=(
            shape((length, width), f32), shape((rows, total * TILE), bf16), shape(small.shape, f32),
        ),
        in_specs=[vmem] * 11 + [anywhere] * 6 + [vmem] * (len(grad_inputs) - 5),
        out_specs=(vmem,) * 3,
        scratch_shapes=[
            scratch(k.shape, bf16), scratch(k.shape, bf16),
            scratch((slabs, 2, length, TILE), bf16), scratch((slabs, 2, length, TILE), bf16),
            scratch((TILE, length), f32), scratch((slabs, 2, 1, length), f32), scratch(q.shape, f32),
            scratch(q.shape, bf16), scratch(q.shape, bf16), scratch(q.shape, bf16),
            scratch((length, width), bf16),
            scratch((n_x,) + pair, bf16), scratch((n_x - 1,) + pair, bf16),
            scratch((length, width), bf16), scratch((length, width), bf16),
            scratch((width, bank.shape[0]), bf16), scratch((2, BLOCK, width), bf16),
            scratch((ring, n_c, width, TILE), bf16), scratch((chunks, n_x, width, TILE), bf16),
            scratch((chunks, n_x - 1, width, TILE), bf16),
            scratch((min(chunks, n_s + 4), width, TILE), f32),
            scratch((2, chunks, n_s - 1, rows, TILE), bf16), scratch((2, chunks, n_s - 1, rows, TILE), bf16),
            scratch(small.shape, f32), scratch(small.shape, f32),
            scratch((n_x,) + small.shape, f32), scratch((n_s,) + small.shape, f32),
            dma((n_x, 2)), dma((n_x, 2)), dma((n_x - 1,)), dma((n_x - 1,)),
            dma((length // BLOCK,)), dma((length // BLOCK,)), dma((2,)),
            dma((chunks, n_x)), dma((chunks, n_x)), dma((chunks, n_x - 1)), dma((chunks, n_x - 1)),
            dma((2, chunks, n_s - 1)), dma((2, chunks, n_s - 1)),
            dma((chunks, n_x - 1)), dma((chunks, n_x - 1)), dma((chunks, n_x)), dma((chunks, n_x)),
            dma((n_x + n_s - 1,)), dma((n_x + n_s - 1,)),
        ],
        compiler_params=pltpu.CompilerParams(collective_id=3, has_side_effects=True, vmem_limit_bytes=64 << 20),
        name="tail",
    )(q, k, v, up, att, lse, tok, norms, w, gfirst, small, bank, *grad_inputs)


def slabbed(matrix):
    rows, columns = matrix.shape
    return matrix.reshape(rows, columns // TILE, TILE).transpose(1, 0, 2)


def shards(
    tokens,
    cotangent,
    neighbours,
    neighbour_ids,
    norm_gains,
    norm_shifts,
    head_bias,
    out_bias,
    up_bias,
    self_input,
    self_output,
    cross_query,
    cross_memory,
    cross_output,
    hidden_up,
    hidden_down,
):
    n_s, n_c = lax.axis_size("shard"), lax.axis_size("ctx")
    slice_rows = self_input.shape[0]
    shard = slabbed(
        jnp.concatenate(
            [
                self_input.reshape(slice_rows, -1),
                cross_memory.reshape(slice_rows, -1),
                self_output.T,
                cross_query,
                cross_output.T,
                hidden_up,
                hidden_down.T,
            ],
            axis=1,
        )
    )
    tok, cot = tokens[0], cotangent[0]
    length, width = tok.shape
    local = self_output.shape[0]
    slabs, units = local // TILE, hidden_up.shape[1] // TILE
    counts = (3 * slabs, 2 * slabs, slabs, slabs, slabs, units, units)
    names = ("self_in", "memory", "self_out", "cross_q", "cross_out", "up", "down")
    at, edge = {}, 0
    for name, count in zip(names, counts):
        at[name] = edge
        edge += count
    bank_shape = neighbours.shape[1:]
    bank = neighbours.reshape(bank_shape[0] * bank_shape[1], width)
    ids = neighbour_ids[0]
    weights, q, k, v, att, lse = front(shard, tok, norm_gains, norm_shifts, head_bias, n_s, n_c)
    (
        n2, n3, sl, fl, act, gh, mx, gcq, ga, dks, dvs, gfirst, result, sums, up_sums, head_cross,
    ) = chain(
        at, ids, att, tok, cot, bank, weights, norm_gains, norm_shifts, head_bias, out_bias, up_bias,
        bank_shape[0], BLOCK,
    )
    mg, mine, send, head_memory = bank_back(
        ids, dks, dvs, weights[at["memory"] : at["self_out"]], bank_shape[0], bank_shape[1]
    )
    received = lax.ppermute(send, "tp", [(0, 1), (1, 0)])
    grad_neighbours = (mine + received.astype(jnp.float32)).reshape((1,) + bank_shape[:2] + (width // 2,))
    norms = jnp.concatenate([norm_gains, norm_shifts])
    small = jnp.concatenate(
        [
            sums[:9],
            jnp.zeros((1, width), jnp.float32),
            jnp.concatenate([head_cross, head_memory]).reshape(1, width),
            up_sums.reshape(-1, width),
        ]
    )
    small = jnp.pad(small, ((0, 16 - small.shape[0]), (0, 0)))
    groups = [(name, count) for name, count in zip(names, counts) if name != "self_in"]
    groups.append(("self_in", counts[0]))
    grad_tokens, grads, small = tail(
        groups, n_s, n_c, q, k, v, ga, att, lse, tok, norms, weights[: at["memory"]], gfirst, small, bank,
        fl, n2, sl, n3, cot, mg, gcq, mx, gh, act,
    )
    grad_head = small[9:11].reshape(4, local)
    grad_up_bias = small[11 : 11 + up_sums.size // width].reshape(-1)
    edge, pieces = 0, {}
    for name, count in groups:
        pieces[name] = grads[:, edge * TILE : (edge + count) * TILE].astype(jnp.float32)
        edge += count
    return (
        result[None],
        grad_tokens[None],
        grad_neighbours,
        small[0:3],
        small[3:6],
        grad_head,
        small[6:9],
        grad_up_bias,
        pieces["self_in"].reshape(slice_rows, 3, local),
        pieces["self_out"].T,
        pieces["cross_q"],
        pieces["memory"].reshape(slice_rows, 2, local),
        pieces["cross_out"].T,
        pieces["up"],
        pieces["down"].T,
    )


def solution(mesh):
    placed = (
        P("shard", "ctx", None),
        P("shard", "ctx", None),
        P("shard", "ctx", None, None),
        P("shard", "ctx", None),
        P(),
        P(),
        P(None, "tp"),
        P(),
        P("tp"),
        P("shard", None, "tp"),
        P("tp", "shard"),
        P("shard", "tp"),
        P("shard", None, "tp"),
        P("tp", "shard"),
        P("shard", "tp"),
        P("tp", "shard"),
    )
    return jax.shard_map(
        shards,
        mesh=mesh,
        in_specs=placed,
        out_specs=(
            P("shard", "ctx", None),
            P("shard", "ctx", None),
            P("shard", "ctx", None, "tp"),
            P(),
            P(),
            P(None, "tp"),
            P(),
            P("tp"),
            P("shard", None, "tp"),
            P("tp", "shard"),
            P("shard", "tp"),
            P("shard", None, "tp"),
            P("tp", "shard"),
            P("shard", "tp"),
            P("tp", "shard"),
        ),
        check_vma=False,
    )
```

```python
from functools import partial

import jax
import jax.numpy as jnp
from jax import lax
from jax.experimental import pallas as pl
from jax.experimental.pallas import tpu as pltpu
from jax.sharding import PartitionSpec as P

HEAD_DIM = 64
BLOCK = 256


EPSILON = 1e-05
NEGATIVE = -1e30
HIGHEST = lax.Precision.HIGHEST


MESH = pl.DeviceIdType.MESH
LOG2E = 1.4426950408889634
TILE = 128


def aligned(index, size):
    return pl.multiple_of(index * size, size)


def rows_at(index, size):
    return pl.ds(pl.multiple_of(index * size, size), size)


def remote(src, dst, send, recv, where):
    return pltpu.make_async_remote_copy(
        src_ref=src, dst_ref=dst, send_sem=send, recv_sem=recv, device_id=where, device_id_type=MESH
    )


class Place:
    def __init__(self, n_s, n_c):
        self.n_s, self.n_c, self.n_x = n_s, n_c, n_c // 2
        self.s, self.c, self.t = lax.axis_index("shard"), lax.axis_index("ctx"), lax.axis_index("tp")
        self.x, self.core = lax.div(self.c, 2), lax.rem(self.c, 2)
        self.sibling_index = self.x * 2 + 1 - self.core
        self.sibling, self.peer = {"ctx": self.sibling_index}, {"tp": 1 - self.t}

    def along_x(self, d):
        return {"ctx": lax.rem(self.x + d, self.n_x) * 2 + self.core}

    def along_s(self, d):
        return {"shard": lax.rem(self.s + d, self.n_s)}

    def source_x(self, d):
        return lax.rem(self.x - d + self.n_x, self.n_x)

    def greet(self):
        barrier = pltpu.get_barrier_semaphore()
        partners = [self.along_x(d) for d in range(1, self.n_x)] + [self.along_s(d) for d in range(1, self.n_s)]
        partners += [self.sibling, self.peer]
        for where in partners:
            pl.semaphore_signal(barrier, inc=1, device_id=where, device_id_type=MESH)
        pl.semaphore_wait(barrier, len(partners))


def gather_semaphores(chunks, n_s, n_c):
    dma, n_x = pltpu.SemaphoreType.DMA, n_c // 2
    shapes = [(chunks, n_s - 1)] * 2 + [(chunks, n_s - 1, n_x - 1)] * 2 + [(chunks, n_s - 1, n_x)] * 2
    return [dma(shape) for shape in shapes] + [dma((1,))]


class Gather:
    def __init__(self, place, own, full, chunks, base, semaphores):
        self.place, self.own, self.full, self.chunks, self.base = place, own, full, chunks, base
        self.zs, self.zr, self.xs, self.xr, self.cs, self.cr, self.local = semaphores
        self.rows = own.shape[1]
        self.last = chunks + 1
        total = chunks * place.n_c
        self.own_copy = pltpu.make_async_copy(
            own.at[pl.ds(base, total)],
            full.at[pl.ds(base, total), pl.ds(aligned(place.s, self.rows), self.rows), :],
            self.local.at[0],
        )

    def block(self, origin, k, quarter):
        slab = self.base + k * self.place.n_c + quarter
        return self.full.at[slab, pl.ds(aligned(origin, self.rows), self.rows), :]

    def source(self, d):
        return lax.rem(self.place.s - d + self.place.n_s, self.place.n_s)

    def own_out(self, d, k):
        return remote(
            self.own.at[self.base + k * self.place.n_c + self.place.c], self.block(self.place.s, k, self.place.c),
            self.zs.at[k, d - 1], self.zr.at[k, d - 1], self.place.along_s(d),
        )

    def z_in(self, d, k):
        here = self.block(self.source(d), k, self.place.c)
        return remote(here, here, self.zs.at[k, d - 1], self.zr.at[k, d - 1], self.place.along_s(d))

    def x_move(self, d, k, e, incoming):
        quarter = self.place.source_x(e) * 2 + self.place.core if incoming else self.place.c
        here = self.block(self.source(d), k, quarter)
        return remote(here, here, self.xs.at[k, d - 1, e - 1], self.xr.at[k, d - 1, e - 1], self.place.along_x(e))

    def core_move(self, d, k, e, incoming):
        core = 1 - self.place.core if incoming else self.place.core
        here = self.block(self.source(d), k, self.place.source_x(e) * 2 + core)
        return remote(here, here, self.cs.at[k, d - 1, e], self.cr.at[k, d - 1, e], self.place.sibling)

    def each(self, low, high, body):
        def one(i, carry):
            body(i)
            return carry

        lax.fori_loop(low, high, one, 0)

    def start(self):
        self.own_copy.start()

        def send(k):
            for d in range(1, self.place.n_s):
                self.own_out(d, k).start()

        self.each(0, self.chunks, send)

    def advance(self, i):
        @pl.when(i < self.chunks)
        def _():
            for d in range(1, self.place.n_s):
                self.z_in(d, i).wait_recv()
                for e in range(1, self.place.n_x):
                    self.x_move(d, i, e, False).start()
                self.core_move(d, i, 0, False).start()

        @pl.when(i > 0)
        def _():
            for d in range(1, self.place.n_s):
                for e in range(1, self.place.n_x):
                    self.x_move(d, i - 1, e, True).wait_recv()
                    self.core_move(d, i - 1, e, False).start()

    def advance_range(self, low, high):
        self.each(low, high, self.advance)

    def complete_range(self, low, high):
        def one(k):
            for d in range(1, self.place.n_s):
                for e in range(self.place.n_x):
                    self.core_move(d, k, e, True).wait_recv()

        self.each(low, high, one)

    def finish(self):
        def one(k):
            for d in range(1, self.place.n_s):
                self.own_out(d, k).wait_send()
                for e in range(1, self.place.n_x):
                    self.x_move(d, k, e, False).wait_send()
                for e in range(self.place.n_x):
                    self.core_move(d, k, e, False).wait_send()

        self.each(0, self.chunks, one)


RING = 4
P_RING = 6


def cross_scratch(chunks, width, n_s, n_c):
    bf16, vmem, dma, n_x = jnp.bfloat16, pltpu.VMEM, pltpu.SemaphoreType.DMA, n_c // 2
    return [
        vmem((min(RING, chunks), n_c, width, TILE), bf16),
        vmem((chunks, n_x, width, TILE), bf16),
        vmem((chunks, n_x - 1, width, TILE), bf16),
        dma((chunks, n_x)), dma((chunks, n_x)), dma((chunks, n_x - 1)), dma((chunks, n_x - 1)),
    ]


def spread_scratch(chunks, width, n_s, n_c):
    bf16, vmem, dma, n_x = jnp.bfloat16, pltpu.VMEM, pltpu.SemaphoreType.DMA, n_c // 2
    rows = width // n_s
    return [
        vmem((chunks, n_s - 1, rows, TILE), bf16),
        dma((chunks, n_s - 1)), dma((chunks, n_s - 1)),
        dma((chunks, n_x - 1)), dma((chunks, n_x - 1)), dma((chunks, n_x)), dma((chunks, n_x)),
    ]


class Cross:
    def __init__(self, place, total, refs):
        self.place, self.total = place, total
        self.gbuf, self.a_buf, self.b_buf, self.as_, self.ar, self.bs, self.br = refs
        self.chunks, self.ring = self.a_buf.shape[0], self.gbuf.shape[0]

    def a_out(self, kk, e):
        slot = lax.rem(kk, self.ring)
        source = self.gbuf.at[slot, e * 2 + 1 - self.place.core]
        return remote(source, self.a_buf.at[kk, e], self.as_.at[kk, e], self.ar.at[kk, e], self.place.sibling)

    def reserve(self, kk):
        if kk >= self.ring:
            for e in range(self.place.n_x):
                self.a_out(kk - self.ring, e).wait_send()
        return kk % self.ring

    def send(self, kk):
        for e in range(self.place.n_x):
            self.a_out(kk, e).start()

    def b_out(self, kk, d):
        to = lax.rem(self.place.x + d, self.place.n_x)
        return remote(
            self.a_buf.at[kk, to], self.b_buf.at[kk, d - 1], self.bs.at[kk, d - 1], self.br.at[kk, d - 1],
            self.place.along_x(d),
        )

    def stage_b(self, kk):
        f32 = jnp.float32
        x, core, slot = self.place.x, self.place.core, lax.rem(kk, self.ring)
        for d in range(1, self.place.n_x):
            e = lax.rem(x + d, self.place.n_x)
            self.a_out(kk, e).wait_recv()
            total = self.gbuf[slot, e * 2 + core].astype(f32) + self.a_buf[kk, e].astype(f32)
            self.a_buf[kk, e] = total.astype(jnp.bfloat16)
            self.b_out(kk, d).start()
        self.a_out(kk, x).wait_recv()
        self.a_buf[kk, x] = (
            self.gbuf[slot, self.place.c].astype(f32) + self.a_buf[kk, x].astype(f32)
        ).astype(jnp.bfloat16)

    def stage_c(self, kk):
        total = self.a_buf[kk, self.place.x].astype(jnp.float32)
        for d in range(1, self.place.n_x):
            self.b_out(kk, d).wait_recv()
            total = total + self.b_buf[kk, d - 1].astype(jnp.float32)
        self.total[kk] = total.astype(jnp.bfloat16)

    def step(self, i, produce, low, high):
        for kk in range(low, high):
            pl.when(i == kk)(partial(produce, kk))
        for lag, stage in ((1, self.stage_b), (2, self.stage_c)):
            kk = i - lag
            pl.when((kk >= 0) & (kk < self.chunks))(partial(stage, kk))

    def finish(self):
        def one(kk, carry):
            @pl.when(kk >= max(self.chunks - self.ring, 0))
            def _():
                for e in range(self.place.n_x):
                    self.a_out(kk, e).wait_send()

            for d in range(1, self.place.n_x):
                self.b_out(kk, d).wait_send()
            return carry

        lax.fori_loop(0, self.chunks, one, 0)


class Spread:
    def __init__(self, place, total, res, refs):
        self.place, self.total, self.res = place, total, res
        self.z_in, self.zs, self.zr, self.fs, self.fr, self.hs, self.hr = refs
        self.chunks, self.rows = self.z_in.shape[0], self.z_in.shape[2]

    def shard_rows(self, index):
        return pl.ds(aligned(index, self.rows), self.rows)

    def z_copy(self, d, kk):
        theirs = self.shard_rows(lax.rem(self.place.s + d, self.place.n_s))
        return remote(
            self.total.at[kk, theirs, :], self.z_in.at[kk, d - 1], self.zs.at[kk, d - 1], self.zr.at[kk, d - 1],
            self.place.along_s(d),
        )

    def send(self, kk):
        for d in range(1, self.place.n_s):
            self.z_copy(d, kk).start()

    def block(self, kk, quarter):
        return self.res.at[:, pl.ds(pl.multiple_of((kk * self.place.n_c + quarter) * TILE, TILE), TILE)]

    def f_move(self, kk, d, incoming):
        here = self.block(kk, self.place.source_x(d) * 2 + self.place.core if incoming else self.place.c)
        return remote(here, here, self.fs.at[kk, d - 1], self.fr.at[kk, d - 1], self.place.along_x(d))

    def h_move(self, kk, d, incoming):
        core = 1 - self.place.core if incoming else self.place.core
        here = self.block(kk, self.place.source_x(d) * 2 + core)
        return remote(here, here, self.hs.at[kk, d], self.hr.at[kk, d], self.place.sibling)

    def stage_d(self, kk):
        total = self.total[kk, self.shard_rows(self.place.s), :].astype(jnp.float32)
        for d in range(1, self.place.n_s):
            self.z_copy(d, kk).wait_recv()
            total = total + self.z_in[kk, d - 1].astype(jnp.float32)
        lanes = pl.ds(pl.multiple_of((kk * self.place.n_c + self.place.c) * TILE, TILE), TILE)
        self.res[:, lanes] = total.astype(jnp.bfloat16)
        for d in range(1, self.place.n_x):
            self.f_move(kk, d, False).start()
        self.h_move(kk, 0, False).start()

    def stage_e(self, kk):
        for d in range(1, self.place.n_x):
            self.f_move(kk, d, True).wait_recv()
            self.h_move(kk, d, False).start()

    def stage_f(self, kk):
        for d in range(self.place.n_x):
            self.h_move(kk, d, True).wait_recv()

    def step(self, i):
        for lag, stage in ((0, self.stage_d), (1, self.stage_e), (2, self.stage_f)):
            kk = i - lag
            pl.when((kk >= 0) & (kk < self.chunks))(partial(stage, kk))

    def finish(self):
        def one(kk, carry):
            for d in range(1, self.place.n_x):
                self.f_move(kk, d, False).wait_send()
            for d in range(self.place.n_x):
                self.h_move(kk, d, False).wait_send()
            for d in range(1, self.place.n_s):
                self.z_copy(d, kk).wait_send()
            return carry

        lax.fori_loop(0, self.chunks, one, 0)


def produce_group(cross, order, kk, left_of, slab_of):
    slot, at, n_c = cross.reserve(kk), 0, cross.place.n_c
    while at < n_c:
        name, index = order[kk * n_c + at]
        count = 1
        while at + count < n_c and order[kk * n_c + at + count][0] == name:
            count += 1
        right = jnp.concatenate([slab_of(name, index + i) for i in range(count)], axis=1)
        product = dot_tn(left_of(name)[...], right).astype(jnp.bfloat16)
        for i in range(count):
            cross.gbuf[slot, at + i] = product[:, i * TILE : (i + 1) * TILE]
        at += count
    cross.send(kk)


def dot_nn(left, right):
    return lax.dot_general(left, right, (((1,), (0,)), ((), ())), preferred_element_type=jnp.float32)


def dot_nt(left, right):
    return lax.dot_general(left, right, (((1,), (1,)), ((), ())), preferred_element_type=jnp.float32)


def dot_tn(left, right):
    return lax.dot_general(left, right, (((0,), (0,)), ((), ())), preferred_element_type=jnp.float32)


def joined(ref, low, high):
    return jnp.concatenate([ref[index] for index in range(low, high)], axis=1)


def norm_parts(values):
    centre = values - jnp.mean(values, axis=-1, keepdims=True)
    spread = jnp.mean(centre * centre, axis=-1, keepdims=True)
    rate = lax.rsqrt(spread + EPSILON)
    return centre * rate, rate


def norm_rows(values, gain, shift):
    return (norm_parts(values)[0] * gain + shift).astype(jnp.bfloat16)


def half_masks(shape):
    lane = lax.broadcasted_iota(jnp.int32, shape, len(shape) - 1)
    return lane < HEAD_DIM


def keep_half(values, low, half):
    zero = jnp.zeros_like(values)
    return jnp.where(low, values, zero) if half == 0 else jnp.where(low, zero, values)


def attend(c, q, k, v, att, lse, scores, after):
    slabs, length, unused = q.shape
    scale = HEAD_DIM ** (-0.5) * LOG2E
    low = half_masks((BLOCK, TILE))
    lane = lax.broadcasted_iota(jnp.int32, (BLOCK, TILE), 1)
    per = length // BLOCK
    lse[...] = jnp.zeros_like(lse)

    def one(step, carry):
        p, qb = lax.div(step, per), lax.rem(step, per)
        rows = pl.ds(pl.multiple_of(qb * BLOCK, BLOCK), BLOCK)
        block_q = q[p, rows, :]
        parts = [keep_half(block_q, low, half) for half in (0, 1)]
        count = c * per + qb + 1

        def first(j, peaks):
            keys = k[p, pl.ds(pl.multiple_of(j * BLOCK, BLOCK), BLOCK), :]
            out = []
            for half in (0, 1):
                s = dot_nt(parts[half], keys) * scale
                scores[half, j] = s
                best = peaks[half]
                for at in range(0, BLOCK, TILE):
                    best = jnp.maximum(best, s[:, at : at + TILE])
                out.append(best)
            return tuple(out)

        start = jnp.full((BLOCK, TILE), NEGATIVE, jnp.float32)
        peaks = lax.fori_loop(0, count, first, (start, start))
        tops = [jnp.max(peak, axis=1, keepdims=True) for peak in peaks]

        def second(j, state):
            values = v[p, pl.ds(pl.multiple_of(j * BLOCK, BLOCK), BLOCK), :]
            out = []
            for half in (0, 1):
                total, mixed = state[half]
                raised = jnp.exp2(scores[half, j] - tops[half])
                for at in range(0, BLOCK, TILE):
                    total = total + raised[:, at : at + TILE]
                mixed = mixed + dot_nn(raised.astype(jnp.bfloat16), values)
                out.append((total, mixed))
            return tuple(out)

        zero = jnp.zeros((BLOCK, TILE), jnp.float32)
        state = lax.fori_loop(0, count, second, ((zero, zero), (zero, zero)))
        outs = []
        logs = lse[rows, :]
        for half in (0, 1):
            total = jnp.sum(state[half][0], axis=1, keepdims=True)
            outs.append(state[half][1] / total)
            logs = jnp.where(lane == p * 2 + half, tops[half] + jnp.log2(total), logs)
        lse[rows, :] = logs
        att[p, rows, :] = jnp.where(low, outs[0], outs[1]).astype(jnp.bfloat16)
        after(step)
        return carry

    lax.fori_loop(0, slabs * per, one, 0)


def front_kernel(
    n_s, n_c, chunks, shard, tok, gains, shifts, bias, w, q, k, v, att, lse,
    others, normed, scores, zs, zr, xs, xr, cs, cr, own_sem, txs, txr, tys, tyr, tcs, tcr,
):
    place = Place(n_s, n_c)
    c, x, core, n_x = place.c, place.x, place.core, place.n_x
    length, width = tok.shape
    slabs = q.shape[0]
    place.greet()
    gather = Gather(place, shard, w, chunks, 0, (zs, zr, xs, xr, cs, cr, own_sem))

    half = length // 2

    def token_half(index, which):
        return others.at[pl.ds(pl.multiple_of(index * length + which * half, half), half), :]

    def run(pair, method):
        copy, valid = pair
        pl.when(valid)(getattr(copy, method))

    def token_x(d):
        own_half = tok.at[pl.ds(pl.multiple_of(place.t * half, half), half), :]
        copy = remote(own_half, token_half(c, place.t), txs.at[d - 1], txr.at[d - 1], place.along_x(d))
        return copy, lax.rem(x + d, n_x) > x

    def token_in(d):
        here = token_half(place.source_x(d) * 2 + core, place.t)
        return remote(here, here, txs.at[d - 1], txr.at[d - 1], place.sibling), place.source_x(d) < x

    def token_peer(d, incoming):
        here = token_half(place.source_x(d) * 2 + core, 1 - place.t if incoming else place.t)
        return remote(here, here, tys.at[d - 1], tyr.at[d - 1], place.peer), place.source_x(d) < x

    def token_relay(d, which, incoming):
        here = token_half(place.source_x(d) * 2 + (1 - core if incoming else core), which)
        return remote(here, here, tcs.at[d, which], tcr.at[d, which], place.sibling), place.source_x(d) < x

    def token_own(which):
        own_half = tok.at[pl.ds(which * half, half), :]
        return remote(own_half, token_half(c, which), tcs.at[0, which], tcr.at[0, which], place.sibling), core == 0

    def token_own_in(which):
        here = token_half(place.sibling_index, which)
        return remote(here, here, tcs.at[0, which], tcr.at[0, which], place.sibling), core == 1

    for d in range(1, n_x):
        run(token_x(d), "start")
    for which in (0, 1):
        run(token_own(which), "start")
    gather.start()

    def norm_block(source, base, j):
        def tile(i, carry):
            rows = source[pl.ds(pl.multiple_of(base + i * TILE, TILE), TILE), :].astype(jnp.float32)
            normed[j, rows_at(i, TILE), :] = norm_rows(rows, gains[0:1, :], shifts[0:1, :])
            return carry

        lax.fori_loop(0, length // TILE, tile, 0)

    norm_block(tok, 0, c)
    needed = -(-3 * slabs // n_c)
    ready = min(needed + 1, gather.last)
    gather.advance_range(0, 1)
    for d in range(1, n_x):
        run(token_in(d), "wait_recv")
        run(token_peer(d, False), "start")
        for which in (0, 1):
            pl.when(place.t == which)(lambda: run(token_relay(d, which, False), "start"))
    gather.advance_range(1, 2)
    for d in range(1, n_x):
        run(token_peer(d, True), "wait_recv")
        for which in (0, 1):
            pl.when(place.t != which)(lambda: run(token_relay(d, which, False), "start"))
    gather.advance_range(2, ready)
    for which in (0, 1):
        for d in range(1, n_x):
            run(token_relay(d, which, True), "wait_recv")
        run(token_own_in(which), "wait_recv")

    def norm_other(j, carry):
        norm_block(others, j * length, j)
        return carry

    lax.fori_loop(0, c, norm_other, 0)
    gather.own_copy.wait()
    gather.complete_range(0, needed)

    def project(j, which, row_bias):
        result = dot_nn(normed[j], joined(w, which * slabs, (which + 1) * slabs))
        if row_bias is not None:
            result = result + row_bias
        return result.astype(jnp.bfloat16)

    def project_keys(j, carry):
        spot = rows_at(j, length)
        for which, target, row_bias in ((1, k, None), (2, v, bias[1:2, :])):
            result = project(j, which, row_bias)
            for p in range(slabs):
                target[p, spot, :] = result[:, p * TILE : (p + 1) * TILE]
        return carry

    lax.fori_loop(0, c + 1, project_keys, 0)
    queries = project(c, 0, bias[0:1, :])
    for p in range(slabs):
        q[p] = queries[:, p * TILE : (p + 1) * TILE]
    pieces = slabs * (length // BLOCK)

    def after(step):
        pl.when(ready + step < gather.last)(lambda: gather.advance(ready + step))

    attend(c, q, k, v, att, lse, scores, after)
    gather.advance_range(min(ready + pieces, gather.last), gather.last)
    gather.complete_range(needed, chunks)
    gather.finish()
    for d in range(1, n_x):
        run(token_x(d), "wait_send")
        run(token_peer(d, False), "wait_send")
        for which in (0, 1):
            run(token_relay(d, which, False), "wait_send")
    for which in (0, 1):
        run(token_own(which), "wait_send")


def front(shard, tok, gains, shifts, bias, n_s, n_c, cut):
    total, rows, unused = shard.shape
    length, width = tok.shape
    slabs = bias.shape[1] // TILE
    chunks, n_x = cut // n_c, n_c // 2
    dma, shape, scratch = pltpu.SemaphoreType.DMA, jax.ShapeDtypeStruct, pltpu.VMEM
    vmem = pl.BlockSpec(memory_space=pltpu.VMEM)
    bf16, f32 = jnp.bfloat16, jnp.float32
    return pl.pallas_call(
        partial(front_kernel, n_s, n_c, chunks),
        out_shape=(
            shape((cut, rows * n_s, TILE), bf16),
            shape((slabs, length, TILE), bf16),
            shape((slabs, length * n_c, TILE), bf16),
            shape((slabs, length * n_c, TILE), bf16),
            shape((slabs, length, TILE), bf16),
            shape((length, TILE), f32),
        ),
        in_specs=[vmem] * 5,
        out_specs=(vmem,) * 6,
        scratch_shapes=[
            scratch((length * n_c, width), bf16), scratch((n_c, length, width), bf16),
            scratch((2, length * n_c // BLOCK, BLOCK, BLOCK), f32),
            *gather_semaphores(chunks, n_s, n_c),
            dma((n_x - 1,)), dma((n_x - 1,)), dma((n_x - 1,)), dma((n_x - 1,)), dma((n_x, 2)), dma((n_x, 2)),
        ],
        compiler_params=pltpu.CompilerParams(collective_id=0, has_side_effects=True, vmem_limit_bytes=60 << 20),
        name="front",
    )(shard, tok, gains, shifts, bias)


def chain_kernel(
    at, chunk, banks, n_s, n_c, ids, att, tok, cot, bank, shard, gains, shifts, bias, out_bias, up_bias, w_front,
    n2, sl, fl, mx, gcq, ga, dks, dvs, gfirst, part, second, sums, up_sums, head_sums, total_out,
    mem_k, mem_v, first, gsecond, weights, gmix, cq, tx, rx, ss, rs, w, wsem, n3, act, gh, *engines
):
    place = Place(n_s, n_c)
    peer = place.peer
    cut = w_front.shape[0]
    place.greet()
    gather = Gather(place, shard, w, (shard.shape[0] - cut) // n_c, cut, engines[:7])
    cross = Cross(place, total_out, engines[7:])
    edges = [at["self_out"], at["memory"], cut]

    def load(i):
        low, high = edges[i], edges[i + 1]
        return pltpu.make_async_copy(w_front.at[pl.ds(low, high - low)], w.at[pl.ds(low, high - low)], wsem.at[i])

    load(0).start()
    load(1).start()
    gather.start()
    f32, bf16 = jnp.float32, jnp.bfloat16
    length, width = tok.shape
    slabs = att.shape[0]
    units = act.shape[0]
    span = bank.shape[0] // banks
    stretches, picks = ids.shape
    stretch = length // stretches
    keys_each = picks * span
    scale = HEAD_DIM ** (-0.5)
    count = length // chunk
    tiles = chunk // TILE
    low = half_masks((stretch, TILE))
    sums[...] = jnp.zeros_like(sums)
    up_sums[...] = jnp.zeros_like(up_sums)
    head_sums[...] = jnp.zeros_like(head_sums)

    def exchange(phase, r):
        rows = rows_at(r, chunk)
        return remote(tx.at[phase, rows, :], rx.at[phase, rows, :], ss.at[phase, r], rs.at[phase, r], peer)

    def every(stage):
        def run(r, carry):
            stage(r)
            return carry

        lax.fori_loop(0, count, run, 0)

    def per_tile(r, body):
        def run(i, carry):
            body(pl.ds(pl.multiple_of(r * chunk + i * TILE, TILE), TILE))
            return carry

        lax.fori_loop(0, tiles, run, 0)

    def out_product(target, r, left, name, total):
        rows = rows_at(r, chunk)
        low_slab = at[name]
        step = 256

        def run(n, carry):
            cols = pl.ds(pl.multiple_of(n * step, step), step)
            weight = jnp.concatenate([w[low_slab + i, cols, :] for i in range(total)], axis=1)
            product = dot_nt(jnp.concatenate([left[i, rows, :] for i in range(total)], axis=1), weight)
            target[rows, cols] = product.astype(bf16)
            return carry

        lax.fori_loop(0, width // step, run, 0)

    def send_attended(r):
        out_product(tx.at[0], r, att, "self_out", slabs)
        exchange(0, r).start()

    load(0).wait()
    every(send_attended)
    load(1).wait()
    total = gather.last
    gather.advance_range(0, min(1, total))

    def memory(i, carry):
        rows = rows_at(i, 4 * span)
        for which, target, row_bias in ((0, mem_k, None), (1, mem_v, bias[3:4, :])):
            base = at["memory"] + which * slabs
            product = dot_nn(bank[rows, :], joined(w, base, base + slabs))
            if row_bias is not None:
                product = product + row_bias
            product = product.astype(bf16)
            for p in range(slabs):
                for e in range(4):
                    target[p, i * 4 + e] = product[e * span : (e + 1) * span, p * TILE : (p + 1) * TILE]
        return carry

    lax.fori_loop(0, banks // 4, memory, 0)
    gather.advance_range(min(1, total), min(2, total))

    def narrow(source, r, base, row_bias, target):
        rows = rows_at(r, chunk)
        product = dot_nn(source[rows, :], joined(w, base, base + slabs))
        if row_bias is not None:
            product = product + row_bias
        product = product.astype(bf16)
        for p in range(slabs):
            target[p, rows, :] = product[:, p * TILE : (p + 1) * TILE]

    def picked(source, p, st):
        return jnp.concatenate(
            [source[p, ids[st, n]] for n in range(picks)], axis=0
        )

    def stacked(source, p, st):
        block = source[p, rows_at(st, stretch), :]
        return jnp.concatenate([keep_half(block, low, 0), keep_half(block, low, 1)], axis=0)

    def unstacked(both):
        return jnp.where(low, both[:stretch], both[stretch:])

    def total_of(phase, rows):
        return tx[phase, rows, :].astype(f32) + rx[phase, rows, :].astype(f32)

    def per_stretch(r, body):
        each = chunk // stretch

        def run(i, carry):
            p, inner = lax.div(i, each), lax.rem(i, each)
            body(p, r * each + inner)
            return carry

        lax.fori_loop(0, slabs * each, run, 0)

    def cross_forward(r):
        exchange(0, r).wait_recv()

        def tile(rows):
            value = tok[rows, :].astype(f32) + total_of(0, rows) + out_bias[0:1, :]
            first[rows, :] = value
            n2[rows, :] = norm_rows(value, gains[1:2, :], shifts[1:2, :])

        per_tile(r, tile)
        narrow(n2, r, at["cross_q"], bias[2:3, :], cq)

        def one(p, st):
            keys, values = picked(mem_k, p, st), picked(mem_v, p, st)
            s = dot_nt(stacked(cq, p, st), keys) * (scale * LOG2E)
            raised = jnp.exp2(s - jnp.max(s, axis=1, keepdims=True))
            probs = raised / jnp.sum(raised, axis=1, keepdims=True)
            weights[p, st] = probs
            mixed = dot_nn(probs.astype(bf16), values)
            mx[p, rows_at(st, stretch), :] = unstacked(mixed).astype(bf16)

        per_stretch(r, one)
        out_product(tx.at[1], r, mx, "cross_out", slabs)
        exchange(1, r).start()
        gather.advance_range(lax.min(2 + r, total), lax.min(3 + r, total))

    every(cross_forward)
    gather.advance_range(min(2 + count, total), total)
    gather.own_copy.wait()
    gather.complete_range(0, gather.chunks)
    curve = 0.7978845608028654
    cubic = 0.044715

    def feed(r):
        exchange(1, r).wait_recv()
        rows_all = rows_at(r, chunk)

        def tile(rows):
            value = first[rows, :] + total_of(1, rows) + out_bias[1:2, :]
            second[rows, :] = value
            n3[rows, :] = norm_rows(value, gains[2:3, :], shifts[2:3, :])

        per_tile(r, tile)

        def unit(j, carry):
            up = jnp.concatenate([w[at["up"] + 2 * j], w[at["up"] + 2 * j + 1]], axis=1)
            down = jnp.concatenate([w[at["down"] + 2 * j], w[at["down"] + 2 * j + 1]], axis=1)
            hidden = dot_nn(n3[rows_all, :], up) + up_bias[j]
            back = dot_nn(cot[rows_all, :], down)
            square = hidden * hidden
            bent = jnp.tanh(curve * hidden * (1.0 + cubic * square))
            half = 0.5 * (1.0 + bent)
            active = (hidden * half).astype(bf16)
            slope = half + 0.5 * hidden * (1.0 - bent * bent) * (curve * (1.0 + 3.0 * cubic * square))
            grad = (slope * back).astype(bf16)
            up_sums[j] = up_sums[j] + jnp.sum(grad.astype(f32), axis=0, keepdims=True)
            for i in range(2):
                lanes = slice(i * TILE, (i + 1) * TILE)
                act[2 * j + i, rows_all, :] = active[:, lanes]
                gh[2 * j + i, rows_all, :] = grad[:, lanes]
            return carry

        lax.fori_loop(0, units // 2, unit, 0)
        out_product(tx.at[2], r, gh, "up", units)
        exchange(2, r).start()

    every(feed)

    def result_product(r):
        out_product(part, r, act, "down", units)

    order = [(name, index) for name in ("up", "down") for index in range(units)]

    def left_of(name):
        return n3 if name == "up" else cot

    def slab_of(name, index):
        return (gh if name == "up" else act)[index]

    def produce(kk):
        produce_group(cross, order, kk, left_of, slab_of)

    steps = cross.chunks + 2

    def reduce_range(low, high):
        def one(i, carry):
            cross.step(i, produce, 0, cross.chunks)
            return carry

        lax.fori_loop(lax.min(low, steps), lax.min(high, steps), one, 0)

    def result_and_step(r):
        result_product(r)
        reduce_range(r, r + 1)

    every(result_and_step)

    def norm_back_rows(value, gain, upstream, row):
        spot, rate = norm_parts(value)
        scaled = upstream * gain
        sums[row : row + 1, :] = sums[row : row + 1, :] + jnp.sum(upstream * spot, axis=0, keepdims=True)
        sums[row + 3 : row + 4, :] = sums[row + 3 : row + 4, :] + jnp.sum(upstream, axis=0, keepdims=True)
        return rate * (
            scaled - jnp.mean(scaled, axis=-1, keepdims=True)
            - spot * jnp.mean(scaled * spot, axis=-1, keepdims=True)
        )

    def add_sum(row, values):
        sums[row : row + 1, :] = sums[row : row + 1, :] + jnp.sum(values, axis=0, keepdims=True)

    def cross_back(r):
        reduce_range(count + 2 * r, count + 2 * r + 1)
        exchange(2, r).wait_recv()

        def tile(rows):
            upstream = cot[rows, :].astype(f32)
            grad = upstream + norm_back_rows(second[rows, :], gains[2:3, :], total_of(2, rows), 2)
            add_sum(8, upstream)
            add_sum(7, grad)
            gsecond[rows, :] = grad
            sl[rows, :] = grad.astype(bf16)

        per_tile(r, tile)
        narrow(sl, r, at["cross_out"], None, gmix)

        def one(p, st):
            keys, values = picked(mem_k, p, st), picked(mem_v, p, st)
            grads, queries = stacked(gmix, p, st), stacked(cq, p, st)
            probs = weights[p, st]
            spread = dot_nt(grads, values)
            ds = (probs * (spread - jnp.sum(probs * spread, axis=1, keepdims=True))).astype(bf16)
            back = unstacked(dot_nn(ds, keys)) * scale
            gcq[p, rows_at(st, stretch), :] = back.astype(bf16)
            dks[p, rows_at(st, keys_each), :] = (dot_tn(ds, queries) * scale).astype(bf16)
            dvs[p, rows_at(st, keys_each), :] = dot_tn(probs.astype(bf16), grads).astype(bf16)

        per_stretch(r, one)
        out_product(tx.at[3], r, gcq, "cross_q", slabs)
        exchange(3, r).start()
        reduce_range(count + 2 * r + 1, count + 2 * r + 2)

    every(cross_back)

    def finish(r):
        exchange(3, r).wait_recv()

        def tile(rows):
            grad = gsecond[rows, :] + norm_back_rows(first[rows, :], gains[1:2, :], total_of(3, rows), 1)
            add_sum(6, grad)
            gfirst[rows, :] = grad
            fl[rows, :] = grad.astype(bf16)

        per_tile(r, tile)
        narrow(fl, r, at["self_out"], None, ga)
        reduce_range(3 * count + r, 3 * count + r + 1)

    every(finish)
    for p in range(slabs):
        head_sums[p] = jnp.sum(gcq[p].astype(f32), axis=0, keepdims=True)

    reduce_range(4 * count, steps)
    gather.finish()
    cross.finish()

    def settle(r):
        for phase in range(4):
            exchange(phase, r).wait_send()

    every(settle)


def chain(at, ids, att, tok, cot, bank, shard, gains, shifts, bias, out_bias, up_bias, w_front, banks, chunk, n_s, n_c):
    length, width = tok.shape
    slabs = att.shape[0]
    units = up_bias.shape[0] // TILE
    stretches, picks = ids.shape
    stretch, span = length // stretches, bank.shape[0] // banks
    keys_each = picks * span
    bf16, f32 = jnp.bfloat16, jnp.float32
    vmem, smem = pl.BlockSpec(memory_space=pltpu.VMEM), pl.BlockSpec(memory_space=pltpu.SMEM)
    shape = jax.ShapeDtypeStruct
    scratch = pltpu.VMEM
    row_slabs = shape((slabs, length, TILE), bf16)
    rows = shape((length, width), bf16)
    anywhere = pl.BlockSpec(memory_space=pl.ANY)
    chunks = 2 * units // n_c
    return pl.pallas_call(
        partial(chain_kernel, at, chunk, banks, n_s, n_c),
        out_shape=(
            rows, rows, rows,
            row_slabs, row_slabs, row_slabs,
            shape((slabs, stretches * keys_each, TILE), bf16), shape((slabs, stretches * keys_each, TILE), bf16),
            shape((length, width), f32), rows, shape((length, width), f32),
            shape((16, width), f32), shape((units // 2, 1, 2 * TILE), f32), shape((slabs, 1, TILE), f32),
            shape((chunks, width, TILE), bf16),
        ),
        in_specs=[smem] + [vmem] * 10 + [anywhere],
        out_specs=(vmem,) * 15,
        scratch_shapes=[
            scratch((slabs, banks, span, TILE), bf16), scratch((slabs, banks, span, TILE), bf16),
            scratch((length, width), f32), scratch((length, width), f32),
            scratch((slabs, stretches, 2 * stretch, keys_each), f32),
            scratch((slabs, length, TILE), bf16), scratch((slabs, length, TILE), bf16),
            scratch((4, length, width), bf16), scratch((4, length, width), bf16),
            pltpu.SemaphoreType.DMA((4, length // chunk)), pltpu.SemaphoreType.DMA((4, length // chunk)),
            scratch((shard.shape[0], width, TILE), bf16), pltpu.SemaphoreType.DMA((2,)),
            scratch((length, width), bf16),
            scratch((units, length, TILE), bf16), scratch((units, length, TILE), bf16),
            *gather_semaphores((shard.shape[0] - w_front.shape[0]) // n_c, n_s, n_c),
            *cross_scratch(chunks, width, n_s, n_c),
        ],
        compiler_params=pltpu.CompilerParams(collective_id=2, has_side_effects=True, vmem_limit_bytes=63 << 20),
        name="chain",
    )(ids, att, tok, cot, bank, shard, gains, shifts, bias, out_bias, up_bias.reshape(units // 2, 1, 2 * TILE), w_front)


def bank_kernel(span, at, ids, dks, dvs, w_all, mg, mine, send, head_sums, acc, w, ws):
    t = lax.axis_index("tp")
    f32, bf16 = jnp.float32, jnp.bfloat16
    slabs = dks.shape[0]
    stretches, picks = ids.shape
    acc[...] = jnp.zeros_like(acc)
    w_copy = pltpu.make_async_copy(w_all.at[pl.ds(at, 2 * slabs)], w, ws)
    w_copy.start()

    def add(i, carry):
        st, n = lax.div(i, picks), lax.rem(i, picks)
        rows = rows_at(ids[st, n], span)
        source = rows_at(i, span)
        for p in range(slabs):
            acc[p, rows, :] = acc[p, rows, :] + dks[p, source, :].astype(f32)
            acc[slabs + p, rows, :] = acc[slabs + p, rows, :] + dvs[p, source, :].astype(f32)
        return carry

    lax.fori_loop(0, stretches * picks, add, 0)
    half = mine.shape[1]
    w_copy.wait()
    total = jnp.zeros((1, slabs * TILE), f32)

    def one(i, sums):
        rows = rows_at(i, BLOCK)
        for p in range(2 * slabs):
            mg[p, rows, :] = acc[p, rows, :].astype(bf16)
        left = jnp.concatenate([mg[p, rows, :] for p in range(2 * slabs)], axis=1)
        for which, target in ((t, mine), (1 - t, send)):
            cols = pl.ds(pl.multiple_of(which * half, half), half)
            weight = jnp.concatenate([w[p, cols, :] for p in range(2 * slabs)], axis=1)
            target[rows, :] = dot_nt(left, weight).astype(target.dtype)
        return sums + jnp.sum(left[:, slabs * TILE :].astype(f32), axis=0, keepdims=True)

    total = lax.fori_loop(0, mine.shape[0] // BLOCK, one, total)
    for p in range(slabs):
        head_sums[p] = total[:, p * TILE : (p + 1) * TILE]


def bank_back(ids, dks, dvs, w, at, banks, span):
    slabs = dks.shape[0]
    rows, half = banks * span, w.shape[1] // 2
    bf16, f32 = jnp.bfloat16, jnp.float32
    vmem, smem = pl.BlockSpec(memory_space=pltpu.VMEM), pl.BlockSpec(memory_space=pltpu.SMEM)
    shape = jax.ShapeDtypeStruct
    return pl.pallas_call(
        partial(bank_kernel, span, at),
        out_shape=(
            shape((2 * slabs, rows, TILE), bf16), shape((rows, half), f32),
            shape((rows, half), bf16), shape((slabs, 1, TILE), f32),
        ),
        in_specs=[smem, vmem, vmem, pl.BlockSpec(memory_space=pl.ANY)],
        out_specs=(vmem,) * 4,
        scratch_shapes=[
            pltpu.VMEM((2 * slabs, rows, TILE), f32), pltpu.VMEM((2 * slabs, w.shape[1], TILE), bf16),
            pltpu.SemaphoreType.DMA,
        ],
        compiler_params=pltpu.CompilerParams(vmem_limit_bytes=40 << 20),
        name="bank_back",
    )(ids, dks, dvs, w)


def tail_kernel(
    n_s, n_c, groups, early,
    q, k, v, up, att, lse, tok, norms, w_all, down_part, small_in, out_bias, gfirst, second, bank, fl, n2, sl, mg, gcq, mx, hidden,
    gtok, result, res, res_hidden, small_out,
    dk, dv, qm, um, lse_t, delta_t, dq_acc, dq, gk, gv, n1, core_in, x_in, tx, rx, rx_part, stage32, w,
    bank_here, totals, sm_mine, sm_core, sm_x, sm_z,
    cs, cr, xs, xr, ts, tr, ds_, ms, mr, ps, pr, es, ws, *engine
):
    f32, bf16 = jnp.float32, jnp.bfloat16
    place = Place(n_s, n_c)
    s, c, x, core, n_x = place.s, place.c, place.x, place.core, place.n_x
    sibling, peer = place.sibling, place.peer
    slabs, length, unused = q.shape
    width = tok.shape[1]
    per = length // BLOCK
    scale = HEAD_DIM ** (-0.5)
    place.greet()
    cross = Cross(place, totals, engine[:7])
    spread = Spread(place, totals, res, engine[7:14])
    extra = Spread(place, hidden, res_hidden, engine[14:])
    chunks = cross.chunks
    bank_copy = pltpu.make_async_copy(bank, bank_here, ds_)
    bank_copy.start()

    def send_hidden(kk, carry):
        extra.send(kk)
        return carry

    lax.fori_loop(0, extra.chunks, send_hidden, 0)
    part_copy = remote(down_part, rx_part, ps, pr, peer)
    part_copy.start()
    w_copy = pltpu.make_async_copy(w_all.at[pl.ds(0, 3 * slabs)], w, ws)
    w_copy.start()

    def staged(source, r):
        return pltpu.make_async_copy(source.at[rows_at(r, BLOCK), :], stage32.at[r], es.at[r])

    for r in range(per):
        staged(second, r).start()

    def owner_rows(index):
        return pl.ds(pl.multiple_of(index * length, length), length)

    def left_of(name):
        return {"self_in": n1, "memory": bank_here, "self_out": fl, "cross_q": n2, "cross_out": sl}[name]

    def slab_of(name, index):
        if name == "self_in":
            return (dq, gk, gv)[index // slabs][index % slabs]
        return {"memory": mg, "self_out": att, "cross_q": gcq, "cross_out": mx}[name][index]

    order = [(name, index) for name, count in groups for index in range(count)]

    def produce(kk):
        if any(order[kk * n_c + i] == ("memory", 0) for i in range(n_c)):
            bank_copy.wait()
        produce_group(cross, order, kk, left_of, slab_of)

    def main_step(i, low, high):
        cross.step(i, produce, low, high)
        spread.step(i - 3)
        done = i - 2
        pl.when((done >= 0) & (done < chunks))(lambda: spread.send(done))

    shift = extra.chunks - 1

    low_all = half_masks((length, TILE))
    low = half_masks((BLOCK, TILE))
    lse_t[...] = lse[...].T
    dq_acc[...] = jnp.zeros_like(dq_acc)

    def prepare(p, carry):
        for half in (0, 1):
            qm[p, half] = keep_half(q[p], low_all, half)
            um[p, half] = keep_half(up[p], low_all, half)
        prod = (up[p].astype(f32) * att[p].astype(f32)).T
        for half in (0, 1):
            delta_t[p, half] = jnp.sum(prod[half * HEAD_DIM : (half + 1) * HEAD_DIM, :], axis=0, keepdims=True)
        return carry

    lax.fori_loop(0, slabs, prepare, 0)

    def to_core(xo, part):
        theirs = owner_rows(xo * 2 + 1 - core)
        source = (dk if part == 0 else dv).at[:, theirs, :]
        return remote(source, core_in.at[xo, part], cs.at[xo, part], cr.at[xo, part], sibling)

    def to_owner(xo):
        d = x - xo
        return remote(core_in.at[xo], x_in.at[d - 1], xs.at[xo], xr.at[d - 1], {"ctx": xo * 2 + core})

    def from_higher(d):
        return remote(x_in.at[d - 1], x_in.at[d - 1], xs.at[0], xr.at[d - 1], sibling)

    def relay(xo):
        mine = owner_rows(xo * 2 + core)
        for part, source in ((0, dk), (1, dv)):
            to_core(xo, part).wait_recv()
            core_in[xo, part] = (source[:, mine, :].astype(f32) + core_in[xo, part].astype(f32)).astype(bf16)
        to_owner(xo).start()

    points = (x + 1) * slabs

    def chip(xo, carry):
        first = xo * 2 * per
        last = lax.min(first + 2 * per, (c + 1) * per)

        def one(p, inner):
            def keys_loop(j, deeper):
                spot = pl.ds(pl.multiple_of(j * BLOCK, BLOCK), BLOCK)
                keys, values = k[p, spot, :], v[p, spot, :]
                kept = [keep_half(keys, low, half) for half in (0, 1)]

                def body(qb, sums_in):
                    dk_sum, dv_sum = sums_in
                    at = pl.ds(pl.multiple_of(qb * BLOCK, BLOCK), BLOCK)
                    back = jnp.zeros((BLOCK, TILE), f32)
                    for half in (0, 1):
                        q_half, u_half = qm[p, half, at, :], um[p, half, at, :]
                        score = dot_nt(keys, q_half) * (scale * LOG2E)
                        probs = jnp.exp2(score - lse_t[pl.ds(p * 2 + half, 1), at])
                        grad = dot_nt(values, u_half)
                        slope = (probs * (grad - delta_t[p, half, :, at])).astype(bf16)
                        dv_sum = dv_sum + dot_nn(probs.astype(bf16), u_half)
                        dk_sum = dk_sum + dot_nn(slope, q_half)
                        back = back + dot_tn(slope, kept[half])
                    dq_acc[p, at, :] = dq_acc[p, at, :] + back
                    return dk_sum, dv_sum

                zero = jnp.zeros((BLOCK, TILE), f32)
                start = lax.max(j - c * per, 0)
                dk_sum, dv_sum = lax.fori_loop(start, per, body, (zero, zero))
                dk[p, spot, :] = (dk_sum * scale).astype(bf16)
                dv[p, spot, :] = dv_sum.astype(bf16)
                return deeper

            lax.fori_loop(first, last, keys_loop, 0)

            @pl.when((p == 0) & (xo > 0))
            def _():
                relay(xo - 1)

            point = xo * slabs + p

            def between(i, deeper):
                extra.step(i)
                pl.when(i >= shift)(lambda: main_step(i - shift, 0, early))
                return deeper

            share = early + shift
            lax.fori_loop(lax.div(point * share, points), lax.div((point + 1) * share, points), between, 0)
            return inner

        lax.fori_loop(0, slabs, one, 0)

        @pl.when(xo < x)
        def _():
            to_core(xo, 0).start()
            to_core(xo, 1).start()

        return carry

    lax.fori_loop(0, x + 1, chip, 0)

    @pl.when(core == 1)
    def _():
        to_core(x, 0).start()
        to_core(x, 1).start()

    for p in range(slabs):
        dq[p] = (dq_acc[p] * scale).astype(bf16)

    def norm_tile(i, carry):
        at = rows_at(i, TILE)
        n1[at, :] = norm_rows(tok[at, :].astype(f32), norms[0:1, :], norms[3:4, :])
        return carry

    lax.fori_loop(0, length // TILE, norm_tile, 0)
    own = owner_rows(c)

    @pl.when(core == 0)
    def _():
        to_core(x, 0).wait_recv()
        to_core(x, 1).wait_recv()

    for d in range(1, n_x):
        pl.when(x + d < n_x)(from_higher(d).wait_recv)
    for part, target in ((0, gk), (1, gv)):
        dq_acc[...] = (dk if part == 0 else dv)[:, own, :].astype(f32)

        @pl.when(core == 0)
        def _():
            dq_acc[...] = dq_acc[...] + core_in[x, part].astype(f32)

        for d in range(1, n_x):

            @pl.when(x + d < n_x)
            def _():
                dq_acc[...] = dq_acc[...] + x_in[d - 1, part].astype(f32)

        target[...] = dq_acc[...].astype(bf16)

    part_copy.wait_recv()

    def result_rows(r, carry):
        staged(second, r).wait()

        def tile(i, inner):
            at = pl.ds(pl.multiple_of(r * BLOCK + i * TILE, TILE), TILE)
            both = down_part[at, :].astype(f32) + rx_part[at, :].astype(f32)
            result[at, :] = (stage32[r, rows_at(i, TILE), :] + both + out_bias[2:3, :]).astype(bf16)
            return inner

        lax.fori_loop(0, BLOCK // TILE, tile, 0)
        staged(gfirst, r).start()
        return carry

    lax.fori_loop(0, per, result_rows, 0)

    def exchange(r):
        at = rows_at(r, BLOCK)
        return remote(tx.at[at, :], rx.at[at, :], ts.at[r], tr.at[r], peer)

    w_copy.wait()

    def product(r, carry):
        at = rows_at(r, BLOCK)
        left = jnp.concatenate([ref[i, at, :] for ref in (dq, gk, gv) for i in range(slabs)], axis=1)

        def run(n, inner):
            cols = pl.ds(pl.multiple_of(n * 256, 256), 256)
            weight = jnp.concatenate([w[i, cols, :] for i in range(3 * slabs)], axis=1)
            tx[at, cols] = dot_nt(left, weight).astype(bf16)
            return inner

        lax.fori_loop(0, width // 256, run, 0)
        exchange(r).start()
        return carry

    lax.fori_loop(0, per, product, 0)

    def late(i, carry):
        extra.step(i + shift)
        main_step(i, early, chunks)
        return carry

    pause = lax.min(early + 4, chunks)
    lax.fori_loop(early, pause, late, 0)
    sm_mine[...] = small_in[...]
    for index, source in ((0, dq), (1, gv)):
        for p in range(slabs):
            lanes = slice((index * slabs + p) * TILE, (index * slabs + p + 1) * TILE)
            sm_mine[9:10, lanes] = jnp.sum(source[p].astype(f32), axis=0, keepdims=True)

    def last_rows(r, carry):
        exchange(r).wait_recv()
        staged(gfirst, r).wait()

        def tile(i, inner):
            at = pl.ds(pl.multiple_of(r * BLOCK + i * TILE, TILE), TILE)
            spot, rate = norm_parts(tok[at, :].astype(f32))
            upstream = tx[at, :].astype(f32) + rx[at, :].astype(f32)
            scaled = upstream * norms[0:1, :]
            sm_mine[0:1, :] = sm_mine[0:1, :] + jnp.sum(upstream * spot, axis=0, keepdims=True)
            sm_mine[3:4, :] = sm_mine[3:4, :] + jnp.sum(upstream, axis=0, keepdims=True)
            gtok[at, :] = stage32[r, rows_at(i, TILE), :] + rate * (
                scaled - jnp.mean(scaled, axis=-1, keepdims=True)
                - spot * jnp.mean(scaled * spot, axis=-1, keepdims=True)
            )
            return inner

        lax.fori_loop(0, BLOCK // TILE, tile, 0)
        return carry

    lax.fori_loop(0, per, last_rows, 0)
    sm_send = remote(sm_mine, sm_core, ms.at[0], mr.at[0], sibling)

    def sm_x_copy(d):
        return remote(sm_x.at[x], sm_x.at[x], ms.at[d], mr.at[d], {"ctx": lax.rem(x + d, n_x) * 2 + core})

    def sm_x_in(d):
        here = sm_x.at[lax.rem(x - d + n_x, n_x)]
        return remote(here, here, ms.at[d], mr.at[d], sibling)

    def sm_z_copy(d):
        return remote(sm_z.at[s], sm_z.at[s], ms.at[n_x + d - 1], mr.at[n_x + d - 1], {"shard": lax.rem(s + d, n_s)})

    def sm_z_in(d):
        here = sm_z.at[lax.rem(s - d + n_s, n_s)]
        return remote(here, here, ms.at[n_x + d - 1], mr.at[n_x + d - 1], peer)

    sm_send.start()

    def rest(i, carry):
        extra.step(i + shift)
        main_step(i, early, chunks)

        @pl.when(i == pause)
        def _():
            sm_send.wait_recv()
            sm_x[x] = sm_mine[...] + sm_core[...]
            for d in range(1, n_x):
                sm_x_copy(d).start()

        @pl.when(i == pause + 1)
        def _():
            for d in range(1, n_x):
                sm_x_in(d).wait_recv()
            both = sm_x[0]
            for e in range(1, n_x):
                both = both + sm_x[e]
            sm_z[s] = both
            for d in range(1, n_s):
                sm_z_copy(d).start()

        return carry

    lax.fori_loop(pause, chunks + 5, rest, 0)
    for d in range(1, n_s):
        sm_z_in(d).wait_recv()
    both = sm_z[0]
    for e in range(1, n_s):
        both = both + sm_z[e]
    small_out[...] = both
    part_copy.wait_send()
    sm_send.wait_send()
    for d in range(1, n_x):
        sm_x_copy(d).wait_send()
    for d in range(1, n_s):
        sm_z_copy(d).wait_send()

    def settle(xo, carry):
        @pl.when(xo < x)
        def _():
            to_core(xo, 0).wait_send()
            to_core(xo, 1).wait_send()
            to_owner(xo).wait_send()

        @pl.when((xo == x) & (core == 1))
        def _():
            to_core(xo, 0).wait_send()
            to_core(xo, 1).wait_send()

        return carry

    lax.fori_loop(0, x + 1, settle, 0)

    def settle_tp(r, carry):
        exchange(r).wait_send()
        return carry

    lax.fori_loop(0, per, settle_tp, 0)

    cross.finish()
    spread.finish()
    extra.finish()


def tail(groups, n_s, n_c, hidden, q, k, v, up, att, lse, tok, norms, w, part, small, out_bias, gfirst, second, bank, *grad_inputs):
    slabs, length, unused = q.shape
    width = tok.shape[1]
    n_x = n_c // 2
    bf16, f32 = jnp.bfloat16, jnp.float32
    vmem, anywhere = pl.BlockSpec(memory_space=pltpu.VMEM), pl.BlockSpec(memory_space=pl.ANY)
    shape, scratch, dma = jax.ShapeDtypeStruct, pltpu.VMEM, pltpu.SemaphoreType.DMA
    pair = (2, slabs, length, TILE)
    total = sum(count for name, count in groups)
    chunks, rows = total // n_c, width // n_s
    early = (total - groups[-1][1]) // n_c
    return pl.pallas_call(
        partial(tail_kernel, n_s, n_c, groups, early),
        out_shape=(
            shape((length, width), f32), shape((length, width), bf16),
            shape((rows, total * TILE), bf16), shape((rows, hidden.shape[0] * n_c * TILE), bf16),
            shape(small.shape, f32),
        ),
        in_specs=[vmem] * 8
        + [anywhere]
        + [vmem] * 3 + [anywhere] * 3 + [vmem] * (len(grad_inputs) + 1),
        out_specs=(vmem,) * 5,
        scratch_shapes=[
            scratch(k.shape, bf16), scratch(k.shape, bf16),
            scratch((slabs, 2, length, TILE), bf16), scratch((slabs, 2, length, TILE), bf16),
            scratch((TILE, length), f32), scratch((slabs, 2, 1, length), f32), scratch(q.shape, f32),
            scratch(q.shape, bf16), scratch(q.shape, bf16), scratch(q.shape, bf16),
            scratch((length, width), bf16),
            scratch((n_x,) + pair, bf16), scratch((n_x - 1,) + pair, bf16),
            scratch((length, width), bf16), scratch((length, width), bf16),
            scratch((length, width), bf16), scratch((length // BLOCK, BLOCK, width), f32),
            scratch((3 * slabs, width, TILE), bf16),
            scratch(bank.shape, bf16), scratch((chunks, width, TILE), bf16),
            scratch(small.shape, f32), scratch(small.shape, f32),
            scratch((n_x,) + small.shape, f32), scratch((n_s,) + small.shape, f32),
            dma((n_x, 2)), dma((n_x, 2)), dma((n_x - 1,)), dma((n_x - 1,)),
            dma((length // BLOCK,)), dma((length // BLOCK,)), dma,
            dma((n_x + n_s - 1,)), dma((n_x + n_s - 1,)),
            dma, dma, dma((length // BLOCK,)), dma,
            *cross_scratch(chunks, width, n_s, n_c),
            *spread_scratch(chunks, width, n_s, n_c),
            *spread_scratch(hidden.shape[0], width, n_s, n_c),
        ],
        compiler_params=pltpu.CompilerParams(collective_id=3, has_side_effects=True, vmem_limit_bytes=64 << 20),
        name="tail",
    )(q, k, v, up, att, lse, tok, norms, w, part, small, out_bias, gfirst, second, bank, *grad_inputs, hidden)


def slabbed(matrix):
    rows, columns = matrix.shape
    return matrix.reshape(rows, columns // TILE, TILE).transpose(1, 0, 2)


def shards(
    tokens,
    cotangent,
    neighbours,
    neighbour_ids,
    norm_gains,
    norm_shifts,
    head_bias,
    out_bias,
    up_bias,
    self_input,
    self_output,
    cross_query,
    cross_memory,
    cross_output,
    hidden_up,
    hidden_down,
):
    n_s, n_c = lax.axis_size("shard"), lax.axis_size("ctx")
    slice_rows = self_input.shape[0]
    shard = slabbed(
        jnp.concatenate(
            [
                self_input.reshape(slice_rows, -1),
                self_output.T,
                cross_memory.reshape(slice_rows, -1),
                cross_query,
                cross_output.T,
                hidden_up,
                hidden_down.T,
            ],
            axis=1,
        )
    )
    tok, cot = tokens[0], cotangent[0]
    length, width = tok.shape
    local = self_output.shape[0]
    slabs, units = local // TILE, hidden_up.shape[1] // TILE
    counts = (3 * slabs, slabs, 2 * slabs, slabs, slabs, units, units)
    names = ("self_in", "self_out", "memory", "cross_q", "cross_out", "up", "down")
    at, edge = {}, 0
    for name, count in zip(names, counts):
        at[name] = edge
        edge += count
    bank_shape = neighbours.shape[1:]
    bank = neighbours.reshape(bank_shape[0] * bank_shape[1], width)
    ids = neighbour_ids[0]
    cut = at["up"]
    weights, q, k, v, att, lse = front(shard, tok, norm_gains, norm_shifts, head_bias, n_s, n_c, cut)
    n2, sl, fl, mx, gcq, ga, dks, dvs, gfirst, part, second, sums, up_sums, head_cross, hidden = chain(
        at, ids, att, tok, cot, bank, shard, norm_gains, norm_shifts, head_bias, out_bias, up_bias, weights,
        bank_shape[0], BLOCK, n_s, n_c,
    )
    mg, mine, send, head_memory = bank_back(
        ids, dks, dvs, weights, at["memory"], bank_shape[0], bank_shape[1]
    )
    received = lax.ppermute(send, "tp", [(0, 1), (1, 0)])
    grad_neighbours = (mine + received.astype(jnp.float32)).reshape((1,) + bank_shape[:2] + (width // 2,))
    norms = jnp.concatenate([norm_gains, norm_shifts])
    small = jnp.concatenate(
        [
            sums[:9],
            jnp.zeros((1, width), jnp.float32),
            jnp.concatenate([head_cross, head_memory]).reshape(1, width),
            up_sums.reshape(-1, width),
        ]
    )
    small = jnp.pad(small, ((0, 16 - small.shape[0]), (0, 0)))
    groups = [(name, count) for name, count in zip(names, counts) if name not in ("self_in", "up", "down")]
    groups.append(("self_in", counts[0]))
    grad_tokens, result, grads, hidden_grads, small = tail(
        groups, n_s, n_c, hidden, q, k, v, ga, att, lse, tok, norms, weights, part, small, out_bias, gfirst, second,
        bank, fl, n2, sl, mg, gcq, mx,
    )
    grad_head = small[9:11].reshape(4, local)
    grad_up_bias = small[11 : 11 + up_sums.size // width].reshape(-1)
    pieces = dict(zip(("up", "down"), jnp.split(hidden_grads.astype(jnp.float32), 2, axis=1)))
    edge = 0
    for name, count in groups:
        pieces[name] = grads[:, edge * TILE : (edge + count) * TILE].astype(jnp.float32)
        edge += count
    return (
        result[None],
        grad_tokens[None],
        grad_neighbours,
        small[0:3],
        small[3:6],
        grad_head,
        small[6:9],
        grad_up_bias,
        pieces["self_in"].reshape(slice_rows, 3, local),
        pieces["self_out"].T,
        pieces["cross_q"],
        pieces["memory"].reshape(slice_rows, 2, local),
        pieces["cross_out"].T,
        pieces["up"],
        pieces["down"].T,
    )


def solution(mesh):
    placed = (
        P("shard", "ctx", None),
        P("shard", "ctx", None),
        P("shard", "ctx", None, None),
        P("shard", "ctx", None),
        P(),
        P(),
        P(None, "tp"),
        P(),
        P("tp"),
        P("shard", None, "tp"),
        P("tp", "shard"),
        P("shard", "tp"),
        P("shard", None, "tp"),
        P("tp", "shard"),
        P("shard", "tp"),
        P("tp", "shard"),
    )
    return jax.shard_map(
        shards,
        mesh=mesh,
        in_specs=placed,
        out_specs=(
            P("shard", "ctx", None),
            P("shard", "ctx", None),
            P("shard", "ctx", None, "tp"),
            P(),
            P(),
            P(None, "tp"),
            P(),
            P("tp"),
            P("shard", None, "tp"),
            P("tp", "shard"),
            P("shard", "tp"),
            P("shard", None, "tp"),
            P("tp", "shard"),
            P("shard", "tp"),
            P("tp", "shard"),
        ),
        check_vma=False,
    )
```

```python
from functools import partial

import jax
import jax.numpy as jnp
from jax import lax
from jax.experimental import pallas as pl
from jax.experimental.pallas import tpu as pltpu
from jax.sharding import PartitionSpec as P

HEAD_DIM = 64
BLOCK = 256


EPSILON = 1e-05
NEGATIVE = -1e30
HIGHEST = lax.Precision.HIGHEST


MESH = pl.DeviceIdType.MESH
LOG2E = 1.4426950408889634
TILE = 128


def aligned(index, size):
    return pl.multiple_of(index * size, size)


def rows_at(index, size):
    return pl.ds(pl.multiple_of(index * size, size), size)


def remote(src, dst, send, recv, where):
    return pltpu.make_async_remote_copy(
        src_ref=src, dst_ref=dst, send_sem=send, recv_sem=recv, device_id=where, device_id_type=MESH
    )


class Place:
    def __init__(self, n_s, n_c):
        self.n_s, self.n_c, self.n_x = n_s, n_c, n_c // 2
        self.s, self.c, self.t = lax.axis_index("shard"), lax.axis_index("ctx"), lax.axis_index("tp")
        self.x, self.core = lax.div(self.c, 2), lax.rem(self.c, 2)
        self.sibling_index = self.x * 2 + 1 - self.core
        self.sibling, self.peer = {"ctx": self.sibling_index}, {"tp": 1 - self.t}

    def along_x(self, d):
        return {"ctx": lax.rem(self.x + d, self.n_x) * 2 + self.core}

    def along_s(self, d):
        return {"shard": lax.rem(self.s + d, self.n_s)}

    def source_x(self, d):
        return lax.rem(self.x - d + self.n_x, self.n_x)

    def greet(self):
        barrier = pltpu.get_barrier_semaphore()
        partners = [self.along_x(d) for d in range(1, self.n_x)] + [self.along_s(d) for d in range(1, self.n_s)]
        partners += [self.sibling, self.peer]
        for where in partners:
            pl.semaphore_signal(barrier, inc=1, device_id=where, device_id_type=MESH)
        pl.semaphore_wait(barrier, len(partners))


def gather_semaphores(chunks, n_s, n_c):
    dma, n_x = pltpu.SemaphoreType.DMA, n_c // 2
    shapes = [(chunks, n_s - 1)] * 2 + [(chunks, n_s - 1, n_x - 1)] * 2 + [(chunks, n_s - 1, n_x)] * 2
    return [dma(shape) for shape in shapes] + [dma((1,))]


class Gather:
    def __init__(self, place, own, full, chunks, base, semaphores):
        self.place, self.own, self.full, self.chunks, self.base = place, own, full, chunks, base
        self.zs, self.zr, self.xs, self.xr, self.cs, self.cr, self.local = semaphores
        self.rows = own.shape[1]
        self.last = chunks + 1
        total = chunks * place.n_c
        self.own_copy = pltpu.make_async_copy(
            own.at[pl.ds(base, total)],
            full.at[pl.ds(base, total), pl.ds(aligned(place.s, self.rows), self.rows), :],
            self.local.at[0],
        )

    def block(self, origin, k, quarter):
        slab = self.base + k * self.place.n_c + quarter
        return self.full.at[slab, pl.ds(aligned(origin, self.rows), self.rows), :]

    def source(self, d):
        return lax.rem(self.place.s - d + self.place.n_s, self.place.n_s)

    def own_out(self, d, k):
        return remote(
            self.own.at[self.base + k * self.place.n_c + self.place.c], self.block(self.place.s, k, self.place.c),
            self.zs.at[k, d - 1], self.zr.at[k, d - 1], self.place.along_s(d),
        )

    def z_in(self, d, k):
        here = self.block(self.source(d), k, self.place.c)
        return remote(here, here, self.zs.at[k, d - 1], self.zr.at[k, d - 1], self.place.along_s(d))

    def x_move(self, d, k, e, incoming):
        quarter = self.place.source_x(e) * 2 + self.place.core if incoming else self.place.c
        here = self.block(self.source(d), k, quarter)
        return remote(here, here, self.xs.at[k, d - 1, e - 1], self.xr.at[k, d - 1, e - 1], self.place.along_x(e))

    def core_move(self, d, k, e, incoming):
        core = 1 - self.place.core if incoming else self.place.core
        here = self.block(self.source(d), k, self.place.source_x(e) * 2 + core)
        return remote(here, here, self.cs.at[k, d - 1, e], self.cr.at[k, d - 1, e], self.place.sibling)

    def each(self, low, high, body):
        def one(i, carry):
            body(i)
            return carry

        lax.fori_loop(low, high, one, 0)

    def start(self):
        self.own_copy.start()

        def send(k):
            for d in range(1, self.place.n_s):
                self.own_out(d, k).start()

        self.each(0, self.chunks, send)

    def advance(self, i):
        @pl.when(i < self.chunks)
        def _():
            for d in range(1, self.place.n_s):
                self.z_in(d, i).wait_recv()
                for e in range(1, self.place.n_x):
                    self.x_move(d, i, e, False).start()
                self.core_move(d, i, 0, False).start()

        @pl.when(i > 0)
        def _():
            for d in range(1, self.place.n_s):
                for e in range(1, self.place.n_x):
                    self.x_move(d, i - 1, e, True).wait_recv()
                    self.core_move(d, i - 1, e, False).start()

    def advance_range(self, low, high):
        self.each(low, high, self.advance)

    def complete_range(self, low, high):
        def one(k):
            for d in range(1, self.place.n_s):
                for e in range(self.place.n_x):
                    self.core_move(d, k, e, True).wait_recv()

        self.each(low, high, one)

    def finish(self):
        def one(k):
            for d in range(1, self.place.n_s):
                self.own_out(d, k).wait_send()
                for e in range(1, self.place.n_x):
                    self.x_move(d, k, e, False).wait_send()
                for e in range(self.place.n_x):
                    self.core_move(d, k, e, False).wait_send()

        self.each(0, self.chunks, one)


RING = 16


def cross_scratch(chunks, width, n_s, n_c):
    bf16, vmem, dma, n_x = jnp.bfloat16, pltpu.VMEM, pltpu.SemaphoreType.DMA, n_c // 2
    return [
        vmem((min(max(RING // n_c, 2), chunks), n_c, width, TILE), bf16),
        vmem((chunks, n_x, width, TILE), bf16),
        vmem((chunks, n_x - 1, width, TILE), bf16),
        dma((chunks, n_x)), dma((chunks, n_x)), dma((chunks, n_x - 1)), dma((chunks, n_x - 1)),
    ]


def spread_scratch(chunks, width, n_s, n_c):
    bf16, vmem, dma, n_x = jnp.bfloat16, pltpu.VMEM, pltpu.SemaphoreType.DMA, n_c // 2
    rows = width // n_s
    return [
        vmem((chunks, n_s - 1, rows, TILE), bf16),
        dma((chunks, n_s - 1)), dma((chunks, n_s - 1)),
        dma((chunks, n_x - 1)), dma((chunks, n_x - 1)), dma((chunks, n_x)), dma((chunks, n_x)),
    ]


class Cross:
    def __init__(self, place, total, refs):
        self.place, self.total = place, total
        self.gbuf, self.a_buf, self.b_buf, self.as_, self.ar, self.bs, self.br = refs
        self.chunks, self.ring = self.a_buf.shape[0], self.gbuf.shape[0]

    def a_out(self, kk, e):
        slot = lax.rem(kk, self.ring)
        source = self.gbuf.at[slot, e * 2 + 1 - self.place.core]
        return remote(source, self.a_buf.at[kk, e], self.as_.at[kk, e], self.ar.at[kk, e], self.place.sibling)

    def reserve(self, kk):
        if kk >= self.ring:
            for e in range(self.place.n_x):
                self.a_out(kk - self.ring, e).wait_send()
        return kk % self.ring

    def send(self, kk):
        for e in range(self.place.n_x):
            self.a_out(kk, e).start()

    def b_out(self, kk, d):
        to = lax.rem(self.place.x + d, self.place.n_x)
        return remote(
            self.a_buf.at[kk, to], self.b_buf.at[kk, d - 1], self.bs.at[kk, d - 1], self.br.at[kk, d - 1],
            self.place.along_x(d),
        )

    def stage_b(self, kk):
        f32 = jnp.float32
        x, core, slot = self.place.x, self.place.core, lax.rem(kk, self.ring)
        for d in range(1, self.place.n_x):
            e = lax.rem(x + d, self.place.n_x)
            self.a_out(kk, e).wait_recv()
            total = self.gbuf[slot, e * 2 + core].astype(f32) + self.a_buf[kk, e].astype(f32)
            self.a_buf[kk, e] = total.astype(jnp.bfloat16)
            self.b_out(kk, d).start()
        self.a_out(kk, x).wait_recv()
        self.a_buf[kk, x] = (
            self.gbuf[slot, self.place.c].astype(f32) + self.a_buf[kk, x].astype(f32)
        ).astype(jnp.bfloat16)

    def stage_c(self, kk):
        total = self.a_buf[kk, self.place.x].astype(jnp.float32)
        for d in range(1, self.place.n_x):
            self.b_out(kk, d).wait_recv()
            total = total + self.b_buf[kk, d - 1].astype(jnp.float32)
        self.total[kk] = total.astype(jnp.bfloat16)

    def step(self, i, produce, low, high):
        for kk in range(low, high):
            pl.when(i == kk)(partial(produce, kk))
        for lag, stage in ((1, self.stage_b), (2, self.stage_c)):
            kk = i - lag
            pl.when((kk >= 0) & (kk < self.chunks))(partial(stage, kk))

    def finish(self):
        def one(kk, carry):
            @pl.when(kk >= max(self.chunks - self.ring, 0))
            def _():
                for e in range(self.place.n_x):
                    self.a_out(kk, e).wait_send()

            for d in range(1, self.place.n_x):
                self.b_out(kk, d).wait_send()
            return carry

        lax.fori_loop(0, self.chunks, one, 0)


class Spread:
    def __init__(self, place, total, res, refs):
        self.place, self.total, self.res = place, total, res
        self.z_in, self.zs, self.zr, self.fs, self.fr, self.hs, self.hr = refs
        self.chunks, self.rows = self.z_in.shape[0], self.z_in.shape[2]

    def shard_rows(self, index):
        return pl.ds(aligned(index, self.rows), self.rows)

    def z_copy(self, d, kk):
        theirs = self.shard_rows(lax.rem(self.place.s + d, self.place.n_s))
        return remote(
            self.total.at[kk, theirs, :], self.z_in.at[kk, d - 1], self.zs.at[kk, d - 1], self.zr.at[kk, d - 1],
            self.place.along_s(d),
        )

    def send(self, kk):
        for d in range(1, self.place.n_s):
            self.z_copy(d, kk).start()

    def block(self, kk, quarter):
        return self.res.at[:, pl.ds(pl.multiple_of((kk * self.place.n_c + quarter) * TILE, TILE), TILE)]

    def f_move(self, kk, d, incoming):
        here = self.block(kk, self.place.source_x(d) * 2 + self.place.core if incoming else self.place.c)
        return remote(here, here, self.fs.at[kk, d - 1], self.fr.at[kk, d - 1], self.place.along_x(d))

    def h_move(self, kk, d, incoming):
        core = 1 - self.place.core if incoming else self.place.core
        here = self.block(kk, self.place.source_x(d) * 2 + core)
        return remote(here, here, self.hs.at[kk, d], self.hr.at[kk, d], self.place.sibling)

    def stage_d(self, kk):
        total = self.total[kk, self.shard_rows(self.place.s), :].astype(jnp.float32)
        for d in range(1, self.place.n_s):
            self.z_copy(d, kk).wait_recv()
            total = total + self.z_in[kk, d - 1].astype(jnp.float32)
        lanes = pl.ds(pl.multiple_of((kk * self.place.n_c + self.place.c) * TILE, TILE), TILE)
        self.res[:, lanes] = total.astype(jnp.bfloat16)
        for d in range(1, self.place.n_x):
            self.f_move(kk, d, False).start()
        self.h_move(kk, 0, False).start()

    def stage_e(self, kk):
        for d in range(1, self.place.n_x):
            self.f_move(kk, d, True).wait_recv()
            self.h_move(kk, d, False).start()

    def stage_f(self, kk):
        for d in range(self.place.n_x):
            self.h_move(kk, d, True).wait_recv()

    def step(self, i):
        for lag, stage in ((0, self.stage_d), (1, self.stage_e), (2, self.stage_f)):
            kk = i - lag
            pl.when((kk >= 0) & (kk < self.chunks))(partial(stage, kk))

    def finish(self):
        def one(kk, carry):
            for d in range(1, self.place.n_x):
                self.f_move(kk, d, False).wait_send()
            for d in range(self.place.n_x):
                self.h_move(kk, d, False).wait_send()
            for d in range(1, self.place.n_s):
                self.z_copy(d, kk).wait_send()
            return carry

        lax.fori_loop(0, self.chunks, one, 0)


def produce_group(cross, order, kk, left_of, slab_of):
    slot, at, n_c = cross.reserve(kk), 0, cross.place.n_c
    while at < n_c:
        name, index = order[kk * n_c + at]
        count = 1
        while at + count < n_c and order[kk * n_c + at + count][0] == name:
            count += 1
        right = jnp.concatenate([slab_of(name, index + i) for i in range(count)], axis=1)
        product = dot_tn(left_of(name)[...], right).astype(jnp.bfloat16)
        for i in range(count):
            cross.gbuf[slot, at + i] = product[:, i * TILE : (i + 1) * TILE]
        at += count
    cross.send(kk)


def dot_nn(left, right):
    return lax.dot_general(left, right, (((1,), (0,)), ((), ())), preferred_element_type=jnp.float32)


def dot_nt(left, right):
    return lax.dot_general(left, right, (((1,), (1,)), ((), ())), preferred_element_type=jnp.float32)


def dot_tn(left, right):
    return lax.dot_general(left, right, (((0,), (0,)), ((), ())), preferred_element_type=jnp.float32)


def joined(ref, low, high):
    return jnp.concatenate([ref[index] for index in range(low, high)], axis=1)


def norm_parts(values):
    centre = values - jnp.mean(values, axis=-1, keepdims=True)
    spread = jnp.mean(centre * centre, axis=-1, keepdims=True)
    rate = lax.rsqrt(spread + EPSILON)
    return centre * rate, rate


def norm_rows(values, gain, shift):
    return (norm_parts(values)[0] * gain + shift).astype(jnp.bfloat16)


def half_masks(shape):
    lane = lax.broadcasted_iota(jnp.int32, shape, len(shape) - 1)
    return lane < HEAD_DIM


def keep_half(values, low, half):
    zero = jnp.zeros_like(values)
    return jnp.where(low, values, zero) if half == 0 else jnp.where(low, zero, values)


def fold(values, combine):
    result = values[:, :TILE]
    for at in range(TILE, values.shape[1], TILE):
        result = combine(result, values[:, at : at + TILE])
    return result


def attend(c, q, k, v, att, lse, scores, after):
    slabs, length, unused = q.shape
    scale = HEAD_DIM ** (-0.5) * LOG2E
    low = half_masks((length, TILE))
    lane = lax.broadcasted_iota(jnp.int32, (length, TILE), 1)
    steps = [(low_row, low_row + BLOCK) for low_row in range(0, length, BLOCK)]

    def one(p, carry):
        outs = []
        logs = lse[...]
        for half in (0, 1):
            part = keep_half(q[p], low, half)

            def first(j, peak):
                s = dot_nt(part, k[p, rows_at(j, length), :]) * scale
                scores[j] = s
                return jnp.maximum(peak, fold(s, jnp.maximum))

            peak = lax.fori_loop(0, c, first, jnp.full((length, TILE), NEGATIVE, jnp.float32))
            own_keys, own_values = k[p, rows_at(c, length), :], v[p, rows_at(c, length), :]
            tops = []
            for begin, end in steps:
                s = dot_nt(part[begin:end], own_keys[:end]) * scale
                scores[c, begin:end, :end] = s
                best = jnp.maximum(peak[begin:end], fold(s, jnp.maximum))
                tops.append(jnp.max(best, axis=1, keepdims=True))
            top = jnp.concatenate(tops, axis=0)

            def second(j, state):
                raised = jnp.exp2(scores[j] - top)
                mixed = dot_nn(raised.astype(jnp.bfloat16), v[p, rows_at(j, length), :])
                return state[0] + fold(raised, jnp.add), state[1] + mixed

            zero = jnp.zeros((length, TILE), jnp.float32)
            total, mixed = lax.fori_loop(0, c, second, (zero, zero))
            totals, mixes = [], []
            for (begin, end), best in zip(steps, tops):
                raised = jnp.exp2(scores[c, begin:end, :end] - best)
                totals.append(total[begin:end] + fold(raised, jnp.add))
                mixes.append(mixed[begin:end] + dot_nn(raised.astype(jnp.bfloat16), own_values[:end]))
            total = jnp.sum(jnp.concatenate(totals, axis=0), axis=1, keepdims=True)
            outs.append(jnp.concatenate(mixes, axis=0) / total)
            logs = jnp.where(lane == p * 2 + half, top + jnp.log2(total), logs)
            after(p * 2 + half)
        lse[...] = logs
        att[p] = jnp.where(low, outs[0], outs[1]).astype(jnp.bfloat16)
        return carry

    lse[...] = jnp.zeros_like(lse)
    lax.fori_loop(0, slabs, one, 0)


def front_kernel(
    n_s, n_c, chunks, shard, tok, gains, shifts, bias, w, q, k, v, att, lse,
    others, normed, scores, zs, zr, xs, xr, cs, cr, own_sem, txs, txr, tys, tyr, tcs, tcr,
):
    place = Place(n_s, n_c)
    c, x, core, n_x = place.c, place.x, place.core, place.n_x
    length, width = tok.shape
    slabs = q.shape[0]
    place.greet()
    gather = Gather(place, shard, w, chunks, 0, (zs, zr, xs, xr, cs, cr, own_sem))

    half = length // 2

    def token_half(index, which):
        return others.at[pl.ds(pl.multiple_of(index * length + which * half, half), half), :]

    def run(pair, method):
        copy, valid = pair
        pl.when(valid)(getattr(copy, method))

    def token_x(d):
        own_half = tok.at[pl.ds(pl.multiple_of(place.t * half, half), half), :]
        copy = remote(own_half, token_half(c, place.t), txs.at[d - 1], txr.at[d - 1], place.along_x(d))
        return copy, lax.rem(x + d, n_x) > x

    def token_in(d):
        here = token_half(place.source_x(d) * 2 + core, place.t)
        return remote(here, here, txs.at[d - 1], txr.at[d - 1], place.sibling), place.source_x(d) < x

    def token_peer(d, incoming):
        here = token_half(place.source_x(d) * 2 + core, 1 - place.t if incoming else place.t)
        return remote(here, here, tys.at[d - 1], tyr.at[d - 1], place.peer), place.source_x(d) < x

    def token_relay(d, which, incoming):
        here = token_half(place.source_x(d) * 2 + (1 - core if incoming else core), which)
        return remote(here, here, tcs.at[d, which], tcr.at[d, which], place.sibling), place.source_x(d) < x

    def token_own(which):
        own_half = tok.at[pl.ds(which * half, half), :]
        return remote(own_half, token_half(c, which), tcs.at[0, which], tcr.at[0, which], place.sibling), core == 0

    def token_own_in(which):
        here = token_half(place.sibling_index, which)
        return remote(here, here, tcs.at[0, which], tcr.at[0, which], place.sibling), core == 1

    for d in range(1, n_x):
        run(token_x(d), "start")
    for which in (0, 1):
        run(token_own(which), "start")
    gather.start()

    def norm_block(source, base, j):
        def tile(i, carry):
            rows = source[pl.ds(pl.multiple_of(base + i * TILE, TILE), TILE), :].astype(jnp.float32)
            normed[j, rows_at(i, TILE), :] = norm_rows(rows, gains[0:1, :], shifts[0:1, :])
            return carry

        lax.fori_loop(0, length // TILE, tile, 0)

    norm_block(tok, 0, c)
    needed = -(-3 * slabs // n_c)
    ready = min(needed + 1, gather.last)
    gather.advance_range(0, 1)
    for d in range(1, n_x):
        run(token_in(d), "wait_recv")
        run(token_peer(d, False), "start")
        for which in (0, 1):
            pl.when(place.t == which)(lambda: run(token_relay(d, which, False), "start"))
    gather.advance_range(1, 2)
    for d in range(1, n_x):
        run(token_peer(d, True), "wait_recv")
        for which in (0, 1):
            pl.when(place.t != which)(lambda: run(token_relay(d, which, False), "start"))
    gather.advance_range(2, ready)
    for which in (0, 1):
        for d in range(1, n_x):
            run(token_relay(d, which, True), "wait_recv")
        run(token_own_in(which), "wait_recv")

    def norm_other(j, carry):
        norm_block(others, j * length, j)
        return carry

    lax.fori_loop(0, c, norm_other, 0)
    gather.own_copy.wait()
    gather.complete_range(0, needed)

    def project(j, which, row_bias):
        result = dot_nn(normed[j], joined(w, which * slabs, (which + 1) * slabs))
        if row_bias is not None:
            result = result + row_bias
        return result.astype(jnp.bfloat16)

    def project_keys(j, carry):
        spot = rows_at(j, length)
        for which, target, row_bias in ((1, k, None), (2, v, bias[1:2, :])):
            result = project(j, which, row_bias)
            for p in range(slabs):
                target[p, spot, :] = result[:, p * TILE : (p + 1) * TILE]
        return carry

    lax.fori_loop(0, c + 1, project_keys, 0)
    queries = project(c, 0, bias[0:1, :])
    for p in range(slabs):
        q[p] = queries[:, p * TILE : (p + 1) * TILE]
    pieces = 2 * slabs

    def after(step):
        pl.when(ready + step < gather.last)(lambda: gather.advance(ready + step))

    attend(c, q, k, v, att, lse, scores, after)
    gather.advance_range(min(ready + pieces, gather.last), gather.last)
    gather.complete_range(needed, chunks)
    gather.finish()
    for d in range(1, n_x):
        run(token_x(d), "wait_send")
        run(token_peer(d, False), "wait_send")
        for which in (0, 1):
            run(token_relay(d, which, False), "wait_send")
    for which in (0, 1):
        run(token_own(which), "wait_send")


def front(shard, tok, gains, shifts, bias, n_s, n_c, cut):
    total, rows, unused = shard.shape
    length, width = tok.shape
    slabs = bias.shape[1] // TILE
    chunks, n_x = cut // n_c, n_c // 2
    dma, shape, scratch = pltpu.SemaphoreType.DMA, jax.ShapeDtypeStruct, pltpu.VMEM
    vmem = pl.BlockSpec(memory_space=pltpu.VMEM)
    bf16, f32 = jnp.bfloat16, jnp.float32
    return pl.pallas_call(
        partial(front_kernel, n_s, n_c, chunks),
        out_shape=(
            shape((cut, rows * n_s, TILE), bf16),
            shape((slabs, length, TILE), bf16),
            shape((slabs, length * n_c, TILE), bf16),
            shape((slabs, length * n_c, TILE), bf16),
            shape((slabs, length, TILE), bf16),
            shape((length, TILE), f32),
        ),
        in_specs=[vmem] * 5,
        out_specs=(vmem,) * 6,
        scratch_shapes=[
            scratch((length * n_c, width), bf16), scratch((n_c, length, width), bf16),
            scratch((n_c, length, length), f32),
            *gather_semaphores(chunks, n_s, n_c),
            dma((n_x - 1,)), dma((n_x - 1,)), dma((n_x - 1,)), dma((n_x - 1,)), dma((n_x, 2)), dma((n_x, 2)),
        ],
        compiler_params=pltpu.CompilerParams(collective_id=0, has_side_effects=True, vmem_limit_bytes=60 << 20),
        name="front",
    )(shard, tok, gains, shifts, bias)


def chain_kernel(
    at, chunk, banks, n_s, n_c, ids, att, tok, cot, bank, shard, gains, shifts, bias, out_bias, up_bias, w_front,
    n2, sl, fl, mx, gcq, ga, dks, dvs, gfirst, part, second, sums, up_sums, head_sums, total_out,
    mem_k, mem_v, first, gsecond, weights, gmix, cq, tx, rx, ss, rs, w, wsem, n3, act, gh, *engines
):
    place = Place(n_s, n_c)
    peer = place.peer
    cut = w_front.shape[0]
    place.greet()
    gather = Gather(place, shard, w, (shard.shape[0] - cut) // n_c, cut, engines[:7])
    cross = Cross(place, total_out, engines[7:])
    edges = [at["self_out"], at["memory"], cut]

    def load(i):
        low, high = edges[i], edges[i + 1]
        return pltpu.make_async_copy(w_front.at[pl.ds(low, high - low)], w.at[pl.ds(low, high - low)], wsem.at[i])

    load(0).start()
    load(1).start()
    gather.start()
    f32, bf16 = jnp.float32, jnp.bfloat16
    length, width = tok.shape
    slabs = att.shape[0]
    units = act.shape[0]
    span = bank.shape[0] // banks
    stretches, picks = ids.shape
    stretch = length // stretches
    keys_each = picks * span
    scale = HEAD_DIM ** (-0.5)
    count = length // chunk
    tiles = chunk // TILE
    low = half_masks((stretch, TILE))
    sums[...] = jnp.zeros_like(sums)
    up_sums[...] = jnp.zeros_like(up_sums)
    head_sums[...] = jnp.zeros_like(head_sums)

    def exchange(phase, r):
        rows = rows_at(r, chunk)
        return remote(tx.at[phase, rows, :], rx.at[phase, rows, :], ss.at[phase, r], rs.at[phase, r], peer)

    def every(stage):
        def run(r, carry):
            stage(r)
            return carry

        lax.fori_loop(0, count, run, 0)

    def per_tile(r, body):
        def run(i, carry):
            body(pl.ds(pl.multiple_of(r * chunk + i * TILE, TILE), TILE))
            return carry

        lax.fori_loop(0, tiles, run, 0)

    def out_product(target, r, left, name, total):
        rows = rows_at(r, chunk)
        low_slab = at[name]
        step = 256

        def run(n, carry):
            cols = pl.ds(pl.multiple_of(n * step, step), step)
            weight = jnp.concatenate([w[low_slab + i, cols, :] for i in range(total)], axis=1)
            product = dot_nt(jnp.concatenate([left[i, rows, :] for i in range(total)], axis=1), weight)
            target[rows, cols] = product.astype(bf16)
            return carry

        lax.fori_loop(0, width // step, run, 0)

    def send_attended(r):
        out_product(tx.at[0], r, att, "self_out", slabs)
        exchange(0, r).start()

    load(0).wait()
    every(send_attended)
    load(1).wait()
    total = gather.last
    gather.advance_range(0, min(1, total))

    def memory(i, carry):
        rows = rows_at(i, 4 * span)
        for which, target, row_bias in ((0, mem_k, None), (1, mem_v, bias[3:4, :])):
            base = at["memory"] + which * slabs
            product = dot_nn(bank[rows, :], joined(w, base, base + slabs))
            if row_bias is not None:
                product = product + row_bias
            product = product.astype(bf16)
            for p in range(slabs):
                for e in range(4):
                    target[p, i * 4 + e] = product[e * span : (e + 1) * span, p * TILE : (p + 1) * TILE]
        return carry

    lax.fori_loop(0, banks // 4, memory, 0)
    gather.advance_range(min(1, total), min(2, total))

    def narrow(source, r, base, row_bias, target):
        rows = rows_at(r, chunk)
        product = dot_nn(source[rows, :], joined(w, base, base + slabs))
        if row_bias is not None:
            product = product + row_bias
        product = product.astype(bf16)
        for p in range(slabs):
            target[p, rows, :] = product[:, p * TILE : (p + 1) * TILE]

    def picked(source, p, st):
        return jnp.concatenate(
            [source[p, ids[st, n]] for n in range(picks)], axis=0
        )

    def stacked(source, p, st):
        block = source[p, rows_at(st, stretch), :]
        return jnp.concatenate([keep_half(block, low, 0), keep_half(block, low, 1)], axis=0)

    def unstacked(both):
        return jnp.where(low, both[:stretch], both[stretch:])

    def total_of(phase, rows):
        return tx[phase, rows, :].astype(f32) + rx[phase, rows, :].astype(f32)

    def per_stretch(r, body):
        each = chunk // stretch

        def run(i, carry):
            p, inner = lax.div(i, each), lax.rem(i, each)
            body(p, r * each + inner)
            return carry

        lax.fori_loop(0, slabs * each, run, 0)

    def cross_forward(r):
        exchange(0, r).wait_recv()

        def tile(rows):
            value = tok[rows, :].astype(f32) + total_of(0, rows) + out_bias[0:1, :]
            first[rows, :] = value
            n2[rows, :] = norm_rows(value, gains[1:2, :], shifts[1:2, :])

        per_tile(r, tile)
        narrow(n2, r, at["cross_q"], bias[2:3, :], cq)

        def one(p, st):
            keys, values = picked(mem_k, p, st), picked(mem_v, p, st)
            s = dot_nt(stacked(cq, p, st), keys) * (scale * LOG2E)
            raised = jnp.exp2(s - jnp.max(s, axis=1, keepdims=True))
            probs = raised / jnp.sum(raised, axis=1, keepdims=True)
            weights[p, st] = probs
            mixed = dot_nn(probs.astype(bf16), values)
            mx[p, rows_at(st, stretch), :] = unstacked(mixed).astype(bf16)

        per_stretch(r, one)
        out_product(tx.at[1], r, mx, "cross_out", slabs)
        exchange(1, r).start()
        gather.advance_range(lax.min(2 + r, total), lax.min(3 + r, total))

    every(cross_forward)
    gather.advance_range(min(2 + count, total), total)
    gather.own_copy.wait()
    gather.complete_range(0, gather.chunks)
    curve = 0.7978845608028654
    cubic = 0.044715

    def feed(r):
        exchange(1, r).wait_recv()
        rows_all = rows_at(r, chunk)

        def tile(rows):
            value = first[rows, :] + total_of(1, rows) + out_bias[1:2, :]
            second[rows, :] = value
            n3[rows, :] = norm_rows(value, gains[2:3, :], shifts[2:3, :])

        per_tile(r, tile)

        def unit(j, carry):
            up = jnp.concatenate([w[at["up"] + 2 * j], w[at["up"] + 2 * j + 1]], axis=1)
            down = jnp.concatenate([w[at["down"] + 2 * j], w[at["down"] + 2 * j + 1]], axis=1)
            hidden = dot_nn(n3[rows_all, :], up) + up_bias[j]
            back = dot_nn(cot[rows_all, :], down)
            square = hidden * hidden
            bent = jnp.tanh(curve * hidden * (1.0 + cubic * square))
            half = 0.5 * (1.0 + bent)
            active = (hidden * half).astype(bf16)
            slope = half + 0.5 * hidden * (1.0 - bent * bent) * (curve * (1.0 + 3.0 * cubic * square))
            grad = (slope * back).astype(bf16)
            up_sums[j] = up_sums[j] + jnp.sum(grad.astype(f32), axis=0, keepdims=True)
            for i in range(2):
                lanes = slice(i * TILE, (i + 1) * TILE)
                act[2 * j + i, rows_all, :] = active[:, lanes]
                gh[2 * j + i, rows_all, :] = grad[:, lanes]
            return carry

        lax.fori_loop(0, units // 2, unit, 0)
        out_product(tx.at[2], r, gh, "up", units)
        exchange(2, r).start()

    every(feed)

    def result_product(r):
        out_product(part, r, act, "down", units)

    order = [(name, index) for name in ("up", "down") for index in range(units)]

    def left_of(name):
        return n3 if name == "up" else cot

    def slab_of(name, index):
        return (gh if name == "up" else act)[index]

    def produce(kk):
        produce_group(cross, order, kk, left_of, slab_of)

    steps = cross.chunks + 2

    def reduce_range(low, high):
        def one(i, carry):
            cross.step(i, produce, 0, cross.chunks)
            return carry

        lax.fori_loop(lax.min(low, steps), lax.min(high, steps), one, 0)

    def result_and_step(r):
        result_product(r)
        reduce_range(r, r + 1)

    every(result_and_step)

    def norm_back_rows(value, gain, upstream, row):
        spot, rate = norm_parts(value)
        scaled = upstream * gain
        sums[row : row + 1, :] = sums[row : row + 1, :] + jnp.sum(upstream * spot, axis=0, keepdims=True)
        sums[row + 3 : row + 4, :] = sums[row + 3 : row + 4, :] + jnp.sum(upstream, axis=0, keepdims=True)
        return rate * (
            scaled - jnp.mean(scaled, axis=-1, keepdims=True)
            - spot * jnp.mean(scaled * spot, axis=-1, keepdims=True)
        )

    def add_sum(row, values):
        sums[row : row + 1, :] = sums[row : row + 1, :] + jnp.sum(values, axis=0, keepdims=True)

    def cross_back(r):
        reduce_range(count + 2 * r, count + 2 * r + 1)
        exchange(2, r).wait_recv()

        def tile(rows):
            upstream = cot[rows, :].astype(f32)
            grad = upstream + norm_back_rows(second[rows, :], gains[2:3, :], total_of(2, rows), 2)
            add_sum(8, upstream)
            add_sum(7, grad)
            gsecond[rows, :] = grad
            sl[rows, :] = grad.astype(bf16)

        per_tile(r, tile)
        narrow(sl, r, at["cross_out"], None, gmix)

        def one(p, st):
            keys, values = picked(mem_k, p, st), picked(mem_v, p, st)
            grads, queries = stacked(gmix, p, st), stacked(cq, p, st)
            probs = weights[p, st]
            spread = dot_nt(grads, values)
            ds = (probs * (spread - jnp.sum(probs * spread, axis=1, keepdims=True))).astype(bf16)
            back = unstacked(dot_nn(ds, keys)) * scale
            gcq[p, rows_at(st, stretch), :] = back.astype(bf16)
            dks[p, rows_at(st, keys_each), :] = (dot_tn(ds, queries) * scale).astype(bf16)
            dvs[p, rows_at(st, keys_each), :] = dot_tn(probs.astype(bf16), grads).astype(bf16)

        per_stretch(r, one)
        out_product(tx.at[3], r, gcq, "cross_q", slabs)
        exchange(3, r).start()
        reduce_range(count + 2 * r + 1, count + 2 * r + 2)

    every(cross_back)

    def finish(r):
        exchange(3, r).wait_recv()

        def tile(rows):
            grad = gsecond[rows, :] + norm_back_rows(first[rows, :], gains[1:2, :], total_of(3, rows), 1)
            add_sum(6, grad)
            gfirst[rows, :] = grad
            fl[rows, :] = grad.astype(bf16)

        per_tile(r, tile)
        narrow(fl, r, at["self_out"], None, ga)
        reduce_range(3 * count + r, 3 * count + r + 1)

    every(finish)
    for p in range(slabs):
        head_sums[p] = jnp.sum(gcq[p].astype(f32), axis=0, keepdims=True)

    reduce_range(4 * count, steps)
    gather.finish()
    cross.finish()

    def settle(r):
        for phase in range(4):
            exchange(phase, r).wait_send()

    every(settle)


def chain(at, ids, att, tok, cot, bank, shard, gains, shifts, bias, out_bias, up_bias, w_front, banks, chunk, n_s, n_c):
    length, width = tok.shape
    slabs = att.shape[0]
    units = up_bias.shape[0] // TILE
    stretches, picks = ids.shape
    stretch, span = length // stretches, bank.shape[0] // banks
    keys_each = picks * span
    bf16, f32 = jnp.bfloat16, jnp.float32
    vmem, smem = pl.BlockSpec(memory_space=pltpu.VMEM), pl.BlockSpec(memory_space=pltpu.SMEM)
    shape = jax.ShapeDtypeStruct
    scratch = pltpu.VMEM
    row_slabs = shape((slabs, length, TILE), bf16)
    rows = shape((length, width), bf16)
    anywhere = pl.BlockSpec(memory_space=pl.ANY)
    chunks = 2 * units // n_c
    return pl.pallas_call(
        partial(chain_kernel, at, chunk, banks, n_s, n_c),
        out_shape=(
            rows, rows, rows,
            row_slabs, row_slabs, row_slabs,
            shape((slabs, stretches * keys_each, TILE), bf16), shape((slabs, stretches * keys_each, TILE), bf16),
            shape((length, width), f32), rows, shape((length, width), f32),
            shape((16, width), f32), shape((units // 2, 1, 2 * TILE), f32), shape((slabs, 1, TILE), f32),
            shape((chunks, width, TILE), bf16),
        ),
        in_specs=[smem] + [vmem] * 10 + [anywhere],
        out_specs=(vmem,) * 15,
        scratch_shapes=[
            scratch((slabs, banks, span, TILE), bf16), scratch((slabs, banks, span, TILE), bf16),
            scratch((length, width), f32), scratch((length, width), f32),
            scratch((slabs, stretches, 2 * stretch, keys_each), f32),
            scratch((slabs, length, TILE), bf16), scratch((slabs, length, TILE), bf16),
            scratch((4, length, width), bf16), scratch((4, length, width), bf16),
            pltpu.SemaphoreType.DMA((4, length // chunk)), pltpu.SemaphoreType.DMA((4, length // chunk)),
            scratch((shard.shape[0], width, TILE), bf16), pltpu.SemaphoreType.DMA((2,)),
            scratch((length, width), bf16),
            scratch((units, length, TILE), bf16), scratch((units, length, TILE), bf16),
            *gather_semaphores((shard.shape[0] - w_front.shape[0]) // n_c, n_s, n_c),
            *cross_scratch(chunks, width, n_s, n_c),
        ],
        compiler_params=pltpu.CompilerParams(collective_id=2, has_side_effects=True, vmem_limit_bytes=63 << 20),
        name="chain",
    )(ids, att, tok, cot, bank, shard, gains, shifts, bias, out_bias, up_bias.reshape(units // 2, 1, 2 * TILE), w_front)


def bank_kernel(span, at, ids, dks, dvs, w_all, mg, mine, send, head_sums, acc, w, ws):
    t = lax.axis_index("tp")
    f32, bf16 = jnp.float32, jnp.bfloat16
    slabs = dks.shape[0]
    stretches, picks = ids.shape
    acc[...] = jnp.zeros_like(acc)
    w_copy = pltpu.make_async_copy(w_all.at[pl.ds(at, 2 * slabs)], w, ws)
    w_copy.start()

    def add(i, carry):
        st, n = lax.div(i, picks), lax.rem(i, picks)
        rows = rows_at(ids[st, n], span)
        source = rows_at(i, span)
        for p in range(slabs):
            acc[p, rows, :] = acc[p, rows, :] + dks[p, source, :].astype(f32)
            acc[slabs + p, rows, :] = acc[slabs + p, rows, :] + dvs[p, source, :].astype(f32)
        return carry

    lax.fori_loop(0, stretches * picks, add, 0)
    half = mine.shape[1]
    w_copy.wait()
    total = jnp.zeros((1, slabs * TILE), f32)

    def one(i, sums):
        rows = rows_at(i, BLOCK)
        for p in range(2 * slabs):
            mg[p, rows, :] = acc[p, rows, :].astype(bf16)
        left = jnp.concatenate([mg[p, rows, :] for p in range(2 * slabs)], axis=1)
        for which, target in ((t, mine), (1 - t, send)):
            cols = pl.ds(pl.multiple_of(which * half, half), half)
            weight = jnp.concatenate([w[p, cols, :] for p in range(2 * slabs)], axis=1)
            target[rows, :] = dot_nt(left, weight).astype(target.dtype)
        return sums + jnp.sum(left[:, slabs * TILE :].astype(f32), axis=0, keepdims=True)

    total = lax.fori_loop(0, mine.shape[0] // BLOCK, one, total)
    for p in range(slabs):
        head_sums[p] = total[:, p * TILE : (p + 1) * TILE]


def bank_back(ids, dks, dvs, w, at, banks, span):
    slabs = dks.shape[0]
    rows, half = banks * span, w.shape[1] // 2
    bf16, f32 = jnp.bfloat16, jnp.float32
    vmem, smem = pl.BlockSpec(memory_space=pltpu.VMEM), pl.BlockSpec(memory_space=pltpu.SMEM)
    shape = jax.ShapeDtypeStruct
    return pl.pallas_call(
        partial(bank_kernel, span, at),
        out_shape=(
            shape((2 * slabs, rows, TILE), bf16), shape((rows, half), bf16),
            shape((rows, half), bf16), shape((slabs, 1, TILE), f32),
        ),
        in_specs=[smem, vmem, vmem, pl.BlockSpec(memory_space=pl.ANY)],
        out_specs=(vmem,) * 4,
        scratch_shapes=[
            pltpu.VMEM((2 * slabs, rows, TILE), f32), pltpu.VMEM((2 * slabs, w.shape[1], TILE), bf16),
            pltpu.SemaphoreType.DMA,
        ],
        compiler_params=pltpu.CompilerParams(vmem_limit_bytes=62 << 20),
        name="bank_back",
    )(ids, dks, dvs, w)


def tail_kernel(
    n_s, n_c, groups, early,
    q, k, v, up, att, lse, tok, norms, w_all, down_part, small_in, out_bias, gfirst, second, bank, bank_send, fl, n2, sl, mg, gcq, mx, hidden,
    gtok, result, res, res_hidden, small_out, bank_in,
    dk, dv, qm, um, lse_t, delta_t, dq_acc, dq, gk, gv, n1, core_in, x_in, tx, rx, rx_part, stage32, w,
    bank_here, totals, sm_mine, sm_core, sm_x, sm_z,
    cs, cr, xs, xr, ts, tr, ds_, ms, mr, ps, pr, es, ws, ns, nr, *engine
):
    f32, bf16 = jnp.float32, jnp.bfloat16
    place = Place(n_s, n_c)
    s, c, x, core, n_x = place.s, place.c, place.x, place.core, place.n_x
    sibling, peer = place.sibling, place.peer
    slabs, length, unused = q.shape
    width = tok.shape[1]
    per = length // BLOCK
    scale = HEAD_DIM ** (-0.5)
    place.greet()
    cross = Cross(place, totals, engine[:7])
    spread = Spread(place, totals, res, engine[7:14])
    extra = Spread(place, hidden, res_hidden, engine[14:])
    chunks = cross.chunks
    bank_copy = pltpu.make_async_copy(bank, bank_here, ds_)
    bank_copy.start()

    def send_hidden(kk, carry):
        extra.send(kk)
        return carry

    lax.fori_loop(0, extra.chunks, send_hidden, 0)
    part_copy = remote(down_part, rx_part, ps, pr, peer)
    neighbour_copy = remote(bank_send, bank_in, ns, nr, peer)
    neighbour_copy.start()
    w_copy = pltpu.make_async_copy(w_all.at[pl.ds(0, 3 * slabs)], w, ws)
    w_copy.start()

    def staged(source, r):
        return pltpu.make_async_copy(source.at[rows_at(r, BLOCK), :], stage32.at[r], es.at[r])

    for r in range(per):
        staged(gfirst, r).start()

    def owner_rows(index):
        return pl.ds(pl.multiple_of(index * length, length), length)

    def left_of(name):
        return {"self_in": n1, "memory": bank_here, "self_out": fl, "cross_q": n2, "cross_out": sl}[name]

    def slab_of(name, index):
        if name == "self_in":
            return (dq, gk, gv)[index // slabs][index % slabs]
        return {"memory": mg, "self_out": att, "cross_q": gcq, "cross_out": mx}[name][index]

    order = [(name, index) for name, count in groups for index in range(count)]

    def produce(kk):
        if any(order[kk * n_c + i] == ("memory", 0) for i in range(n_c)):
            bank_copy.wait()
        produce_group(cross, order, kk, left_of, slab_of)

    def loop(low, high, action):
        def run(i, carry):
            action(i)
            return carry

        lax.fori_loop(low, high, run, 0)

    def produce_some(i, low, high):
        for kk in range(low, high):
            pl.when(i == kk)(partial(produce, kk))

    def sum_and_send(kk):
        cross.stage_c(kk)
        spread.send(kk)


    low_all = half_masks((length, TILE))
    lse_t[...] = lse[...].T
    dq_acc[...] = jnp.zeros_like(dq_acc)

    def prepare(p, carry):
        for half in (0, 1):
            qm[p, half] = keep_half(q[p], low_all, half)
            um[p, half] = keep_half(up[p], low_all, half)
        prod = (up[p].astype(f32) * att[p].astype(f32)).T
        for half in (0, 1):
            delta_t[p, half] = jnp.sum(prod[half * HEAD_DIM : (half + 1) * HEAD_DIM, :], axis=0, keepdims=True)
        return carry

    lax.fori_loop(0, slabs, prepare, 0)

    def to_core(xo, part):
        theirs = owner_rows(xo * 2 + 1 - core)
        source = (dk if part == 0 else dv).at[:, theirs, :]
        return remote(source, core_in.at[xo, part], cs.at[xo, part], cr.at[xo, part], sibling)

    def to_owner(xo):
        d = x - xo
        return remote(core_in.at[xo], x_in.at[d - 1], xs.at[xo], xr.at[d - 1], {"ctx": xo * 2 + core})

    def from_higher(d):
        return remote(x_in.at[d - 1], x_in.at[d - 1], xs.at[0], xr.at[d - 1], sibling)

    def relay(xo):
        mine = owner_rows(xo * 2 + core)
        for part, source in ((0, dk), (1, dv)):
            to_core(xo, part).wait_recv()
            core_in[xo, part] = (source[:, mine, :].astype(f32) + core_in[xo, part].astype(f32)).astype(bf16)
        to_owner(xo).start()

    points = (x + 1) * slabs

    def key_block(p, spot, size, begin):
        keys, values = k[p, spot, :], v[p, spot, :]
        low_keys = half_masks((size, TILE))
        dk_sum = dv_sum = jnp.zeros((size, TILE), f32)
        back = jnp.zeros((length - begin, TILE), f32)
        for half in (0, 1):
            q_half, u_half = qm[p, half, begin:, :], um[p, half, begin:, :]
            score = dot_nt(keys, q_half) * (scale * LOG2E)
            probs = jnp.exp2(score - lse_t[pl.ds(p * 2 + half, 1), begin:])
            grad = dot_nt(values, u_half)
            slope = (probs * (grad - delta_t[p, half, :, begin:])).astype(bf16)
            dv_sum = dv_sum + dot_nn(probs.astype(bf16), u_half)
            dk_sum = dk_sum + dot_nn(slope, q_half)
            back = back + dot_tn(slope, keep_half(keys, low_keys, half))
        dq_acc[p, begin:, :] = dq_acc[p, begin:, :] + back
        dk[p, spot, :] = (dk_sum * scale).astype(bf16)
        dv[p, spot, :] = dv_sum.astype(bf16)

    def chip(xo, carry):
        def one(p, inner):
            def whole(j, deeper):
                key_block(p, rows_at(j, length), length, 0)
                return deeper

            lax.fori_loop(xo * 2, lax.min(xo * 2 + 2, c), whole, 0)

            @pl.when(xo == x)
            def _():
                for begin in range(0, length, BLOCK):
                    key_block(p, pl.ds(pl.multiple_of(c * length + begin, BLOCK), BLOCK), BLOCK, begin)

            @pl.when((p == 0) & (xo > 0))
            def _():
                relay(xo - 1)

            point = xo * slabs + p

            def between(i):
                produce_some(i, 0, early)
                pl.when(i == early)(lambda: loop(0, early, cross.stage_b))

            share = early + 1
            loop(lax.div(point * share, points), lax.div((point + 1) * share, points), between)
            return inner

        lax.fori_loop(0, slabs, one, 0)

        @pl.when(xo < x)
        def _():
            to_core(xo, 0).start()
            to_core(xo, 1).start()

        return carry

    lax.fori_loop(0, x + 1, chip, 0)

    @pl.when(core == 1)
    def _():
        to_core(x, 0).start()
        to_core(x, 1).start()

    for p in range(slabs):
        dq[p] = (dq_acc[p] * scale).astype(bf16)

    loop(0, extra.chunks, extra.stage_d)

    def norm_tile(i, carry):
        at = rows_at(i, TILE)
        n1[at, :] = norm_rows(tok[at, :].astype(f32), norms[0:1, :], norms[3:4, :])
        return carry

    lax.fori_loop(0, length // TILE, norm_tile, 0)
    loop(0, extra.chunks, extra.stage_e)
    own = owner_rows(c)

    @pl.when(core == 0)
    def _():
        to_core(x, 0).wait_recv()
        to_core(x, 1).wait_recv()

    for d in range(1, n_x):
        pl.when(x + d < n_x)(from_higher(d).wait_recv)
    for part, target in ((0, gk), (1, gv)):
        dq_acc[...] = (dk if part == 0 else dv)[:, own, :].astype(f32)

        @pl.when(core == 0)
        def _():
            dq_acc[...] = dq_acc[...] + core_in[x, part].astype(f32)

        for d in range(1, n_x):

            @pl.when(x + d < n_x)
            def _():
                dq_acc[...] = dq_acc[...] + x_in[d - 1, part].astype(f32)

        target[...] = dq_acc[...].astype(bf16)

    def exchange(r):
        at = rows_at(r, BLOCK)
        return remote(tx.at[at, :], rx.at[at, :], ts.at[r], tr.at[r], peer)

    w_copy.wait()

    def product(r, carry):
        at = rows_at(r, BLOCK)
        left = jnp.concatenate([ref[i, at, :] for ref in (dq, gk, gv) for i in range(slabs)], axis=1)

        def run(n, inner):
            cols = pl.ds(pl.multiple_of(n * 256, 256), 256)
            weight = jnp.concatenate([w[i, cols, :] for i in range(3 * slabs)], axis=1)
            tx[at, cols] = dot_nt(left, weight).astype(bf16)
            return inner

        lax.fori_loop(0, width // 256, run, 0)
        exchange(r).start()
        return carry

    lax.fori_loop(0, per, product, 0)

    part_copy.start()
    loop(early, chunks, lambda i: produce_some(i, early, chunks))
    loop(0, extra.chunks, extra.stage_f)
    loop(0, early, sum_and_send)
    loop(early, chunks, cross.stage_b)
    sm_mine[...] = small_in[...]
    for index, source in ((0, dq), (1, gv)):
        for p in range(slabs):
            lanes = slice((index * slabs + p) * TILE, (index * slabs + p + 1) * TILE)
            sm_mine[9:10, lanes] = jnp.sum(source[p].astype(f32), axis=0, keepdims=True)

    loop(early, chunks, sum_and_send)

    def last_rows(r, carry):
        exchange(r).wait_recv()
        staged(gfirst, r).wait()

        def tile(i, inner):
            at = pl.ds(pl.multiple_of(r * BLOCK + i * TILE, TILE), TILE)
            spot, rate = norm_parts(tok[at, :].astype(f32))
            upstream = tx[at, :].astype(f32) + rx[at, :].astype(f32)
            scaled = upstream * norms[0:1, :]
            sm_mine[0:1, :] = sm_mine[0:1, :] + jnp.sum(upstream * spot, axis=0, keepdims=True)
            sm_mine[3:4, :] = sm_mine[3:4, :] + jnp.sum(upstream, axis=0, keepdims=True)
            gtok[at, :] = stage32[r, rows_at(i, TILE), :] + rate * (
                scaled - jnp.mean(scaled, axis=-1, keepdims=True)
                - spot * jnp.mean(scaled * spot, axis=-1, keepdims=True)
            )
            return inner

        lax.fori_loop(0, BLOCK // TILE, tile, 0)
        staged(second, r).start()
        return carry

    lax.fori_loop(0, per, last_rows, 0)
    sm_send = remote(sm_mine, sm_core, ms.at[0], mr.at[0], sibling)

    def sm_x_copy(d):
        return remote(sm_x.at[x], sm_x.at[x], ms.at[d], mr.at[d], {"ctx": lax.rem(x + d, n_x) * 2 + core})

    def sm_x_in(d):
        here = sm_x.at[lax.rem(x - d + n_x, n_x)]
        return remote(here, here, ms.at[d], mr.at[d], sibling)

    def sm_z_copy(d):
        return remote(sm_z.at[s], sm_z.at[s], ms.at[n_x + d - 1], mr.at[n_x + d - 1], {"shard": lax.rem(s + d, n_s)})

    def sm_z_in(d):
        here = sm_z.at[lax.rem(s - d + n_s, n_s)]
        return remote(here, here, ms.at[n_x + d - 1], mr.at[n_x + d - 1], peer)

    sm_send.start()

    loop(0, early, spread.stage_d)
    sm_send.wait_recv()
    sm_x[x] = sm_mine[...] + sm_core[...]
    for d in range(1, n_x):
        sm_x_copy(d).start()
    loop(0, early, spread.stage_e)
    for d in range(1, n_x):
        sm_x_in(d).wait_recv()
    both = sm_x[0]
    for e in range(1, n_x):
        both = both + sm_x[e]
    sm_z[s] = both
    for d in range(1, n_s):
        sm_z_copy(d).start()
    loop(0, early, spread.stage_f)
    loop(early, chunks, spread.stage_d)
    loop(early, chunks, spread.stage_e)
    part_copy.wait_recv()

    def result_rows(r, carry):
        staged(second, r).wait()

        def tile(i, inner):
            at = pl.ds(pl.multiple_of(r * BLOCK + i * TILE, TILE), TILE)
            both = down_part[at, :].astype(f32) + rx_part[at, :].astype(f32)
            result[at, :] = (stage32[r, rows_at(i, TILE), :] + both + out_bias[2:3, :]).astype(bf16)
            return inner

        lax.fori_loop(0, BLOCK // TILE, tile, 0)
        return carry

    lax.fori_loop(0, per, result_rows, 0)

    for d in range(1, n_s):
        sm_z_in(d).wait_recv()
    both = sm_z[0]
    for e in range(1, n_s):
        both = both + sm_z[e]
    small_out[...] = both
    loop(early, chunks, spread.stage_f)
    part_copy.wait_send()
    neighbour_copy.wait()
    sm_send.wait_send()
    for d in range(1, n_x):
        sm_x_copy(d).wait_send()
    for d in range(1, n_s):
        sm_z_copy(d).wait_send()

    def settle(xo, carry):
        @pl.when(xo < x)
        def _():
            to_core(xo, 0).wait_send()
            to_core(xo, 1).wait_send()
            to_owner(xo).wait_send()

        @pl.when((xo == x) & (core == 1))
        def _():
            to_core(xo, 0).wait_send()
            to_core(xo, 1).wait_send()

        return carry

    lax.fori_loop(0, x + 1, settle, 0)

    def settle_tp(r, carry):
        exchange(r).wait_send()
        return carry

    lax.fori_loop(0, per, settle_tp, 0)

    cross.finish()
    spread.finish()
    extra.finish()


def tail(groups, n_s, n_c, hidden, q, k, v, up, att, lse, tok, norms, w, part, small, out_bias, gfirst, second, bank, bank_send, *grad_inputs):
    slabs, length, unused = q.shape
    width = tok.shape[1]
    n_x = n_c // 2
    bf16, f32 = jnp.bfloat16, jnp.float32
    vmem, anywhere = pl.BlockSpec(memory_space=pltpu.VMEM), pl.BlockSpec(memory_space=pl.ANY)
    shape, scratch, dma = jax.ShapeDtypeStruct, pltpu.VMEM, pltpu.SemaphoreType.DMA
    pair = (2, slabs, length, TILE)
    total = sum(count for name, count in groups)
    chunks, rows = total // n_c, width // n_s
    early = (total - groups[-1][1]) // n_c
    return pl.pallas_call(
        partial(tail_kernel, n_s, n_c, groups, early),
        out_shape=(
            shape((length, width), f32), shape((length, width), bf16),
            shape((rows, total * TILE), bf16), shape((rows, hidden.shape[0] * n_c * TILE), bf16),
            shape(small.shape, f32), shape(bank_send.shape, bf16),
        ),
        in_specs=[vmem] * 8
        + [anywhere]
        + [vmem] * 3 + [anywhere] * 4 + [vmem] * (len(grad_inputs) + 1),
        out_specs=(vmem,) * 5 + (anywhere,),
        scratch_shapes=[
            scratch(k.shape, bf16), scratch(k.shape, bf16),
            scratch((slabs, 2, length, TILE), bf16), scratch((slabs, 2, length, TILE), bf16),
            scratch((TILE, length), f32), scratch((slabs, 2, 1, length), f32), scratch(q.shape, f32),
            scratch(q.shape, bf16), scratch(q.shape, bf16), scratch(q.shape, bf16),
            scratch((length, width), bf16),
            scratch((n_x,) + pair, bf16), scratch((n_x - 1,) + pair, bf16),
            scratch((length, width), bf16), scratch((length, width), bf16),
            scratch((length, width), bf16), scratch((length // BLOCK, BLOCK, width), f32),
            scratch((3 * slabs, width, TILE), bf16),
            scratch(bank.shape, bf16), scratch((chunks, width, TILE), bf16),
            scratch(small.shape, f32), scratch(small.shape, f32),
            scratch((n_x,) + small.shape, f32), scratch((n_s,) + small.shape, f32),
            dma((n_x, 2)), dma((n_x, 2)), dma((n_x - 1,)), dma((n_x - 1,)),
            dma((length // BLOCK,)), dma((length // BLOCK,)), dma,
            dma((n_x + n_s - 1,)), dma((n_x + n_s - 1,)),
            dma, dma, dma((length // BLOCK,)), dma, dma, dma,
            *cross_scratch(chunks, width, n_s, n_c),
            *spread_scratch(chunks, width, n_s, n_c),
            *spread_scratch(hidden.shape[0], width, n_s, n_c),
        ],
        compiler_params=pltpu.CompilerParams(collective_id=3, has_side_effects=True, vmem_limit_bytes=64 << 20),
        name="tail",
    )(q, k, v, up, att, lse, tok, norms, w, part, small, out_bias, gfirst, second, bank, bank_send, *grad_inputs, hidden)


def final_kernel(
    slabs, units, res, hidden, mine, received, small,
    neigh, gains, shifts, head, outs, up_bias, self_in, self_out, cross_q, memory, cross_out, up, down,
):
    f32 = jnp.float32
    neigh[...] = mine[...].astype(f32) + received[...].astype(f32)
    local = slabs * TILE
    at = 0
    for j in range(2):
        memory[:, j, :] = res[:, (at + j * slabs) * TILE : (at + (j + 1) * slabs) * TILE].astype(f32)
    at += 2 * slabs
    self_out[...] = res[:, at * TILE : (at + slabs) * TILE].astype(f32)
    at += slabs
    cross_q[...] = res[:, at * TILE : (at + slabs) * TILE].astype(f32)
    at += slabs
    cross_out[...] = res[:, at * TILE : (at + slabs) * TILE].astype(f32)
    at += slabs
    for j in range(3):
        self_in[j] = res[:, (at + j * slabs) * TILE : (at + (j + 1) * slabs) * TILE].astype(f32)
    up[...] = hidden[:, : units * TILE].astype(f32)
    down[...] = hidden[:, units * TILE :].astype(f32)
    gains[...] = small[0:3, :]
    shifts[...] = small[3:6, :]
    outs[...] = small[6:9, :]
    width = small.shape[1]
    for j in range(4):
        head[j : j + 1, :] = small[9 + j // 2 : 10 + j // 2, (j % 2) * local : (j % 2 + 1) * local]
    for j in range(units * TILE // width):
        up_bias[:, j * width : (j + 1) * width] = small[11 + j : 12 + j, :]


def final(slabs, units, res, hidden, mine, received, small):
    f32 = jnp.float32
    vmem, shape = pl.BlockSpec(memory_space=pltpu.VMEM), jax.ShapeDtypeStruct
    rows, local, width = res.shape[0], slabs * TILE, small.shape[1]
    return pl.pallas_call(
        partial(final_kernel, slabs, units),
        out_shape=(
            shape(mine.shape, f32), shape((3, width), f32), shape((3, width), f32), shape((4, local), f32),
            shape((3, width), f32), shape((1, units * TILE), f32),
            shape((3, rows, local), f32), shape((rows, local), f32), shape((rows, local), f32),
            shape((rows, 2, local), f32), shape((rows, local), f32),
            shape((rows, units * TILE), f32), shape((rows, units * TILE), f32),
        ),
        in_specs=[vmem] * 5,
        out_specs=(vmem,) * 13,
        compiler_params=pltpu.CompilerParams(vmem_limit_bytes=60 << 20),
        name="final",
    )(res, hidden, mine, received, small)


def slabbed(matrix):
    rows, columns = matrix.shape
    return matrix.reshape(rows, columns // TILE, TILE).transpose(1, 0, 2)


def shards(
    tokens,
    cotangent,
    neighbours,
    neighbour_ids,
    norm_gains,
    norm_shifts,
    head_bias,
    out_bias,
    up_bias,
    self_input,
    self_output,
    cross_query,
    cross_memory,
    cross_output,
    hidden_up,
    hidden_down,
):
    n_s, n_c = lax.axis_size("shard"), lax.axis_size("ctx")
    slice_rows = self_input.shape[0]
    shard = slabbed(
        jnp.concatenate(
            [
                self_input.reshape(slice_rows, -1),
                self_output.T,
                cross_memory.reshape(slice_rows, -1),
                cross_query,
                cross_output.T,
                hidden_up,
                hidden_down.T,
            ],
            axis=1,
        )
    )
    tok, cot = tokens[0], cotangent[0]
    length, width = tok.shape
    local = self_output.shape[0]
    slabs, units = local // TILE, hidden_up.shape[1] // TILE
    counts = (3 * slabs, slabs, 2 * slabs, slabs, slabs, units, units)
    names = ("self_in", "self_out", "memory", "cross_q", "cross_out", "up", "down")
    at, edge = {}, 0
    for name, count in zip(names, counts):
        at[name] = edge
        edge += count
    bank_shape = neighbours.shape[1:]
    bank = neighbours.reshape(bank_shape[0] * bank_shape[1], width)
    ids = neighbour_ids[0]
    cut = at["up"]
    weights, q, k, v, att, lse = front(shard, tok, norm_gains, norm_shifts, head_bias, n_s, n_c, cut)
    n2, sl, fl, mx, gcq, ga, dks, dvs, gfirst, part, second, sums, up_sums, head_cross, hidden = chain(
        at, ids, att, tok, cot, bank, shard, norm_gains, norm_shifts, head_bias, out_bias, up_bias, weights,
        bank_shape[0], BLOCK, n_s, n_c,
    )
    mg, mine, send, head_memory = bank_back(
        ids, dks, dvs, weights, at["memory"], bank_shape[0], bank_shape[1]
    )
    norms = jnp.concatenate([norm_gains, norm_shifts])
    small = jnp.concatenate(
        [
            sums[:9],
            jnp.zeros((1, width), jnp.float32),
            jnp.concatenate([head_cross, head_memory]).reshape(1, width),
            up_sums.reshape(-1, width),
        ]
    )
    small = jnp.pad(small, ((0, 16 - small.shape[0]), (0, 0)))
    lengths = dict(zip(names, counts))
    groups = [(name, lengths[name]) for name in ("memory", "self_out", "cross_q", "cross_out", "self_in")]
    grad_tokens, result, grads, hidden_grads, small, received = tail(
        groups, n_s, n_c, hidden, q, k, v, ga, att, lse, tok, norms, weights, part, small, out_bias, gfirst, second,
        bank, send, fl, n2, sl, mg, gcq, mx,
    )
    (
        neigh, gains, shifts, head, outs, bias_up, self_in, self_out, cross_q, memory, cross_out, up, down,
    ) = final(slabs, units, grads, hidden_grads, mine, received, small)
    return (
        result[None],
        grad_tokens[None],
        neigh.reshape((1,) + bank_shape[:2] + (width // 2,)),
        gains,
        shifts,
        head,
        outs,
        bias_up.reshape(-1),
        self_in.transpose(1, 0, 2),
        self_out.T,
        cross_q,
        memory,
        cross_out.T,
        up,
        down.T,
    )


def solution(mesh):
    placed = (
        P("shard", "ctx", None),
        P("shard", "ctx", None),
        P("shard", "ctx", None, None),
        P("shard", "ctx", None),
        P(),
        P(),
        P(None, "tp"),
        P(),
        P("tp"),
        P("shard", None, "tp"),
        P("tp", "shard"),
        P("shard", "tp"),
        P("shard", None, "tp"),
        P("tp", "shard"),
        P("shard", "tp"),
        P("tp", "shard"),
    )
    return jax.shard_map(
        shards,
        mesh=mesh,
        in_specs=placed,
        out_specs=(
            P("shard", "ctx", None),
            P("shard", "ctx", None),
            P("shard", "ctx", None, "tp"),
            P(),
            P(),
            P(None, "tp"),
            P(),
            P("tp"),
            P("shard", None, "tp"),
            P("tp", "shard"),
            P("shard", "tp"),
            P("shard", None, "tp"),
            P("tp", "shard"),
            P("shard", "tp"),
            P("tp", "shard"),
        ),
        check_vma=False,
    )
```

```python
from functools import partial

import jax
import jax.numpy as jnp
from jax import lax
from jax.experimental import pallas as pl
from jax.experimental.pallas import tpu as pltpu
from jax.sharding import PartitionSpec as P

HEAD_DIM = 64
BLOCK = 256


EPSILON = 1e-05
NEGATIVE = -1e30
HIGHEST = lax.Precision.HIGHEST


MESH = pl.DeviceIdType.MESH
LOG2E = 1.4426950408889634
TILE = 128


def aligned(index, size):
    return pl.multiple_of(index * size, size)


def rows_at(index, size):
    return pl.ds(pl.multiple_of(index * size, size), size)


def remote(src, dst, send, recv, where):
    return pltpu.make_async_remote_copy(
        src_ref=src, dst_ref=dst, send_sem=send, recv_sem=recv, device_id=where, device_id_type=MESH
    )


class Place:
    def __init__(self, n_s, n_c):
        self.n_s, self.n_c, self.n_x = n_s, n_c, n_c // 2
        self.s, self.c, self.t = lax.axis_index("shard"), lax.axis_index("ctx"), lax.axis_index("tp")
        self.x, self.core = lax.div(self.c, 2), lax.rem(self.c, 2)
        self.sibling_index = self.x * 2 + 1 - self.core
        self.sibling, self.peer = {"ctx": self.sibling_index}, {"tp": 1 - self.t}

    def along_x(self, d):
        return {"ctx": lax.rem(self.x + d, self.n_x) * 2 + self.core}

    def along_s(self, d):
        return {"shard": lax.rem(self.s + d, self.n_s)}

    def source_x(self, d):
        return lax.rem(self.x - d + self.n_x, self.n_x)

    def greet(self):
        barrier = pltpu.get_barrier_semaphore()
        partners = [self.along_x(d) for d in range(1, self.n_x)] + [self.along_s(d) for d in range(1, self.n_s)]
        partners += [self.sibling, self.peer]
        for where in partners:
            pl.semaphore_signal(barrier, inc=1, device_id=where, device_id_type=MESH)
        pl.semaphore_wait(barrier, len(partners))


def gather_semaphores(chunks, n_s, n_c):
    dma, n_x = pltpu.SemaphoreType.DMA, n_c // 2
    shapes = [(chunks, n_s - 1)] * 2 + [(chunks, n_s - 1, n_x - 1)] * 2 + [(chunks, n_s - 1, n_x)] * 2
    return [dma(shape) for shape in shapes] + [dma((1,))]


class Gather:
    def __init__(self, place, own, full, chunks, base, semaphores):
        self.place, self.own, self.full, self.chunks, self.base = place, own, full, chunks, base
        self.zs, self.zr, self.xs, self.xr, self.cs, self.cr, self.local = semaphores
        self.rows = own.shape[1]
        self.last = chunks + 1
        total = chunks * place.n_c
        self.own_copy = pltpu.make_async_copy(
            own.at[pl.ds(base, total)],
            full.at[pl.ds(base, total), pl.ds(aligned(place.s, self.rows), self.rows), :],
            self.local.at[0],
        )

    def block(self, origin, k, quarter):
        slab = self.base + k * self.place.n_c + quarter
        return self.full.at[slab, pl.ds(aligned(origin, self.rows), self.rows), :]

    def source(self, d):
        return lax.rem(self.place.s - d + self.place.n_s, self.place.n_s)

    def own_out(self, d, k):
        return remote(
            self.own.at[self.base + k * self.place.n_c + self.place.c], self.block(self.place.s, k, self.place.c),
            self.zs.at[k, d - 1], self.zr.at[k, d - 1], self.place.along_s(d),
        )

    def z_in(self, d, k):
        here = self.block(self.source(d), k, self.place.c)
        return remote(here, here, self.zs.at[k, d - 1], self.zr.at[k, d - 1], self.place.along_s(d))

    def x_move(self, d, k, e, incoming):
        quarter = self.place.source_x(e) * 2 + self.place.core if incoming else self.place.c
        here = self.block(self.source(d), k, quarter)
        return remote(here, here, self.xs.at[k, d - 1, e - 1], self.xr.at[k, d - 1, e - 1], self.place.along_x(e))

    def core_move(self, d, k, e, incoming):
        core = 1 - self.place.core if incoming else self.place.core
        here = self.block(self.source(d), k, self.place.source_x(e) * 2 + core)
        return remote(here, here, self.cs.at[k, d - 1, e], self.cr.at[k, d - 1, e], self.place.sibling)

    def each(self, low, high, body):
        def one(i, carry):
            body(i)
            return carry

        lax.fori_loop(low, high, one, 0)

    def start(self):
        self.own_copy.start()

        def send(k):
            for d in range(1, self.place.n_s):
                self.own_out(d, k).start()

        self.each(0, self.chunks, send)

    def advance(self, i):
        @pl.when(i < self.chunks)
        def _():
            for d in range(1, self.place.n_s):
                self.z_in(d, i).wait_recv()
                for e in range(1, self.place.n_x):
                    self.x_move(d, i, e, False).start()
                self.core_move(d, i, 0, False).start()

        @pl.when(i > 0)
        def _():
            for d in range(1, self.place.n_s):
                for e in range(1, self.place.n_x):
                    self.x_move(d, i - 1, e, True).wait_recv()
                    self.core_move(d, i - 1, e, False).start()

    def advance_range(self, low, high):
        self.each(low, high, self.advance)

    def complete_range(self, low, high):
        def one(k):
            for d in range(1, self.place.n_s):
                for e in range(self.place.n_x):
                    self.core_move(d, k, e, True).wait_recv()

        self.each(low, high, one)

    def finish(self):
        def one(k):
            for d in range(1, self.place.n_s):
                self.own_out(d, k).wait_send()
                for e in range(1, self.place.n_x):
                    self.x_move(d, k, e, False).wait_send()
                for e in range(self.place.n_x):
                    self.core_move(d, k, e, False).wait_send()

        self.each(0, self.chunks, one)


RING = 16


def cross_scratch(chunks, width, n_s, n_c):
    bf16, vmem, dma, n_x = jnp.bfloat16, pltpu.VMEM, pltpu.SemaphoreType.DMA, n_c // 2
    return [
        vmem((min(max(RING // n_c, 2), chunks), n_c, width, TILE), bf16),
        vmem((chunks, n_x, width, TILE), bf16),
        vmem((chunks, n_x - 1, width, TILE), bf16),
        dma((chunks, n_x)), dma((chunks, n_x)), dma((chunks, n_x - 1)), dma((chunks, n_x - 1)),
    ]


def spread_scratch(chunks, width, n_s, n_c):
    bf16, vmem, dma, n_x = jnp.bfloat16, pltpu.VMEM, pltpu.SemaphoreType.DMA, n_c // 2
    rows = width // n_s
    return [
        vmem((chunks, n_s - 1, rows, TILE), bf16),
        dma((chunks, n_s - 1)), dma((chunks, n_s - 1)),
        dma((chunks, n_x - 1)), dma((chunks, n_x - 1)), dma((chunks, n_x)), dma((chunks, n_x)),
    ]


class Cross:
    def __init__(self, place, total, refs):
        self.place, self.total = place, total
        self.gbuf, self.a_buf, self.b_buf, self.as_, self.ar, self.bs, self.br = refs
        self.chunks, self.ring = self.a_buf.shape[0], self.gbuf.shape[0]

    def a_out(self, kk, e):
        slot = lax.rem(kk, self.ring)
        source = self.gbuf.at[slot, e * 2 + 1 - self.place.core]
        return remote(source, self.a_buf.at[kk, e], self.as_.at[kk, e], self.ar.at[kk, e], self.place.sibling)

    def reserve(self, kk):
        if kk >= self.ring:
            for e in range(self.place.n_x):
                self.a_out(kk - self.ring, e).wait_send()
        return kk % self.ring

    def send(self, kk):
        for e in range(self.place.n_x):
            self.a_out(kk, e).start()

    def b_out(self, kk, d):
        to = lax.rem(self.place.x + d, self.place.n_x)
        return remote(
            self.a_buf.at[kk, to], self.b_buf.at[kk, d - 1], self.bs.at[kk, d - 1], self.br.at[kk, d - 1],
            self.place.along_x(d),
        )

    def stage_b(self, kk):
        x, core, slot = self.place.x, self.place.core, lax.rem(kk, self.ring)
        for d in range(1, self.place.n_x):
            e = lax.rem(x + d, self.place.n_x)
            self.a_out(kk, e).wait_recv()
            self.a_buf[kk, e] = self.gbuf[slot, e * 2 + core] + self.a_buf[kk, e]
            self.b_out(kk, d).start()
        self.a_out(kk, x).wait_recv()
        self.a_buf[kk, x] = self.gbuf[slot, self.place.c] + self.a_buf[kk, x]

    def stage_c(self, kk):
        total = self.a_buf[kk, self.place.x]
        for d in range(1, self.place.n_x):
            self.b_out(kk, d).wait_recv()
            total = total + self.b_buf[kk, d - 1]
        self.total[kk] = total

    def step(self, i, produce, low, high):
        for kk in range(low, high):
            pl.when(i == kk)(partial(produce, kk))
        for lag, stage in ((1, self.stage_b), (2, self.stage_c)):
            kk = i - lag
            pl.when((kk >= 0) & (kk < self.chunks))(partial(stage, kk))

    def finish(self):
        def one(kk, carry):
            @pl.when(kk >= max(self.chunks - self.ring, 0))
            def _():
                for e in range(self.place.n_x):
                    self.a_out(kk, e).wait_send()

            for d in range(1, self.place.n_x):
                self.b_out(kk, d).wait_send()
            return carry

        lax.fori_loop(0, self.chunks, one, 0)


class Spread:
    def __init__(self, place, total, res, refs):
        self.place, self.total, self.res = place, total, res
        self.z_in, self.zs, self.zr, self.fs, self.fr, self.hs, self.hr = refs
        self.chunks, self.rows = self.z_in.shape[0], self.z_in.shape[2]

    def shard_rows(self, index):
        return pl.ds(aligned(index, self.rows), self.rows)

    def z_copy(self, d, kk):
        theirs = self.shard_rows(lax.rem(self.place.s + d, self.place.n_s))
        return remote(
            self.total.at[kk, theirs, :], self.z_in.at[kk, d - 1], self.zs.at[kk, d - 1], self.zr.at[kk, d - 1],
            self.place.along_s(d),
        )

    def send(self, kk):
        for d in range(1, self.place.n_s):
            self.z_copy(d, kk).start()

    def block(self, kk, quarter):
        return self.res.at[:, pl.ds(pl.multiple_of((kk * self.place.n_c + quarter) * TILE, TILE), TILE)]

    def f_move(self, kk, d, incoming):
        here = self.block(kk, self.place.source_x(d) * 2 + self.place.core if incoming else self.place.c)
        return remote(here, here, self.fs.at[kk, d - 1], self.fr.at[kk, d - 1], self.place.along_x(d))

    def h_move(self, kk, d, incoming):
        core = 1 - self.place.core if incoming else self.place.core
        here = self.block(kk, self.place.source_x(d) * 2 + core)
        return remote(here, here, self.hs.at[kk, d], self.hr.at[kk, d], self.place.sibling)

    def stage_d(self, kk):
        total = self.total[kk, self.shard_rows(self.place.s), :].astype(jnp.float32)
        for d in range(1, self.place.n_s):
            self.z_copy(d, kk).wait_recv()
            total = total + self.z_in[kk, d - 1].astype(jnp.float32)
        lanes = pl.ds(pl.multiple_of((kk * self.place.n_c + self.place.c) * TILE, TILE), TILE)
        self.res[:, lanes] = total.astype(jnp.bfloat16)
        for d in range(1, self.place.n_x):
            self.f_move(kk, d, False).start()
        self.h_move(kk, 0, False).start()

    def stage_e(self, kk):
        for d in range(1, self.place.n_x):
            self.f_move(kk, d, True).wait_recv()
            self.h_move(kk, d, False).start()

    def stage_f(self, kk):
        for d in range(self.place.n_x):
            self.h_move(kk, d, True).wait_recv()

    def step(self, i):
        for lag, stage in ((0, self.stage_d), (1, self.stage_e), (2, self.stage_f)):
            kk = i - lag
            pl.when((kk >= 0) & (kk < self.chunks))(partial(stage, kk))

    def finish(self):
        def one(kk, carry):
            for d in range(1, self.place.n_x):
                self.f_move(kk, d, False).wait_send()
            for d in range(self.place.n_x):
                self.h_move(kk, d, False).wait_send()
            for d in range(1, self.place.n_s):
                self.z_copy(d, kk).wait_send()
            return carry

        lax.fori_loop(0, self.chunks, one, 0)


def produce_group(cross, order, kk, left_of, slab_of):
    slot, at, n_c = cross.reserve(kk), 0, cross.place.n_c
    while at < n_c:
        name, index = order[kk * n_c + at]
        count = 1
        while at + count < n_c and order[kk * n_c + at + count][0] == name:
            count += 1
        right = jnp.concatenate([slab_of(name, index + i) for i in range(count)], axis=1)
        product = dot_tn(left_of(name)[...], right).astype(jnp.bfloat16)
        for i in range(count):
            cross.gbuf[slot, at + i] = product[:, i * TILE : (i + 1) * TILE]
        at += count
    cross.send(kk)


def dot_nn(left, right):
    return lax.dot_general(left, right, (((1,), (0,)), ((), ())), preferred_element_type=jnp.float32)


def dot_nt(left, right):
    return lax.dot_general(left, right, (((1,), (1,)), ((), ())), preferred_element_type=jnp.float32)


def dot_tn(left, right):
    return lax.dot_general(left, right, (((0,), (0,)), ((), ())), preferred_element_type=jnp.float32)


def joined(ref, low, high):
    return jnp.concatenate([ref[index] for index in range(low, high)], axis=1)


def norm_parts(values):
    centre = values - jnp.mean(values, axis=-1, keepdims=True)
    spread = jnp.mean(centre * centre, axis=-1, keepdims=True)
    rate = lax.rsqrt(spread + EPSILON)
    return centre * rate, rate


def norm_rows(values, gain, shift):
    return (norm_parts(values)[0] * gain + shift).astype(jnp.bfloat16)


def half_masks(shape):
    lane = lax.broadcasted_iota(jnp.int32, shape, len(shape) - 1)
    return lane < HEAD_DIM


def keep_half(values, low, half):
    zero = jnp.zeros_like(values)
    return jnp.where(low, values, zero) if half == 0 else jnp.where(low, zero, values)


def fold(values, combine):
    result = values[:, :TILE]
    for at in range(TILE, values.shape[1], TILE):
        result = combine(result, values[:, at : at + TILE])
    return result


def attend(c, q, k, v, att, lse, scores, after):
    slabs, length, unused = q.shape
    scale = HEAD_DIM ** (-0.5) * LOG2E
    low = half_masks((length, TILE))
    lane = lax.broadcasted_iota(jnp.int32, (length, TILE), 1)
    steps = [(low_row, low_row + BLOCK) for low_row in range(0, length, BLOCK)]

    def one(p, carry):
        outs = []
        logs = lse[...]
        for half in (0, 1):
            part = keep_half(q[p], low, half)

            def first(j, peak):
                s = dot_nt(part, k[p, rows_at(j, length), :]) * scale
                scores[j] = s
                return jnp.maximum(peak, fold(s, jnp.maximum))

            peak = lax.fori_loop(0, c, first, jnp.full((length, TILE), NEGATIVE, jnp.float32))
            own_keys, own_values = k[p, rows_at(c, length), :], v[p, rows_at(c, length), :]
            tops = []
            for begin, end in steps:
                s = dot_nt(part[begin:end], own_keys[:end]) * scale
                scores[c, begin:end, :end] = s
                best = jnp.maximum(peak[begin:end], fold(s, jnp.maximum))
                tops.append(jnp.max(best, axis=1, keepdims=True))
            top = jnp.concatenate(tops, axis=0)

            def second(j, state):
                raised = jnp.exp2(scores[j] - top)
                mixed = dot_nn(raised.astype(jnp.bfloat16), v[p, rows_at(j, length), :])
                return state[0] + fold(raised, jnp.add), state[1] + mixed

            zero = jnp.zeros((length, TILE), jnp.float32)
            total, mixed = lax.fori_loop(0, c, second, (zero, zero))
            totals, mixes = [], []
            for (begin, end), best in zip(steps, tops):
                raised = jnp.exp2(scores[c, begin:end, :end] - best)
                totals.append(total[begin:end] + fold(raised, jnp.add))
                mixes.append(mixed[begin:end] + dot_nn(raised.astype(jnp.bfloat16), own_values[:end]))
            total = jnp.sum(jnp.concatenate(totals, axis=0), axis=1, keepdims=True)
            outs.append(jnp.concatenate(mixes, axis=0) / total)
            logs = jnp.where(lane == p * 2 + half, top + jnp.log2(total), logs)
            after(p * 2 + half)
        lse[...] = logs
        att[p] = jnp.where(low, outs[0], outs[1]).astype(jnp.bfloat16)
        return carry

    lse[...] = jnp.zeros_like(lse)
    lax.fori_loop(0, slabs, one, 0)


def front_kernel(
    n_s, n_c, chunks, shard, tok, gains, shifts, bias, w, q, k, v, att, lse,
    others, normed, scores, zs, zr, xs, xr, cs, cr, own_sem, txs, txr, tys, tyr, tcs, tcr,
):
    place = Place(n_s, n_c)
    c, x, core, n_x = place.c, place.x, place.core, place.n_x
    length, width = tok.shape
    slabs = q.shape[0]
    place.greet()
    gather = Gather(place, shard, w, chunks, 0, (zs, zr, xs, xr, cs, cr, own_sem))

    half = length // 2

    def token_half(index, which):
        return others.at[pl.ds(pl.multiple_of(index * length + which * half, half), half), :]

    def run(pair, method):
        copy, valid = pair
        pl.when(valid)(getattr(copy, method))

    def token_x(d):
        own_half = tok.at[pl.ds(pl.multiple_of(place.t * half, half), half), :]
        copy = remote(own_half, token_half(c, place.t), txs.at[d - 1], txr.at[d - 1], place.along_x(d))
        return copy, lax.rem(x + d, n_x) > x

    def token_in(d):
        here = token_half(place.source_x(d) * 2 + core, place.t)
        return remote(here, here, txs.at[d - 1], txr.at[d - 1], place.sibling), place.source_x(d) < x

    def token_peer(d, incoming):
        here = token_half(place.source_x(d) * 2 + core, 1 - place.t if incoming else place.t)
        return remote(here, here, tys.at[d - 1], tyr.at[d - 1], place.peer), place.source_x(d) < x

    def token_relay(d, which, incoming):
        here = token_half(place.source_x(d) * 2 + (1 - core if incoming else core), which)
        return remote(here, here, tcs.at[d, which], tcr.at[d, which], place.sibling), place.source_x(d) < x

    def token_own(which):
        own_half = tok.at[pl.ds(which * half, half), :]
        return remote(own_half, token_half(c, which), tcs.at[0, which], tcr.at[0, which], place.sibling), core == 0

    def token_own_in(which):
        here = token_half(place.sibling_index, which)
        return remote(here, here, tcs.at[0, which], tcr.at[0, which], place.sibling), core == 1

    for d in range(1, n_x):
        run(token_x(d), "start")
    for which in (0, 1):
        run(token_own(which), "start")
    gather.start()

    def norm_block(source, base, j):
        def tile(i, carry):
            rows = source[pl.ds(pl.multiple_of(base + i * TILE, TILE), TILE), :].astype(jnp.float32)
            normed[j, rows_at(i, TILE), :] = norm_rows(rows, gains[0:1, :], shifts[0:1, :])
            return carry

        lax.fori_loop(0, length // TILE, tile, 0)

    norm_block(tok, 0, c)
    needed = -(-3 * slabs // n_c)
    ready = min(needed + 1, gather.last)
    gather.advance_range(0, 1)
    for d in range(1, n_x):
        run(token_in(d), "wait_recv")
        run(token_peer(d, False), "start")
        for which in (0, 1):
            pl.when(place.t == which)(lambda: run(token_relay(d, which, False), "start"))
    gather.advance_range(1, 2)
    for d in range(1, n_x):
        run(token_peer(d, True), "wait_recv")
        for which in (0, 1):
            pl.when(place.t != which)(lambda: run(token_relay(d, which, False), "start"))
    gather.advance_range(2, ready)
    for which in (0, 1):
        for d in range(1, n_x):
            run(token_relay(d, which, True), "wait_recv")
        run(token_own_in(which), "wait_recv")

    def norm_other(j, carry):
        norm_block(others, j * length, j)
        return carry

    lax.fori_loop(0, c, norm_other, 0)
    gather.own_copy.wait()
    gather.complete_range(0, needed)

    def project(j, which, row_bias):
        result = dot_nn(normed[j], joined(w, which * slabs, (which + 1) * slabs))
        if row_bias is not None:
            result = result + row_bias
        return result.astype(jnp.bfloat16)

    def project_keys(j, carry):
        spot = rows_at(j, length)
        for which, target, row_bias in ((1, k, None), (2, v, bias[1:2, :])):
            result = project(j, which, row_bias)
            for p in range(slabs):
                target[p, spot, :] = result[:, p * TILE : (p + 1) * TILE]
        return carry

    lax.fori_loop(0, c + 1, project_keys, 0)
    queries = project(c, 0, bias[0:1, :])
    for p in range(slabs):
        q[p] = queries[:, p * TILE : (p + 1) * TILE]
    pieces = 2 * slabs

    def after(step):
        pl.when(ready + step < gather.last)(lambda: gather.advance(ready + step))

    attend(c, q, k, v, att, lse, scores, after)
    gather.advance_range(min(ready + pieces, gather.last), gather.last)
    gather.complete_range(needed, chunks)
    gather.finish()
    for d in range(1, n_x):
        run(token_x(d), "wait_send")
        run(token_peer(d, False), "wait_send")
        for which in (0, 1):
            run(token_relay(d, which, False), "wait_send")
    for which in (0, 1):
        run(token_own(which), "wait_send")


def front(shard, tok, gains, shifts, bias, n_s, n_c, cut):
    total, rows, unused = shard.shape
    length, width = tok.shape
    slabs = bias.shape[1] // TILE
    chunks, n_x = cut // n_c, n_c // 2
    dma, shape, scratch = pltpu.SemaphoreType.DMA, jax.ShapeDtypeStruct, pltpu.VMEM
    vmem = pl.BlockSpec(memory_space=pltpu.VMEM)
    bf16, f32 = jnp.bfloat16, jnp.float32
    return pl.pallas_call(
        partial(front_kernel, n_s, n_c, chunks),
        out_shape=(
            shape((cut, rows * n_s, TILE), bf16),
            shape((slabs, length, TILE), bf16),
            shape((slabs, length * n_c, TILE), bf16),
            shape((slabs, length * n_c, TILE), bf16),
            shape((slabs, length, TILE), bf16),
            shape((length, TILE), f32),
        ),
        in_specs=[vmem] * 5,
        out_specs=(vmem,) * 6,
        scratch_shapes=[
            scratch((length * n_c, width), bf16), scratch((n_c, length, width), bf16),
            scratch((n_c, length, length), f32),
            *gather_semaphores(chunks, n_s, n_c),
            dma((n_x - 1,)), dma((n_x - 1,)), dma((n_x - 1,)), dma((n_x - 1,)), dma((n_x, 2)), dma((n_x, 2)),
        ],
        compiler_params=pltpu.CompilerParams(collective_id=0, has_side_effects=True, vmem_limit_bytes=60 << 20),
        name="front",
    )(shard, tok, gains, shifts, bias)


WIDE = 2


def chain_kernel(
    at, chunk, banks, n_s, n_c, ids, att, tok, cot, bank, shard, gains, shifts, bias, out_bias, up_bias, w_front,
    n2, sl, fl, mx, gcq, ga, dks, dvs, gfirst, part, second, sums, up_sums, head_sums, total_out,
    mem_k, mem_v, first, gsecond, weights, gmix, cq, tx, rx, ss, rs, w, wsem, n3, act, gh, *engines
):
    place = Place(n_s, n_c)
    peer = place.peer
    cut = w_front.shape[0]
    place.greet()
    gather = Gather(place, shard, w, (shard.shape[0] - cut) // n_c, cut, engines[:7])
    cross = Cross(place, total_out, engines[7:])
    edges = [at["self_out"], at["memory"], cut]

    def load(i):
        low, high = edges[i], edges[i + 1]
        return pltpu.make_async_copy(w_front.at[pl.ds(low, high - low)], w.at[pl.ds(low, high - low)], wsem.at[i])

    load(0).start()
    load(1).start()
    gather.start()
    f32, bf16 = jnp.float32, jnp.bfloat16
    length, width = tok.shape
    slabs = att.shape[0]
    units = act.shape[0]
    span = bank.shape[0] // banks
    stretches, picks = ids.shape
    stretch = length // stretches
    keys_each = picks * span
    scale = HEAD_DIM ** (-0.5)
    count = length // chunk
    tiles = chunk // TILE
    low = half_masks((stretch, TILE))
    sums[...] = jnp.zeros_like(sums)
    up_sums[...] = jnp.zeros_like(up_sums)
    head_sums[...] = jnp.zeros_like(head_sums)

    def exchange(phase, r):
        rows = rows_at(r, chunk)
        return remote(tx.at[phase, rows, :], rx.at[phase, rows, :], ss.at[phase, r], rs.at[phase, r], peer)

    def every(stage):
        def run(r, carry):
            stage(r)
            return carry

        lax.fori_loop(0, count, run, 0)

    def per_tile(r, body):
        def run(i, carry):
            body(pl.ds(pl.multiple_of(r * chunk + i * TILE, TILE), TILE))
            return carry

        lax.fori_loop(0, tiles, run, 0)

    def out_product(target, r, left, name, total):
        rows = rows_at(r, chunk)
        low_slab = at[name]
        step = 256

        def run(n, carry):
            cols = pl.ds(pl.multiple_of(n * step, step), step)
            weight = jnp.concatenate([w[low_slab + i, cols, :] for i in range(total)], axis=1)
            product = dot_nt(jnp.concatenate([left[i, rows, :] for i in range(total)], axis=1), weight)
            target[rows, cols] = product.astype(bf16)
            return carry

        lax.fori_loop(0, width // step, run, 0)

    def send_attended(r):
        out_product(tx.at[0], r, att, "self_out", slabs)
        exchange(0, r).start()

    load(0).wait()
    every(send_attended)
    load(1).wait()
    total = gather.last
    gather.advance_range(0, min(1, total))

    def memory(i, carry):
        rows = rows_at(i, 4 * span)
        for which, target, row_bias in ((0, mem_k, None), (1, mem_v, bias[3:4, :])):
            base = at["memory"] + which * slabs
            product = dot_nn(bank[rows, :], joined(w, base, base + slabs))
            if row_bias is not None:
                product = product + row_bias
            product = product.astype(bf16)
            for p in range(slabs):
                for e in range(4):
                    target[p, i * 4 + e] = product[e * span : (e + 1) * span, p * TILE : (p + 1) * TILE]
        return carry

    lax.fori_loop(0, banks // 4, memory, 0)
    gather.advance_range(min(1, total), min(2, total))

    def narrow(source, r, base, row_bias, target):
        rows = rows_at(r, chunk)
        product = dot_nn(source[rows, :], joined(w, base, base + slabs))
        if row_bias is not None:
            product = product + row_bias
        product = product.astype(bf16)
        for p in range(slabs):
            target[p, rows, :] = product[:, p * TILE : (p + 1) * TILE]

    def picked(source, p, st):
        return jnp.concatenate(
            [source[p, ids[st, n]] for n in range(picks)], axis=0
        )

    def stacked(source, p, st):
        block = source[p, rows_at(st, stretch), :]
        return jnp.concatenate([keep_half(block, low, 0), keep_half(block, low, 1)], axis=0)

    def unstacked(both):
        return jnp.where(low, both[:stretch], both[stretch:])

    def total_of(phase, rows):
        return tx[phase, rows, :].astype(f32) + rx[phase, rows, :].astype(f32)

    def per_stretch(r, body):
        each = chunk // stretch

        def run(i, carry):
            writes = [body(p, r * each + i * WIDE + j) for j in range(WIDE) for p in range(slabs)]
            for write in writes:
                write()
            return carry

        lax.fori_loop(0, each // WIDE, run, 0)

    def cross_forward(r):
        exchange(0, r).wait_recv()

        def tile(rows):
            value = tok[rows, :].astype(f32) + total_of(0, rows) + out_bias[0:1, :]
            first[rows, :] = value
            n2[rows, :] = norm_rows(value, gains[1:2, :], shifts[1:2, :])

        per_tile(r, tile)
        narrow(n2, r, at["cross_q"], bias[2:3, :], cq)

        def one(p, st):
            keys, values = picked(mem_k, p, st), picked(mem_v, p, st)
            s = dot_nt(stacked(cq, p, st), keys) * (scale * LOG2E)
            raised = jnp.exp2(s - jnp.max(s, axis=1, keepdims=True))
            probs = raised / jnp.sum(raised, axis=1, keepdims=True)
            mixed = unstacked(dot_nn(probs.astype(bf16), values)).astype(bf16)

            def write():
                weights[p, st] = probs
                mx[p, rows_at(st, stretch), :] = mixed

            return write

        per_stretch(r, one)
        out_product(tx.at[1], r, mx, "cross_out", slabs)
        exchange(1, r).start()
        gather.advance_range(lax.min(2 + r, total), lax.min(3 + r, total))

    every(cross_forward)
    gather.advance_range(min(2 + count, total), total)
    gather.own_copy.wait()
    gather.complete_range(0, gather.chunks)
    curve = 0.7978845608028654
    cubic = 0.044715

    def feed(r):
        exchange(1, r).wait_recv()
        rows_all = rows_at(r, chunk)

        def tile(rows):
            value = first[rows, :] + total_of(1, rows) + out_bias[1:2, :]
            second[rows, :] = value
            n3[rows, :] = norm_rows(value, gains[2:3, :], shifts[2:3, :])

        per_tile(r, tile)

        def unit(j, carry):
            up = jnp.concatenate([w[at["up"] + 2 * j], w[at["up"] + 2 * j + 1]], axis=1)
            down = jnp.concatenate([w[at["down"] + 2 * j], w[at["down"] + 2 * j + 1]], axis=1)
            hidden = dot_nn(n3[rows_all, :], up) + up_bias[j]
            back = dot_nn(cot[rows_all, :], down)
            square = hidden * hidden
            bent = jnp.tanh(curve * hidden * (1.0 + cubic * square))
            half = 0.5 * (1.0 + bent)
            active = (hidden * half).astype(bf16)
            slope = half + 0.5 * hidden * (1.0 - bent * bent) * (curve * (1.0 + 3.0 * cubic * square))
            grad = (slope * back).astype(bf16)
            up_sums[j] = up_sums[j] + jnp.sum(grad.astype(f32), axis=0, keepdims=True)
            for i in range(2):
                lanes = slice(i * TILE, (i + 1) * TILE)
                act[2 * j + i, rows_all, :] = active[:, lanes]
                gh[2 * j + i, rows_all, :] = grad[:, lanes]
            return carry

        lax.fori_loop(0, units // 2, unit, 0)
        out_product(tx.at[2], r, gh, "up", units)
        exchange(2, r).start()

    every(feed)

    def result_product(r):
        out_product(part, r, act, "down", units)

    order = [(name, index) for name in ("up", "down") for index in range(units)]

    def left_of(name):
        return n3 if name == "up" else cot

    def slab_of(name, index):
        return (gh if name == "up" else act)[index]

    def produce(kk):
        produce_group(cross, order, kk, left_of, slab_of)

    steps = cross.chunks + 2

    def reduce_range(low, high):
        def one(i, carry):
            cross.step(i, produce, 0, cross.chunks)
            return carry

        lax.fori_loop(lax.min(low, steps), lax.min(high, steps), one, 0)

    def result_and_step(r):
        result_product(r)
        reduce_range(r, r + 1)

    every(result_and_step)

    def norm_back_rows(value, gain, upstream, row):
        spot, rate = norm_parts(value)
        scaled = upstream * gain
        sums[row : row + 1, :] = sums[row : row + 1, :] + jnp.sum(upstream * spot, axis=0, keepdims=True)
        sums[row + 3 : row + 4, :] = sums[row + 3 : row + 4, :] + jnp.sum(upstream, axis=0, keepdims=True)
        return rate * (
            scaled - jnp.mean(scaled, axis=-1, keepdims=True)
            - spot * jnp.mean(scaled * spot, axis=-1, keepdims=True)
        )

    def add_sum(row, values):
        sums[row : row + 1, :] = sums[row : row + 1, :] + jnp.sum(values, axis=0, keepdims=True)

    def cross_back(r):
        reduce_range(count + 2 * r, count + 2 * r + 1)
        exchange(2, r).wait_recv()

        def tile(rows):
            upstream = cot[rows, :].astype(f32)
            grad = upstream + norm_back_rows(second[rows, :], gains[2:3, :], total_of(2, rows), 2)
            add_sum(8, upstream)
            add_sum(7, grad)
            gsecond[rows, :] = grad
            sl[rows, :] = grad.astype(bf16)

        per_tile(r, tile)
        narrow(sl, r, at["cross_out"], None, gmix)

        def one(p, st):
            keys, values = picked(mem_k, p, st), picked(mem_v, p, st)
            grads, queries = stacked(gmix, p, st), stacked(cq, p, st)
            probs = weights[p, st]
            spread = dot_nt(grads, values)
            ds = (probs * (spread - jnp.sum(probs * spread, axis=1, keepdims=True))).astype(bf16)
            back = (unstacked(dot_nn(ds, keys)) * scale).astype(bf16)
            grad_keys = (dot_tn(ds, queries) * scale).astype(bf16)
            grad_values = dot_tn(probs.astype(bf16), grads).astype(bf16)

            def write():
                gcq[p, rows_at(st, stretch), :] = back
                dks[p, rows_at(st, keys_each), :] = grad_keys
                dvs[p, rows_at(st, keys_each), :] = grad_values

            return write

        per_stretch(r, one)
        out_product(tx.at[3], r, gcq, "cross_q", slabs)
        exchange(3, r).start()
        reduce_range(count + 2 * r + 1, count + 2 * r + 2)

    every(cross_back)

    def finish(r):
        exchange(3, r).wait_recv()

        def tile(rows):
            grad = gsecond[rows, :] + norm_back_rows(first[rows, :], gains[1:2, :], total_of(3, rows), 1)
            add_sum(6, grad)
            gfirst[rows, :] = grad
            fl[rows, :] = grad.astype(bf16)

        per_tile(r, tile)
        narrow(fl, r, at["self_out"], None, ga)
        reduce_range(3 * count + r, 3 * count + r + 1)

    every(finish)
    for p in range(slabs):
        head_sums[p] = jnp.sum(gcq[p].astype(f32), axis=0, keepdims=True)

    reduce_range(4 * count, steps)
    gather.finish()
    cross.finish()

    def settle(r):
        for phase in range(4):
            exchange(phase, r).wait_send()

    every(settle)


def chain(at, ids, att, tok, cot, bank, shard, gains, shifts, bias, out_bias, up_bias, w_front, banks, chunk, n_s, n_c):
    length, width = tok.shape
    slabs = att.shape[0]
    units = up_bias.shape[0] // TILE
    stretches, picks = ids.shape
    stretch, span = length // stretches, bank.shape[0] // banks
    keys_each = picks * span
    bf16, f32 = jnp.bfloat16, jnp.float32
    vmem, smem = pl.BlockSpec(memory_space=pltpu.VMEM), pl.BlockSpec(memory_space=pltpu.SMEM)
    shape = jax.ShapeDtypeStruct
    scratch = pltpu.VMEM
    row_slabs = shape((slabs, length, TILE), bf16)
    rows = shape((length, width), bf16)
    anywhere = pl.BlockSpec(memory_space=pl.ANY)
    chunks = 2 * units // n_c
    return pl.pallas_call(
        partial(chain_kernel, at, chunk, banks, n_s, n_c),
        out_shape=(
            rows, rows, rows,
            row_slabs, row_slabs, row_slabs,
            shape((slabs, stretches * keys_each, TILE), bf16), shape((slabs, stretches * keys_each, TILE), bf16),
            shape((length, width), f32), rows, shape((length, width), f32),
            shape((16, width), f32), shape((units // 2, 1, 2 * TILE), f32), shape((slabs, 1, TILE), f32),
            shape((chunks, width, TILE), bf16),
        ),
        in_specs=[smem] + [vmem] * 10 + [anywhere],
        out_specs=(vmem,) * 15,
        scratch_shapes=[
            scratch((slabs, banks, span, TILE), bf16), scratch((slabs, banks, span, TILE), bf16),
            scratch((length, width), f32), scratch((length, width), f32),
            scratch((slabs, stretches, 2 * stretch, keys_each), f32),
            scratch((slabs, length, TILE), bf16), scratch((slabs, length, TILE), bf16),
            scratch((4, length, width), bf16), scratch((4, length, width), bf16),
            pltpu.SemaphoreType.DMA((4, length // chunk)), pltpu.SemaphoreType.DMA((4, length // chunk)),
            scratch((shard.shape[0], width, TILE), bf16), pltpu.SemaphoreType.DMA((2,)),
            scratch((length, width), bf16),
            scratch((units, length, TILE), bf16), scratch((units, length, TILE), bf16),
            *gather_semaphores((shard.shape[0] - w_front.shape[0]) // n_c, n_s, n_c),
            *cross_scratch(chunks, width, n_s, n_c),
        ],
        compiler_params=pltpu.CompilerParams(collective_id=2, has_side_effects=True, vmem_limit_bytes=63 << 20),
        name="chain",
    )(ids, att, tok, cot, bank, shard, gains, shifts, bias, out_bias, up_bias.reshape(units // 2, 1, 2 * TILE), w_front)


def bank_kernel(span, at, ids, dks, dvs, w_all, mg, mine, send, head_sums, acc, w, ws):
    t = lax.axis_index("tp")
    f32, bf16 = jnp.float32, jnp.bfloat16
    slabs = dks.shape[0]
    stretches, picks = ids.shape
    acc[...] = jnp.zeros_like(acc)
    w_copy = pltpu.make_async_copy(w_all.at[pl.ds(at, 2 * slabs)], w, ws)
    w_copy.start()

    def add(i, carry):
        st, n = lax.div(i, picks), lax.rem(i, picks)
        rows = rows_at(ids[st, n], span)
        source = rows_at(i, span)
        for p in range(slabs):
            acc[p, rows, :] = acc[p, rows, :] + dks[p, source, :].astype(f32)
            acc[slabs + p, rows, :] = acc[slabs + p, rows, :] + dvs[p, source, :].astype(f32)
        return carry

    lax.fori_loop(0, stretches * picks, add, 0)
    half = mine.shape[1]
    w_copy.wait()
    total = jnp.zeros((1, slabs * TILE), f32)

    def one(i, sums):
        rows = rows_at(i, BLOCK)
        for p in range(2 * slabs):
            mg[p, rows, :] = acc[p, rows, :].astype(bf16)
        left = jnp.concatenate([mg[p, rows, :] for p in range(2 * slabs)], axis=1)
        for which, target in ((t, mine), (1 - t, send)):
            cols = pl.ds(pl.multiple_of(which * half, half), half)
            weight = jnp.concatenate([w[p, cols, :] for p in range(2 * slabs)], axis=1)
            target[rows, :] = dot_nt(left, weight).astype(target.dtype)
        return sums + jnp.sum(left[:, slabs * TILE :].astype(f32), axis=0, keepdims=True)

    total = lax.fori_loop(0, mine.shape[0] // BLOCK, one, total)
    for p in range(slabs):
        head_sums[p] = total[:, p * TILE : (p + 1) * TILE]


def bank_back(ids, dks, dvs, w, at, banks, span):
    slabs = dks.shape[0]
    rows, half = banks * span, w.shape[1] // 2
    bf16, f32 = jnp.bfloat16, jnp.float32
    vmem, smem = pl.BlockSpec(memory_space=pltpu.VMEM), pl.BlockSpec(memory_space=pltpu.SMEM)
    shape = jax.ShapeDtypeStruct
    return pl.pallas_call(
        partial(bank_kernel, span, at),
        out_shape=(
            shape((2 * slabs, rows, TILE), bf16), shape((rows, half), bf16),
            shape((rows, half), bf16), shape((slabs, 1, TILE), f32),
        ),
        in_specs=[smem, vmem, vmem, pl.BlockSpec(memory_space=pl.ANY)],
        out_specs=(vmem,) * 4,
        scratch_shapes=[
            pltpu.VMEM((2 * slabs, rows, TILE), f32), pltpu.VMEM((2 * slabs, w.shape[1], TILE), bf16),
            pltpu.SemaphoreType.DMA,
        ],
        compiler_params=pltpu.CompilerParams(vmem_limit_bytes=62 << 20),
        name="bank_back",
    )(ids, dks, dvs, w)


def tail_kernel(
    n_s, n_c, groups, early,
    q, k_far, v_far, up, att, lse, tok, norms, w_all, down_part, small_in, out_bias, gfirst, second, bank, bank_send, fl, n2, sl, mg, gcq, mx, hidden,
    gtok, result, res, res_hidden, small_out, bank_in,
    dk, dv, qm, um, lse_t, delta_t, dq_acc, dq, gk, gv, n1, core_in, x_in, tx, rx, rx_part, stage32, w,
    k, v, bank_here, totals, sm_mine, sm_core, sm_x, sm_z,
    cs, cr, xs, xr, ts, tr, ds_, ms, mr, ps, pr, es, ws, ns, nr, kvs, *engine
):
    f32, bf16 = jnp.float32, jnp.bfloat16
    place = Place(n_s, n_c)
    s, c, x, core, n_x = place.s, place.c, place.x, place.core, place.n_x
    sibling, peer = place.sibling, place.peer
    slabs, length, unused = q.shape
    width = tok.shape[1]
    per = length // BLOCK
    scale = HEAD_DIM ** (-0.5)
    place.greet()
    cross = Cross(place, totals, engine[:7])
    spread = Spread(place, totals, res, engine[7:14])
    extra = Spread(place, hidden, res_hidden, engine[14:])
    chunks = cross.chunks
    bank_copy = pltpu.make_async_copy(bank, bank_here, ds_)
    bank_copy.start()
    kv_copies = [pltpu.make_async_copy(far, here, kvs.at[i]) for i, (far, here) in enumerate(((k_far, k), (v_far, v)))]
    kv_copies[0].start()
    kv_copies[1].start()

    def send_hidden(kk, carry):
        extra.send(kk)
        return carry

    lax.fori_loop(0, extra.chunks, send_hidden, 0)
    part_copy = remote(down_part, rx_part, ps, pr, peer)
    neighbour_copy = remote(bank_send, bank_in, ns, nr, peer)
    neighbour_copy.start()
    w_copy = pltpu.make_async_copy(w_all.at[pl.ds(0, 3 * slabs)], w, ws)
    w_copy.start()

    def staged(source, r):
        return pltpu.make_async_copy(source.at[rows_at(r, BLOCK), :], stage32.at[r], es.at[r])

    for r in range(per):
        staged(gfirst, r).start()

    def owner_rows(index):
        return pl.ds(pl.multiple_of(index * length, length), length)

    def left_of(name):
        return {"self_in": n1, "memory": bank_here, "self_out": fl, "cross_q": n2, "cross_out": sl}[name]

    def slab_of(name, index):
        if name == "self_in":
            return (dq, gk, gv)[index // slabs][index % slabs]
        return {"memory": mg, "self_out": att, "cross_q": gcq, "cross_out": mx}[name][index]

    order = [(name, index) for name, count in groups for index in range(count)]

    def produce(kk):
        if any(order[kk * n_c + i] == ("memory", 0) for i in range(n_c)):
            bank_copy.wait()
        produce_group(cross, order, kk, left_of, slab_of)

    def loop(low, high, action):
        def run(i, carry):
            action(i)
            return carry

        lax.fori_loop(low, high, run, 0)

    def produce_some(i, low, high):
        for kk in range(low, high):
            pl.when(i == kk)(partial(produce, kk))

    def sum_and_send(kk):
        cross.stage_c(kk)
        spread.send(kk)


    low_all = half_masks((length, TILE))
    lse_t[...] = lse[...].T
    dq_acc[...] = jnp.zeros_like(dq_acc)

    def prepare(p, carry):
        for half in (0, 1):
            qm[p, half] = keep_half(q[p], low_all, half)
            um[p, half] = keep_half(up[p], low_all, half)
        prod = (up[p].astype(f32) * att[p].astype(f32)).T
        for half in (0, 1):
            delta_t[p, half] = jnp.sum(prod[half * HEAD_DIM : (half + 1) * HEAD_DIM, :], axis=0, keepdims=True)
        return carry

    loop(0, early, lambda i: produce_some(i, 0, early))
    kv_copies[0].wait()
    kv_copies[1].wait()
    lax.fori_loop(0, slabs, prepare, 0)

    def to_core(xo, part):
        theirs = owner_rows(xo * 2 + 1 - core)
        source = (dk if part == 0 else dv).at[:, theirs, :]
        return remote(source, core_in.at[xo, part], cs.at[xo, part], cr.at[xo, part], sibling)

    def to_owner(xo):
        d = x - xo
        return remote(core_in.at[xo], x_in.at[d - 1], xs.at[xo], xr.at[d - 1], {"ctx": xo * 2 + core})

    def from_higher(d):
        return remote(x_in.at[d - 1], x_in.at[d - 1], xs.at[0], xr.at[d - 1], sibling)

    def relay(xo):
        mine = owner_rows(xo * 2 + core)
        for part, source in ((0, dk), (1, dv)):
            to_core(xo, part).wait_recv()
            core_in[xo, part] = (source[:, mine, :].astype(f32) + core_in[xo, part].astype(f32)).astype(bf16)
        to_owner(xo).start()

    points = (x + 1) * slabs

    def key_block(p, spot, size, begin):
        keys, values = k[p, spot, :], v[p, spot, :]
        low_keys = half_masks((size, TILE))
        dk_sum = dv_sum = jnp.zeros((size, TILE), f32)
        back = jnp.zeros((length - begin, TILE), f32)
        for half in (0, 1):
            q_half, u_half = qm[p, half, begin:, :], um[p, half, begin:, :]
            score = dot_nt(keys, q_half) * (scale * LOG2E)
            probs = jnp.exp2(score - lse_t[pl.ds(p * 2 + half, 1), begin:])
            grad = dot_nt(values, u_half)
            slope = (probs * (grad - delta_t[p, half, :, begin:])).astype(bf16)
            dv_sum = dv_sum + dot_nn(probs.astype(bf16), u_half)
            dk_sum = dk_sum + dot_nn(slope, q_half)
            back = back + dot_tn(slope, keep_half(keys, low_keys, half))
        dq_acc[p, begin:, :] = dq_acc[p, begin:, :] + back
        dk[p, spot, :] = (dk_sum * scale).astype(bf16)
        dv[p, spot, :] = dv_sum.astype(bf16)

    def chip(xo, carry):
        def one(p, inner):
            def whole(j, deeper):
                key_block(p, rows_at(j, length), length, 0)
                return deeper

            lax.fori_loop(xo * 2, lax.min(xo * 2 + 2, c), whole, 0)

            @pl.when(xo == x)
            def _():
                for begin in range(0, length, BLOCK):
                    key_block(p, pl.ds(pl.multiple_of(c * length + begin, BLOCK), BLOCK), BLOCK, begin)

            @pl.when((p == 0) & (xo > 0))
            def _():
                relay(xo - 1)

            point = xo * slabs + p

            pl.when(point == 0)(lambda: loop(0, early, cross.stage_b))
            pl.when(point == points - 1)(lambda: loop(0, early, sum_and_send))
            return inner

        lax.fori_loop(0, slabs, one, 0)

        @pl.when(xo < x)
        def _():
            to_core(xo, 0).start()
            to_core(xo, 1).start()

        return carry

    lax.fori_loop(0, x + 1, chip, 0)

    @pl.when(core == 1)
    def _():
        to_core(x, 0).start()
        to_core(x, 1).start()

    for p in range(slabs):
        dq[p] = (dq_acc[p] * scale).astype(bf16)

    loop(0, extra.chunks, extra.stage_d)

    def norm_tile(i, carry):
        at = rows_at(i, TILE)
        n1[at, :] = norm_rows(tok[at, :].astype(f32), norms[0:1, :], norms[3:4, :])
        return carry

    lax.fori_loop(0, length // TILE, norm_tile, 0)
    loop(0, extra.chunks, extra.stage_e)
    own = owner_rows(c)

    @pl.when(core == 0)
    def _():
        to_core(x, 0).wait_recv()
        to_core(x, 1).wait_recv()

    for d in range(1, n_x):
        pl.when(x + d < n_x)(from_higher(d).wait_recv)
    for part, target in ((0, gk), (1, gv)):
        dq_acc[...] = (dk if part == 0 else dv)[:, own, :].astype(f32)

        @pl.when(core == 0)
        def _():
            dq_acc[...] = dq_acc[...] + core_in[x, part].astype(f32)

        for d in range(1, n_x):

            @pl.when(x + d < n_x)
            def _():
                dq_acc[...] = dq_acc[...] + x_in[d - 1, part].astype(f32)

        target[...] = dq_acc[...].astype(bf16)

    def exchange(r):
        at = rows_at(r, BLOCK)
        return remote(tx.at[at, :], rx.at[at, :], ts.at[r], tr.at[r], peer)

    w_copy.wait()

    def product(r, carry):
        at = rows_at(r, BLOCK)
        left = jnp.concatenate([ref[i, at, :] for ref in (dq, gk, gv) for i in range(slabs)], axis=1)

        def run(n, inner):
            cols = pl.ds(pl.multiple_of(n * 256, 256), 256)
            weight = jnp.concatenate([w[i, cols, :] for i in range(3 * slabs)], axis=1)
            tx[at, cols] = dot_nt(left, weight).astype(bf16)
            return inner

        lax.fori_loop(0, width // 256, run, 0)
        exchange(r).start()
        return carry

    lax.fori_loop(0, per, product, 0)

    part_copy.start()
    loop(early, chunks, lambda i: produce_some(i, early, chunks))
    loop(0, extra.chunks, extra.stage_f)
    loop(early, chunks, cross.stage_b)
    sm_mine[...] = small_in[...]
    for index, source in ((0, dq), (1, gv)):
        for p in range(slabs):
            lanes = slice((index * slabs + p) * TILE, (index * slabs + p + 1) * TILE)
            sm_mine[9:10, lanes] = jnp.sum(source[p].astype(f32), axis=0, keepdims=True)

    loop(early, chunks, sum_and_send)

    def last_rows(r, carry):
        exchange(r).wait_recv()
        staged(gfirst, r).wait()

        def tile(i, inner):
            at = pl.ds(pl.multiple_of(r * BLOCK + i * TILE, TILE), TILE)
            spot, rate = norm_parts(tok[at, :].astype(f32))
            upstream = tx[at, :].astype(f32) + rx[at, :].astype(f32)
            scaled = upstream * norms[0:1, :]
            sm_mine[0:1, :] = sm_mine[0:1, :] + jnp.sum(upstream * spot, axis=0, keepdims=True)
            sm_mine[3:4, :] = sm_mine[3:4, :] + jnp.sum(upstream, axis=0, keepdims=True)
            gtok[at, :] = stage32[r, rows_at(i, TILE), :] + rate * (
                scaled - jnp.mean(scaled, axis=-1, keepdims=True)
                - spot * jnp.mean(scaled * spot, axis=-1, keepdims=True)
            )
            return inner

        lax.fori_loop(0, BLOCK // TILE, tile, 0)
        staged(second, r).start()
        return carry

    lax.fori_loop(0, per, last_rows, 0)
    sm_send = remote(sm_mine, sm_core, ms.at[0], mr.at[0], sibling)

    def sm_x_copy(d):
        return remote(sm_x.at[x], sm_x.at[x], ms.at[d], mr.at[d], {"ctx": lax.rem(x + d, n_x) * 2 + core})

    def sm_x_in(d):
        here = sm_x.at[lax.rem(x - d + n_x, n_x)]
        return remote(here, here, ms.at[d], mr.at[d], sibling)

    def sm_z_copy(d):
        return remote(sm_z.at[s], sm_z.at[s], ms.at[n_x + d - 1], mr.at[n_x + d - 1], {"shard": lax.rem(s + d, n_s)})

    def sm_z_in(d):
        here = sm_z.at[lax.rem(s - d + n_s, n_s)]
        return remote(here, here, ms.at[n_x + d - 1], mr.at[n_x + d - 1], peer)

    sm_send.start()

    loop(0, early, spread.stage_d)
    sm_send.wait_recv()
    sm_x[x] = sm_mine[...] + sm_core[...]
    for d in range(1, n_x):
        sm_x_copy(d).start()
    loop(0, early, spread.stage_e)
    for d in range(1, n_x):
        sm_x_in(d).wait_recv()
    both = sm_x[0]
    for e in range(1, n_x):
        both = both + sm_x[e]
    sm_z[s] = both
    for d in range(1, n_s):
        sm_z_copy(d).start()
    loop(0, early, spread.stage_f)
    loop(early, chunks, spread.stage_d)
    loop(early, chunks, spread.stage_e)
    part_copy.wait_recv()

    def result_rows(r, carry):
        staged(second, r).wait()

        def tile(i, inner):
            at = pl.ds(pl.multiple_of(r * BLOCK + i * TILE, TILE), TILE)
            both = down_part[at, :].astype(f32) + rx_part[at, :].astype(f32)
            result[at, :] = (stage32[r, rows_at(i, TILE), :] + both + out_bias[2:3, :]).astype(bf16)
            return inner

        lax.fori_loop(0, BLOCK // TILE, tile, 0)
        return carry

    lax.fori_loop(0, per, result_rows, 0)

    for d in range(1, n_s):
        sm_z_in(d).wait_recv()
    both = sm_z[0]
    for e in range(1, n_s):
        both = both + sm_z[e]
    small_out[...] = both
    loop(early, chunks, spread.stage_f)
    part_copy.wait_send()
    neighbour_copy.wait()
    sm_send.wait_send()
    for d in range(1, n_x):
        sm_x_copy(d).wait_send()
    for d in range(1, n_s):
        sm_z_copy(d).wait_send()

    def settle(xo, carry):
        @pl.when(xo < x)
        def _():
            to_core(xo, 0).wait_send()
            to_core(xo, 1).wait_send()
            to_owner(xo).wait_send()

        @pl.when((xo == x) & (core == 1))
        def _():
            to_core(xo, 0).wait_send()
            to_core(xo, 1).wait_send()

        return carry

    lax.fori_loop(0, x + 1, settle, 0)

    def settle_tp(r, carry):
        exchange(r).wait_send()
        return carry

    lax.fori_loop(0, per, settle_tp, 0)

    cross.finish()
    spread.finish()
    extra.finish()


def tail(groups, n_s, n_c, hidden, q, k, v, up, att, lse, tok, norms, w, part, small, out_bias, gfirst, second, bank, bank_send, *grad_inputs):
    slabs, length, unused = q.shape
    width = tok.shape[1]
    n_x = n_c // 2
    bf16, f32 = jnp.bfloat16, jnp.float32
    vmem, anywhere = pl.BlockSpec(memory_space=pltpu.VMEM), pl.BlockSpec(memory_space=pl.ANY)
    shape, scratch, dma = jax.ShapeDtypeStruct, pltpu.VMEM, pltpu.SemaphoreType.DMA
    pair = (2, slabs, length, TILE)
    total = sum(count for name, count in groups)
    chunks, rows = total // n_c, width // n_s
    early = (total - groups[-1][1]) // n_c
    return pl.pallas_call(
        partial(tail_kernel, n_s, n_c, groups, early),
        out_shape=(
            shape((length, width), f32), shape((length, width), bf16),
            shape((rows, total * TILE), bf16), shape((rows, hidden.shape[0] * n_c * TILE), bf16),
            shape(small.shape, f32), shape(bank_send.shape, bf16),
        ),
        in_specs=[vmem, anywhere, anywhere] + [vmem] * 5
        + [anywhere]
        + [vmem] * 3 + [anywhere] * 4 + [vmem] * (len(grad_inputs) + 1),
        out_specs=(vmem,) * 5 + (anywhere,),
        scratch_shapes=[
            scratch(k.shape, bf16), scratch(k.shape, bf16),
            scratch((slabs, 2, length, TILE), bf16), scratch((slabs, 2, length, TILE), bf16),
            scratch((TILE, length), f32), scratch((slabs, 2, 1, length), f32), scratch(q.shape, f32),
            scratch(q.shape, bf16), scratch(q.shape, bf16), scratch(q.shape, bf16),
            scratch((length, width), bf16),
            scratch((n_x,) + pair, bf16), scratch((n_x - 1,) + pair, bf16),
            scratch((length, width), bf16), scratch((length, width), bf16),
            scratch((length, width), bf16), scratch((length // BLOCK, BLOCK, width), f32),
            scratch((3 * slabs, width, TILE), bf16),
            scratch(k.shape, bf16), scratch(k.shape, bf16),
            scratch(bank.shape, bf16), scratch((chunks, width, TILE), bf16),
            scratch(small.shape, f32), scratch(small.shape, f32),
            scratch((n_x,) + small.shape, f32), scratch((n_s,) + small.shape, f32),
            dma((n_x, 2)), dma((n_x, 2)), dma((n_x - 1,)), dma((n_x - 1,)),
            dma((length // BLOCK,)), dma((length // BLOCK,)), dma,
            dma((n_x + n_s - 1,)), dma((n_x + n_s - 1,)),
            dma, dma, dma((length // BLOCK,)), dma, dma, dma, dma((2,)),
            *cross_scratch(chunks, width, n_s, n_c),
            *spread_scratch(chunks, width, n_s, n_c),
            *spread_scratch(hidden.shape[0], width, n_s, n_c),
        ],
        compiler_params=pltpu.CompilerParams(collective_id=3, has_side_effects=True, vmem_limit_bytes=64 << 20),
        name="tail",
    )(q, k, v, up, att, lse, tok, norms, w, part, small, out_bias, gfirst, second, bank, bank_send, *grad_inputs, hidden)


def final_kernel(
    slabs, units, res, hidden, mine, received, small,
    neigh, gains, shifts, head, outs, up_bias, self_in, self_out, cross_q, memory, cross_out, up, down,
):
    f32 = jnp.float32
    neigh[...] = mine[...].astype(f32) + received[...].astype(f32)
    local = slabs * TILE
    at = 0
    for j in range(2):
        memory[:, j, :] = res[:, (at + j * slabs) * TILE : (at + (j + 1) * slabs) * TILE].astype(f32)
    at += 2 * slabs
    self_out[...] = res[:, at * TILE : (at + slabs) * TILE].astype(f32)
    at += slabs
    cross_q[...] = res[:, at * TILE : (at + slabs) * TILE].astype(f32)
    at += slabs
    cross_out[...] = res[:, at * TILE : (at + slabs) * TILE].astype(f32)
    at += slabs
    for j in range(3):
        self_in[j] = res[:, (at + j * slabs) * TILE : (at + (j + 1) * slabs) * TILE].astype(f32)
    up[...] = hidden[:, : units * TILE].astype(f32)
    down[...] = hidden[:, units * TILE :].astype(f32)
    gains[...] = small[0:3, :]
    shifts[...] = small[3:6, :]
    outs[...] = small[6:9, :]
    width = small.shape[1]
    for j in range(4):
        head[j : j + 1, :] = small[9 + j // 2 : 10 + j // 2, (j % 2) * local : (j % 2 + 1) * local]
    for j in range(units * TILE // width):
        up_bias[:, j * width : (j + 1) * width] = small[11 + j : 12 + j, :]


def final(slabs, units, res, hidden, mine, received, small):
    f32 = jnp.float32
    vmem, shape = pl.BlockSpec(memory_space=pltpu.VMEM), jax.ShapeDtypeStruct
    rows, local, width = res.shape[0], slabs * TILE, small.shape[1]
    return pl.pallas_call(
        partial(final_kernel, slabs, units),
        out_shape=(
            shape(mine.shape, f32), shape((3, width), f32), shape((3, width), f32), shape((4, local), f32),
            shape((3, width), f32), shape((1, units * TILE), f32),
            shape((3, rows, local), f32), shape((rows, local), f32), shape((rows, local), f32),
            shape((rows, 2, local), f32), shape((rows, local), f32),
            shape((rows, units * TILE), f32), shape((rows, units * TILE), f32),
        ),
        in_specs=[vmem] * 5,
        out_specs=(vmem,) * 13,
        compiler_params=pltpu.CompilerParams(vmem_limit_bytes=60 << 20),
        name="final",
    )(res, hidden, mine, received, small)


def slabbed(matrix):
    rows, columns = matrix.shape
    return matrix.reshape(rows, columns // TILE, TILE).transpose(1, 0, 2)


def shards(
    tokens,
    cotangent,
    neighbours,
    neighbour_ids,
    norm_gains,
    norm_shifts,
    head_bias,
    out_bias,
    up_bias,
    self_input,
    self_output,
    cross_query,
    cross_memory,
    cross_output,
    hidden_up,
    hidden_down,
):
    n_s, n_c = lax.axis_size("shard"), lax.axis_size("ctx")
    slice_rows = self_input.shape[0]
    shard = slabbed(
        jnp.concatenate(
            [
                self_input.reshape(slice_rows, -1),
                self_output.T,
                cross_memory.reshape(slice_rows, -1),
                cross_query,
                cross_output.T,
                hidden_up,
                hidden_down.T,
            ],
            axis=1,
        )
    )
    tok, cot = tokens[0], cotangent[0]
    length, width = tok.shape
    local = self_output.shape[0]
    slabs, units = local // TILE, hidden_up.shape[1] // TILE
    counts = (3 * slabs, slabs, 2 * slabs, slabs, slabs, units, units)
    names = ("self_in", "self_out", "memory", "cross_q", "cross_out", "up", "down")
    at, edge = {}, 0
    for name, count in zip(names, counts):
        at[name] = edge
        edge += count
    bank_shape = neighbours.shape[1:]
    bank = neighbours.reshape(bank_shape[0] * bank_shape[1], width)
    ids = neighbour_ids[0]
    cut = at["up"]
    weights, q, k, v, att, lse = front(shard, tok, norm_gains, norm_shifts, head_bias, n_s, n_c, cut)
    n2, sl, fl, mx, gcq, ga, dks, dvs, gfirst, part, second, sums, up_sums, head_cross, hidden = chain(
        at, ids, att, tok, cot, bank, shard, norm_gains, norm_shifts, head_bias, out_bias, up_bias, weights,
        bank_shape[0], BLOCK, n_s, n_c,
    )
    mg, mine, send, head_memory = bank_back(
        ids, dks, dvs, weights, at["memory"], bank_shape[0], bank_shape[1]
    )
    norms = jnp.concatenate([norm_gains, norm_shifts])
    small = jnp.concatenate(
        [
            sums[:9],
            jnp.zeros((1, width), jnp.float32),
            jnp.concatenate([head_cross, head_memory]).reshape(1, width),
            up_sums.reshape(-1, width),
        ]
    )
    small = jnp.pad(small, ((0, 16 - small.shape[0]), (0, 0)))
    lengths = dict(zip(names, counts))
    groups = [(name, lengths[name]) for name in ("memory", "self_out", "cross_q", "cross_out", "self_in")]
    grad_tokens, result, grads, hidden_grads, small, received = tail(
        groups, n_s, n_c, hidden, q, k, v, ga, att, lse, tok, norms, weights, part, small, out_bias, gfirst, second,
        bank, send, fl, n2, sl, mg, gcq, mx,
    )
    (
        neigh, gains, shifts, head, outs, bias_up, self_in, self_out, cross_q, memory, cross_out, up, down,
    ) = final(slabs, units, grads, hidden_grads, mine, received, small)
    return (
        result[None],
        grad_tokens[None],
        neigh.reshape((1,) + bank_shape[:2] + (width // 2,)),
        gains,
        shifts,
        head,
        outs,
        bias_up.reshape(-1),
        self_in.transpose(1, 0, 2),
        self_out.T,
        cross_q,
        memory,
        cross_out.T,
        up,
        down.T,
    )


def solution(mesh):
    placed = (
        P("shard", "ctx", None),
        P("shard", "ctx", None),
        P("shard", "ctx", None, None),
        P("shard", "ctx", None),
        P(),
        P(),
        P(None, "tp"),
        P(),
        P("tp"),
        P("shard", None, "tp"),
        P("tp", "shard"),
        P("shard", "tp"),
        P("shard", None, "tp"),
        P("tp", "shard"),
        P("shard", "tp"),
        P("tp", "shard"),
    )
    return jax.shard_map(
        shards,
        mesh=mesh,
        in_specs=placed,
        out_specs=(
            P("shard", "ctx", None),
            P("shard", "ctx", None),
            P("shard", "ctx", None, "tp"),
            P(),
            P(),
            P(None, "tp"),
            P(),
            P("tp"),
            P("shard", None, "tp"),
            P("tp", "shard"),
            P("shard", "tp"),
            P("shard", None, "tp"),
            P("tp", "shard"),
            P("shard", "tp"),
            P("tp", "shard"),
        ),
        check_vma=False,
    )
```

```python
from functools import partial

import jax
import jax.numpy as jnp
from jax import lax
from jax.experimental import pallas as pl
from jax.experimental.pallas import tpu as pltpu
from jax.sharding import PartitionSpec as P

HEAD_DIM = 64
BLOCK = 256


EPSILON = 1e-05
NEGATIVE = -1e30
HIGHEST = lax.Precision.HIGHEST


MESH = pl.DeviceIdType.MESH
LOG2E = 1.4426950408889634
TILE = 128


def aligned(index, size):
    return pl.multiple_of(index * size, size)


def rows_at(index, size):
    return pl.ds(pl.multiple_of(index * size, size), size)


def remote(src, dst, send, recv, where):
    return pltpu.make_async_remote_copy(
        src_ref=src, dst_ref=dst, send_sem=send, recv_sem=recv, device_id=where, device_id_type=MESH
    )


class Place:
    def __init__(self, n_s, n_c):
        self.n_s, self.n_c, self.n_x = n_s, n_c, n_c // 2
        self.s, self.c, self.t = lax.axis_index("shard"), lax.axis_index("ctx"), lax.axis_index("tp")
        self.x, self.core = lax.div(self.c, 2), lax.rem(self.c, 2)
        self.sibling_index = self.x * 2 + 1 - self.core
        self.sibling, self.peer = {"ctx": self.sibling_index}, {"tp": 1 - self.t}

    def along_x(self, d):
        return {"ctx": lax.rem(self.x + d, self.n_x) * 2 + self.core}

    def along_s(self, d):
        return {"shard": lax.rem(self.s + d, self.n_s)}

    def source_x(self, d):
        return lax.rem(self.x - d + self.n_x, self.n_x)

    def greet(self):
        barrier = pltpu.get_barrier_semaphore()
        partners = [self.along_x(d) for d in range(1, self.n_x)] + [self.along_s(d) for d in range(1, self.n_s)]
        partners += [self.sibling, self.peer]
        for where in partners:
            pl.semaphore_signal(barrier, inc=1, device_id=where, device_id_type=MESH)
        pl.semaphore_wait(barrier, len(partners))


def gather_semaphores(chunks, n_s, n_c):
    dma, n_x = pltpu.SemaphoreType.DMA, n_c // 2
    shapes = [(chunks, n_s - 1)] * 2 + [(chunks, n_s - 1, n_x - 1)] * 2 + [(chunks, n_s - 1, n_x)] * 2
    return [dma(shape) for shape in shapes] + [dma((1,))]


class Gather:
    def __init__(self, place, own, full, chunks, base, semaphores):
        self.place, self.own, self.full, self.chunks, self.base = place, own, full, chunks, base
        self.zs, self.zr, self.xs, self.xr, self.cs, self.cr, self.local = semaphores
        self.rows = own.shape[1]
        self.last = chunks + 1
        total = chunks * place.n_c
        self.own_copy = pltpu.make_async_copy(
            own.at[pl.ds(base, total)],
            full.at[pl.ds(base, total), pl.ds(aligned(place.s, self.rows), self.rows), :],
            self.local.at[0],
        )

    def block(self, origin, k, quarter):
        slab = self.base + k * self.place.n_c + quarter
        return self.full.at[slab, pl.ds(aligned(origin, self.rows), self.rows), :]

    def source(self, d):
        return lax.rem(self.place.s - d + self.place.n_s, self.place.n_s)

    def own_out(self, d, k):
        return remote(
            self.own.at[self.base + k * self.place.n_c + self.place.c], self.block(self.place.s, k, self.place.c),
            self.zs.at[k, d - 1], self.zr.at[k, d - 1], self.place.along_s(d),
        )

    def z_in(self, d, k):
        here = self.block(self.source(d), k, self.place.c)
        return remote(here, here, self.zs.at[k, d - 1], self.zr.at[k, d - 1], self.place.along_s(d))

    def x_move(self, d, k, e, incoming):
        quarter = self.place.source_x(e) * 2 + self.place.core if incoming else self.place.c
        here = self.block(self.source(d), k, quarter)
        return remote(here, here, self.xs.at[k, d - 1, e - 1], self.xr.at[k, d - 1, e - 1], self.place.along_x(e))

    def core_move(self, d, k, e, incoming):
        core = 1 - self.place.core if incoming else self.place.core
        here = self.block(self.source(d), k, self.place.source_x(e) * 2 + core)
        return remote(here, here, self.cs.at[k, d - 1, e], self.cr.at[k, d - 1, e], self.place.sibling)

    def each(self, low, high, body):
        def one(i, carry):
            body(i)
            return carry

        lax.fori_loop(low, high, one, 0)

    def start(self):
        self.own_copy.start()

        def send(k):
            for d in range(1, self.place.n_s):
                self.own_out(d, k).start()

        self.each(0, self.chunks, send)

    def advance(self, i):
        @pl.when(i < self.chunks)
        def _():
            for d in range(1, self.place.n_s):
                self.z_in(d, i).wait_recv()
                for e in range(1, self.place.n_x):
                    self.x_move(d, i, e, False).start()
                self.core_move(d, i, 0, False).start()

        @pl.when(i > 0)
        def _():
            for d in range(1, self.place.n_s):
                for e in range(1, self.place.n_x):
                    self.x_move(d, i - 1, e, True).wait_recv()
                    self.core_move(d, i - 1, e, False).start()

    def advance_range(self, low, high):
        self.each(low, high, self.advance)

    def complete_range(self, low, high):
        def one(k):
            for d in range(1, self.place.n_s):
                for e in range(self.place.n_x):
                    self.core_move(d, k, e, True).wait_recv()

        self.each(low, high, one)

    def finish(self):
        def one(k):
            for d in range(1, self.place.n_s):
                self.own_out(d, k).wait_send()
                for e in range(1, self.place.n_x):
                    self.x_move(d, k, e, False).wait_send()
                for e in range(self.place.n_x):
                    self.core_move(d, k, e, False).wait_send()

        self.each(0, self.chunks, one)


RING = 16


def cross_scratch(chunks, width, n_s, n_c):
    bf16, vmem, dma, n_x = jnp.bfloat16, pltpu.VMEM, pltpu.SemaphoreType.DMA, n_c // 2
    return [
        vmem((min(max(RING // n_c, 2), chunks), n_c, width, TILE), bf16),
        vmem((chunks, n_x, width, TILE), bf16),
        vmem((chunks, n_x - 1, width, TILE), bf16),
        dma((chunks, n_x)), dma((chunks, n_x)), dma((chunks, n_x - 1)), dma((chunks, n_x - 1)),
    ]


def spread_scratch(chunks, width, n_s, n_c):
    bf16, vmem, dma, n_x = jnp.bfloat16, pltpu.VMEM, pltpu.SemaphoreType.DMA, n_c // 2
    rows = width // n_s
    return [
        vmem((chunks, n_s - 1, rows, TILE), bf16),
        dma((chunks, n_s - 1)), dma((chunks, n_s - 1)),
        dma((chunks, n_x - 1)), dma((chunks, n_x - 1)), dma((chunks, n_x)), dma((chunks, n_x)),
    ]


class Cross:
    def __init__(self, place, total, refs):
        self.place, self.total = place, total
        self.gbuf, self.a_buf, self.b_buf, self.as_, self.ar, self.bs, self.br = refs
        self.chunks, self.ring = self.a_buf.shape[0], self.gbuf.shape[0]

    def a_out(self, kk, e):
        slot = lax.rem(kk, self.ring)
        source = self.gbuf.at[slot, e * 2 + 1 - self.place.core]
        return remote(source, self.a_buf.at[kk, e], self.as_.at[kk, e], self.ar.at[kk, e], self.place.sibling)

    def reserve(self, kk):
        if kk >= self.ring:
            for e in range(self.place.n_x):
                self.a_out(kk - self.ring, e).wait_send()
        return kk % self.ring

    def send(self, kk):
        for e in range(self.place.n_x):
            self.a_out(kk, e).start()

    def b_out(self, kk, d):
        to = lax.rem(self.place.x + d, self.place.n_x)
        return remote(
            self.a_buf.at[kk, to], self.b_buf.at[kk, d - 1], self.bs.at[kk, d - 1], self.br.at[kk, d - 1],
            self.place.along_x(d),
        )

    def stage_b(self, kk):
        x, core, slot = self.place.x, self.place.core, lax.rem(kk, self.ring)
        for d in range(1, self.place.n_x):
            e = lax.rem(x + d, self.place.n_x)
            self.a_out(kk, e).wait_recv()
            self.a_buf[kk, e] = self.gbuf[slot, e * 2 + core] + self.a_buf[kk, e]
            self.b_out(kk, d).start()
        self.a_out(kk, x).wait_recv()
        self.a_buf[kk, x] = self.gbuf[slot, self.place.c] + self.a_buf[kk, x]

    def stage_c(self, kk):
        total = self.a_buf[kk, self.place.x]
        for d in range(1, self.place.n_x):
            self.b_out(kk, d).wait_recv()
            total = total + self.b_buf[kk, d - 1]
        self.total[kk] = total

    def step(self, i, produce, low, high):
        for kk in range(low, high):
            pl.when(i == kk)(partial(produce, kk))
        for lag, stage in ((1, self.stage_b), (2, self.stage_c)):
            kk = i - lag
            pl.when((kk >= 0) & (kk < self.chunks))(partial(stage, kk))

    def finish(self):
        def one(kk, carry):
            @pl.when(kk >= max(self.chunks - self.ring, 0))
            def _():
                for e in range(self.place.n_x):
                    self.a_out(kk, e).wait_send()

            for d in range(1, self.place.n_x):
                self.b_out(kk, d).wait_send()
            return carry

        lax.fori_loop(0, self.chunks, one, 0)


class Spread:
    def __init__(self, place, total, res, refs):
        self.place, self.total, self.res = place, total, res
        self.z_in, self.zs, self.zr, self.fs, self.fr, self.hs, self.hr = refs
        self.chunks, self.rows = self.z_in.shape[0], self.z_in.shape[2]

    def shard_rows(self, index):
        return pl.ds(aligned(index, self.rows), self.rows)

    def z_copy(self, d, kk):
        theirs = self.shard_rows(lax.rem(self.place.s + d, self.place.n_s))
        return remote(
            self.total.at[kk, theirs, :], self.z_in.at[kk, d - 1], self.zs.at[kk, d - 1], self.zr.at[kk, d - 1],
            self.place.along_s(d),
        )

    def send(self, kk):
        for d in range(1, self.place.n_s):
            self.z_copy(d, kk).start()

    def block(self, kk, quarter):
        return self.res.at[:, pl.ds(pl.multiple_of((kk * self.place.n_c + quarter) * TILE, TILE), TILE)]

    def f_move(self, kk, d, incoming):
        here = self.block(kk, self.place.source_x(d) * 2 + self.place.core if incoming else self.place.c)
        return remote(here, here, self.fs.at[kk, d - 1], self.fr.at[kk, d - 1], self.place.along_x(d))

    def h_move(self, kk, d, incoming):
        core = 1 - self.place.core if incoming else self.place.core
        here = self.block(kk, self.place.source_x(d) * 2 + core)
        return remote(here, here, self.hs.at[kk, d], self.hr.at[kk, d], self.place.sibling)

    def stage_d(self, kk):
        total = self.total[kk, self.shard_rows(self.place.s), :].astype(jnp.float32)
        for d in range(1, self.place.n_s):
            self.z_copy(d, kk).wait_recv()
            total = total + self.z_in[kk, d - 1].astype(jnp.float32)
        lanes = pl.ds(pl.multiple_of((kk * self.place.n_c + self.place.c) * TILE, TILE), TILE)
        self.res[:, lanes] = total.astype(jnp.bfloat16)
        for d in range(1, self.place.n_x):
            self.f_move(kk, d, False).start()
        self.h_move(kk, 0, False).start()

    def stage_e(self, kk):
        for d in range(1, self.place.n_x):
            self.f_move(kk, d, True).wait_recv()
            self.h_move(kk, d, False).start()

    def stage_f(self, kk):
        for d in range(self.place.n_x):
            self.h_move(kk, d, True).wait_recv()

    def step(self, i):
        for lag, stage in ((0, self.stage_d), (1, self.stage_e), (2, self.stage_f)):
            kk = i - lag
            pl.when((kk >= 0) & (kk < self.chunks))(partial(stage, kk))

    def finish(self):
        def one(kk, carry):
            for d in range(1, self.place.n_x):
                self.f_move(kk, d, False).wait_send()
            for d in range(self.place.n_x):
                self.h_move(kk, d, False).wait_send()
            for d in range(1, self.place.n_s):
                self.z_copy(d, kk).wait_send()
            return carry

        lax.fori_loop(0, self.chunks, one, 0)


def produce_group(cross, order, kk, left_of, slab_of):
    slot, at, n_c = cross.reserve(kk), 0, cross.place.n_c
    while at < n_c:
        name, index = order[kk * n_c + at]
        count = 1
        while at + count < n_c and order[kk * n_c + at + count][0] == name:
            count += 1
        right = jnp.concatenate([slab_of(name, index + i) for i in range(count)], axis=1)
        product = dot_tn(left_of(name)[...], right).astype(jnp.bfloat16)
        for i in range(count):
            cross.gbuf[slot, at + i] = product[:, i * TILE : (i + 1) * TILE]
        at += count
    cross.send(kk)


def dot_nn(left, right):
    return lax.dot_general(left, right, (((1,), (0,)), ((), ())), preferred_element_type=jnp.float32)


def dot_nt(left, right):
    return lax.dot_general(left, right, (((1,), (1,)), ((), ())), preferred_element_type=jnp.float32)


def dot_tn(left, right):
    return lax.dot_general(left, right, (((0,), (0,)), ((), ())), preferred_element_type=jnp.float32)


def joined(ref, low, high):
    return jnp.concatenate([ref[index] for index in range(low, high)], axis=1)


def norm_parts(values):
    centre = values - jnp.mean(values, axis=-1, keepdims=True)
    spread = jnp.mean(centre * centre, axis=-1, keepdims=True)
    rate = lax.rsqrt(spread + EPSILON)
    return centre * rate, rate


def norm_rows(values, gain, shift):
    return (norm_parts(values)[0] * gain + shift).astype(jnp.bfloat16)


def half_masks(shape):
    lane = lax.broadcasted_iota(jnp.int32, shape, len(shape) - 1)
    return lane < HEAD_DIM


def keep_half(values, low, half):
    zero = jnp.zeros_like(values)
    return jnp.where(low, values, zero) if half == 0 else jnp.where(low, zero, values)


def fold(values, combine):
    result = values[:, :TILE]
    for at in range(TILE, values.shape[1], TILE):
        result = combine(result, values[:, at : at + TILE])
    return result


def attend(c, q, k, v, att, lse, scores, after):
    slabs, length, unused = q.shape
    scale = HEAD_DIM ** (-0.5) * LOG2E
    low = half_masks((length, TILE))
    lane = lax.broadcasted_iota(jnp.int32, (length, TILE), 1)
    steps = [(low_row, low_row + BLOCK) for low_row in range(0, length, BLOCK)]

    def one(p, carry):
        outs = []
        logs = lse[...]
        for half in (0, 1):
            part = keep_half(q[p], low, half)

            def first(j, peak):
                s = dot_nt(part, k[p, rows_at(j, length), :]) * scale
                scores[j] = s
                return jnp.maximum(peak, fold(s, jnp.maximum))

            peak = lax.fori_loop(0, c, first, jnp.full((length, TILE), NEGATIVE, jnp.float32))
            own_keys, own_values = k[p, rows_at(c, length), :], v[p, rows_at(c, length), :]
            tops = []
            for begin, end in steps:
                s = dot_nt(part[begin:end], own_keys[:end]) * scale
                scores[c, begin:end, :end] = s
                best = jnp.maximum(peak[begin:end], fold(s, jnp.maximum))
                tops.append(jnp.max(best, axis=1, keepdims=True))
            top = jnp.concatenate(tops, axis=0)

            def second(j, state):
                raised = jnp.exp2(scores[j] - top)
                mixed = dot_nn(raised.astype(jnp.bfloat16), v[p, rows_at(j, length), :])
                return state[0] + fold(raised, jnp.add), state[1] + mixed

            zero = jnp.zeros((length, TILE), jnp.float32)
            total, mixed = lax.fori_loop(0, c, second, (zero, zero))
            totals, mixes = [], []
            for (begin, end), best in zip(steps, tops):
                raised = jnp.exp2(scores[c, begin:end, :end] - best)
                totals.append(total[begin:end] + fold(raised, jnp.add))
                mixes.append(mixed[begin:end] + dot_nn(raised.astype(jnp.bfloat16), own_values[:end]))
            total = jnp.sum(jnp.concatenate(totals, axis=0), axis=1, keepdims=True)
            outs.append(jnp.concatenate(mixes, axis=0) / total)
            logs = jnp.where(lane == p * 2 + half, top + jnp.log2(total), logs)
            after(p * 2 + half)
        lse[...] = logs
        att[p] = jnp.where(low, outs[0], outs[1]).astype(jnp.bfloat16)
        return carry

    lse[...] = jnp.zeros_like(lse)
    lax.fori_loop(0, slabs, one, 0)


def front_kernel(
    n_s, n_c, chunks, shard, tok, gains, shifts, bias, w, q, k, v, att, lse,
    others, normed, scores, zs, zr, xs, xr, cs, cr, own_sem, txs, txr, tys, tyr, tcs, tcr,
):
    place = Place(n_s, n_c)
    c, x, core, n_x = place.c, place.x, place.core, place.n_x
    length, width = tok.shape
    slabs = q.shape[0]
    place.greet()
    gather = Gather(place, shard, w, chunks, 0, (zs, zr, xs, xr, cs, cr, own_sem))

    half = length // 2

    def token_half(index, which):
        return others.at[pl.ds(pl.multiple_of(index * length + which * half, half), half), :]

    def run(pair, method):
        copy, valid = pair
        pl.when(valid)(getattr(copy, method))

    def token_x(d):
        own_half = tok.at[pl.ds(pl.multiple_of(place.t * half, half), half), :]
        copy = remote(own_half, token_half(c, place.t), txs.at[d - 1], txr.at[d - 1], place.along_x(d))
        return copy, lax.rem(x + d, n_x) > x

    def token_in(d):
        here = token_half(place.source_x(d) * 2 + core, place.t)
        return remote(here, here, txs.at[d - 1], txr.at[d - 1], place.sibling), place.source_x(d) < x

    def token_peer(d, incoming):
        here = token_half(place.source_x(d) * 2 + core, 1 - place.t if incoming else place.t)
        return remote(here, here, tys.at[d - 1], tyr.at[d - 1], place.peer), place.source_x(d) < x

    def token_relay(d, which, incoming):
        here = token_half(place.source_x(d) * 2 + (1 - core if incoming else core), which)
        return remote(here, here, tcs.at[d, which], tcr.at[d, which], place.sibling), place.source_x(d) < x

    def token_own(which):
        own_half = tok.at[pl.ds(which * half, half), :]
        return remote(own_half, token_half(c, which), tcs.at[0, which], tcr.at[0, which], place.sibling), core == 0

    def token_own_in(which):
        here = token_half(place.sibling_index, which)
        return remote(here, here, tcs.at[0, which], tcr.at[0, which], place.sibling), core == 1

    for d in range(1, n_x):
        run(token_x(d), "start")
    for which in (0, 1):
        run(token_own(which), "start")
    gather.start()

    def norm_block(source, base, j):
        def tile(i, carry):
            rows = source[pl.ds(pl.multiple_of(base + i * TILE, TILE), TILE), :].astype(jnp.float32)
            normed[j, rows_at(i, TILE), :] = norm_rows(rows, gains[0:1, :], shifts[0:1, :])
            return carry

        lax.fori_loop(0, length // TILE, tile, 0)

    norm_block(tok, 0, c)
    needed = -(-3 * slabs // n_c)
    ready = min(needed + 1, gather.last)
    gather.advance_range(0, 1)
    for d in range(1, n_x):
        run(token_in(d), "wait_recv")
        run(token_peer(d, False), "start")
        for which in (0, 1):
            pl.when(place.t == which)(lambda: run(token_relay(d, which, False), "start"))
    gather.advance_range(1, 2)
    for d in range(1, n_x):
        run(token_peer(d, True), "wait_recv")
        for which in (0, 1):
            pl.when(place.t != which)(lambda: run(token_relay(d, which, False), "start"))
    gather.advance_range(2, ready)
    for which in (0, 1):
        for d in range(1, n_x):
            run(token_relay(d, which, True), "wait_recv")
        run(token_own_in(which), "wait_recv")

    def norm_other(j, carry):
        norm_block(others, j * length, j)
        return carry

    lax.fori_loop(0, c, norm_other, 0)
    gather.own_copy.wait()
    gather.complete_range(0, needed)

    def project(j, which, row_bias):
        result = dot_nn(normed[j], joined(w, which * slabs, (which + 1) * slabs))
        if row_bias is not None:
            result = result + row_bias
        return result.astype(jnp.bfloat16)

    def project_keys(j, carry):
        spot = rows_at(j, length)
        for which, target, row_bias in ((1, k, None), (2, v, bias[1:2, :])):
            result = project(j, which, row_bias)
            for p in range(slabs):
                target[p, spot, :] = result[:, p * TILE : (p + 1) * TILE]
        return carry

    lax.fori_loop(0, c + 1, project_keys, 0)
    queries = project(c, 0, bias[0:1, :])
    for p in range(slabs):
        q[p] = queries[:, p * TILE : (p + 1) * TILE]
    pieces = 2 * slabs

    def after(step):
        pl.when(ready + step < gather.last)(lambda: gather.advance(ready + step))

    attend(c, q, k, v, att, lse, scores, after)
    gather.advance_range(min(ready + pieces, gather.last), gather.last)
    gather.complete_range(needed, chunks)
    gather.finish()
    for d in range(1, n_x):
        run(token_x(d), "wait_send")
        run(token_peer(d, False), "wait_send")
        for which in (0, 1):
            run(token_relay(d, which, False), "wait_send")
    for which in (0, 1):
        run(token_own(which), "wait_send")


def front(shard, tok, gains, shifts, bias, n_s, n_c, cut):
    total, rows, unused = shard.shape
    length, width = tok.shape
    slabs = bias.shape[1] // TILE
    chunks, n_x = cut // n_c, n_c // 2
    dma, shape, scratch = pltpu.SemaphoreType.DMA, jax.ShapeDtypeStruct, pltpu.VMEM
    vmem = pl.BlockSpec(memory_space=pltpu.VMEM)
    bf16, f32 = jnp.bfloat16, jnp.float32
    return pl.pallas_call(
        partial(front_kernel, n_s, n_c, chunks),
        out_shape=(
            shape((cut, rows * n_s, TILE), bf16),
            shape((slabs, length, TILE), bf16),
            shape((slabs, length * n_c, TILE), bf16),
            shape((slabs, length * n_c, TILE), bf16),
            shape((slabs, length, TILE), bf16),
            shape((length, TILE), f32),
        ),
        in_specs=[vmem] * 5,
        out_specs=(vmem,) * 6,
        scratch_shapes=[
            scratch((length * n_c, width), bf16), scratch((n_c, length, width), bf16),
            scratch((n_c, length, length), f32),
            *gather_semaphores(chunks, n_s, n_c),
            dma((n_x - 1,)), dma((n_x - 1,)), dma((n_x - 1,)), dma((n_x - 1,)), dma((n_x, 2)), dma((n_x, 2)),
        ],
        compiler_params=pltpu.CompilerParams(collective_id=0, has_side_effects=True, vmem_limit_bytes=60 << 20),
        name="front",
    )(shard, tok, gains, shifts, bias)


WIDE = 4
ROWS = 256


def chain_kernel(
    at, chunk, banks, n_s, n_c, ids, att, tok, cot, bank_far, shard, gains, shifts, bias, out_bias, up_bias, w_front,
    n2, sl, fl, mx, gcq, ga, dks, dvs, gfirst, part, second, sums, up_sums, head_sums, total_out,
    mem_k, mem_v, first, gsecond, weights, gmix, cq, tx, rx, ss, rs, w, wsem, n3, act, gh, bank, bank_sem, *engines
):
    place = Place(n_s, n_c)
    peer = place.peer
    cut = w_front.shape[0]
    place.greet()
    gather = Gather(place, shard, w, (shard.shape[0] - cut) // n_c, cut, engines[:7])
    cross = Cross(place, total_out, engines[7:])
    edges = [at["self_out"], at["memory"], cut]

    def load(i):
        low, high = edges[i], edges[i + 1]
        return pltpu.make_async_copy(w_front.at[pl.ds(low, high - low)], w.at[pl.ds(low, high - low)], wsem.at[i])

    load(0).start()
    bank_copy = pltpu.make_async_copy(bank_far, bank, bank_sem)
    bank_copy.start()
    load(1).start()
    gather.start()
    f32, bf16 = jnp.float32, jnp.bfloat16
    length, width = tok.shape
    slabs = att.shape[0]
    units = act.shape[0]
    span = bank_far.shape[0] // banks
    picks, stretches = ids.shape
    stretch = length // stretches
    keys_each = picks * span
    scale = HEAD_DIM ** (-0.5)
    count = length // chunk
    tiles = chunk // ROWS
    low = half_masks((stretch, TILE))
    sums[...] = jnp.zeros_like(sums)
    up_sums[...] = jnp.zeros_like(up_sums)
    head_sums[...] = jnp.zeros_like(head_sums)

    def exchange(phase, r):
        rows = rows_at(r, chunk)
        return remote(tx.at[phase, rows, :], rx.at[phase, rows, :], ss.at[phase, r], rs.at[phase, r], peer)

    def every(stage):
        def run(r, carry):
            stage(r)
            return carry

        lax.fori_loop(0, count, run, 0)

    def per_tile(r, body):
        def run(i, carry):
            body(pl.ds(pl.multiple_of(r * chunk + i * ROWS, ROWS), ROWS))
            return carry

        lax.fori_loop(0, tiles, run, 0)

    def out_product(target, r, left, name, total):
        rows = rows_at(r, chunk)
        low_slab = at[name]
        step = 256

        def run(n, carry):
            cols = pl.ds(pl.multiple_of(n * step, step), step)
            weight = jnp.concatenate([w[low_slab + i, cols, :] for i in range(total)], axis=1)
            product = dot_nt(jnp.concatenate([left[i, rows, :] for i in range(total)], axis=1), weight)
            target[rows, cols] = product.astype(bf16)
            return carry

        lax.fori_loop(0, width // step, run, 0)

    def send_attended(r):
        out_product(tx.at[0], r, att, "self_out", slabs)
        exchange(0, r).start()

    load(0).wait()
    every(send_attended)
    load(1).wait()
    total = gather.last
    gather.advance_range(0, min(1, total))

    def memory(i, carry):
        rows = rows_at(i, 4 * span)
        for which, target, row_bias in ((0, mem_k, None), (1, mem_v, bias[3:4, :])):
            base = at["memory"] + which * slabs
            product = dot_nn(bank[rows, :], joined(w, base, base + slabs))
            if row_bias is not None:
                product = product + row_bias
            product = product.astype(bf16)
            for p in range(slabs):
                for e in range(4):
                    target[p, i * 4 + e] = product[e * span : (e + 1) * span, p * TILE : (p + 1) * TILE]
        return carry

    bank_copy.wait()
    lax.fori_loop(0, banks // 4, memory, 0)
    gather.advance_range(min(1, total), min(2, total))

    def narrow(source, r, base, row_bias, target):
        rows = rows_at(r, chunk)
        product = dot_nn(source[rows, :], joined(w, base, base + slabs))
        if row_bias is not None:
            product = product + row_bias
        product = product.astype(bf16)
        for p in range(slabs):
            target[p, rows, :] = product[:, p * TILE : (p + 1) * TILE]

    def picked(source, p, st):
        return jnp.concatenate(
            [source[p, ids[n, st]] for n in range(picks)], axis=0
        )

    def stacked(source, p, st):
        block = source[p, rows_at(st, stretch), :]
        return jnp.concatenate([keep_half(block, low, 0), keep_half(block, low, 1)], axis=0)

    def unstacked(both):
        return jnp.where(low, both[:stretch], both[stretch:])

    def total_of(phase, rows):
        return tx[phase, rows, :].astype(f32) + rx[phase, rows, :].astype(f32)

    def per_stretch(r, body):
        each = chunk // stretch

        def run(i, carry):
            writes = [body(p, r * each + i * WIDE + j) for j in range(WIDE) for p in range(slabs)]
            for write in writes:
                write()
            return carry

        lax.fori_loop(0, each // WIDE, run, 0)

    def cross_forward(r):
        exchange(0, r).wait_recv()

        def tile(rows):
            value = tok[rows, :].astype(f32) + total_of(0, rows) + out_bias[0:1, :]
            first[rows, :] = value
            n2[rows, :] = norm_rows(value, gains[1:2, :], shifts[1:2, :])

        per_tile(r, tile)
        narrow(n2, r, at["cross_q"], bias[2:3, :], cq)

        def one(p, st):
            keys, values = picked(mem_k, p, st), picked(mem_v, p, st)
            s = dot_nt(stacked(cq, p, st), keys) * (scale * LOG2E)
            raised = jnp.exp2(s - jnp.max(s, axis=1, keepdims=True))
            probs = raised / jnp.sum(raised, axis=1, keepdims=True)
            mixed = unstacked(dot_nn(probs.astype(bf16), values)).astype(bf16)

            def write():
                weights[p, st] = probs
                mx[p, rows_at(st, stretch), :] = mixed

            return write

        per_stretch(r, one)
        out_product(tx.at[1], r, mx, "cross_out", slabs)
        exchange(1, r).start()
        gather.advance_range(lax.min(2 + r, total), lax.min(3 + r, total))

    every(cross_forward)
    gather.advance_range(min(2 + count, total), total)
    gather.own_copy.wait()
    gather.complete_range(0, gather.chunks)
    curve = 0.7978845608028654
    cubic = 0.044715

    def feed(r):
        exchange(1, r).wait_recv()
        rows_all = rows_at(r, chunk)

        def tile(rows):
            value = first[rows, :] + total_of(1, rows) + out_bias[1:2, :]
            second[rows, :] = value
            n3[rows, :] = norm_rows(value, gains[2:3, :], shifts[2:3, :])

        per_tile(r, tile)

        def unit(j, carry):
            up = jnp.concatenate([w[at["up"] + 2 * j], w[at["up"] + 2 * j + 1]], axis=1)
            down = jnp.concatenate([w[at["down"] + 2 * j], w[at["down"] + 2 * j + 1]], axis=1)
            hidden = dot_nn(n3[rows_all, :], up) + up_bias[:, rows_at(j, 2 * TILE)]
            back = dot_nn(cot[rows_all, :], down)
            square = hidden * hidden
            bent = jnp.tanh(curve * hidden * (1.0 + cubic * square))
            half = 0.5 * (1.0 + bent)
            active = (hidden * half).astype(bf16)
            slope = half + 0.5 * hidden * (1.0 - bent * bent) * (curve * (1.0 + 3.0 * cubic * square))
            grad = (slope * back).astype(bf16)
            up_sums[j] = up_sums[j] + jnp.sum(grad.astype(f32), axis=0, keepdims=True)
            for i in range(2):
                lanes = slice(i * TILE, (i + 1) * TILE)
                act[2 * j + i, rows_all, :] = active[:, lanes]
                gh[2 * j + i, rows_all, :] = grad[:, lanes]
            return carry

        lax.fori_loop(0, units // 2, unit, 0)
        out_product(tx.at[2], r, gh, "up", units)
        exchange(2, r).start()

    every(feed)

    def result_product(r):
        out_product(part, r, act, "down", units)

    order = [(name, index) for name in ("up", "down") for index in range(units)]

    def left_of(name):
        return n3 if name == "up" else cot

    def slab_of(name, index):
        return (gh if name == "up" else act)[index]

    def produce(kk):
        produce_group(cross, order, kk, left_of, slab_of)

    steps = cross.chunks + 2

    def reduce_range(low, high):
        def one(i, carry):
            cross.step(i, produce, 0, cross.chunks)
            return carry

        lax.fori_loop(lax.min(low, steps), lax.min(high, steps), one, 0)

    def result_and_step(r):
        result_product(r)
        reduce_range(r, r + 1)

    every(result_and_step)

    def norm_back_rows(value, gain, upstream, row):
        spot, rate = norm_parts(value)
        scaled = upstream * gain
        sums[row : row + 1, :] = sums[row : row + 1, :] + jnp.sum(upstream * spot, axis=0, keepdims=True)
        sums[row + 3 : row + 4, :] = sums[row + 3 : row + 4, :] + jnp.sum(upstream, axis=0, keepdims=True)
        return rate * (
            scaled - jnp.mean(scaled, axis=-1, keepdims=True)
            - spot * jnp.mean(scaled * spot, axis=-1, keepdims=True)
        )

    def add_sum(row, values):
        sums[row : row + 1, :] = sums[row : row + 1, :] + jnp.sum(values, axis=0, keepdims=True)

    def cross_back(r):
        reduce_range(count + 2 * r, count + 2 * r + 1)
        exchange(2, r).wait_recv()

        def tile(rows):
            upstream = cot[rows, :].astype(f32)
            grad = upstream + norm_back_rows(second[rows, :], gains[2:3, :], total_of(2, rows), 2)
            add_sum(8, upstream)
            add_sum(7, grad)
            gsecond[rows, :] = grad
            sl[rows, :] = grad.astype(bf16)

        per_tile(r, tile)
        narrow(sl, r, at["cross_out"], None, gmix)

        def one(p, st):
            keys, values = picked(mem_k, p, st), picked(mem_v, p, st)
            grads, queries = stacked(gmix, p, st), stacked(cq, p, st)
            probs = weights[p, st]
            spread = dot_nt(grads, values)
            ds = (probs * (spread - jnp.sum(probs * spread, axis=1, keepdims=True))).astype(bf16)
            back = (unstacked(dot_nn(ds, keys)) * scale).astype(bf16)
            grad_keys = (dot_tn(ds, queries) * scale).astype(bf16)
            grad_values = dot_tn(probs.astype(bf16), grads).astype(bf16)

            def write():
                gcq[p, rows_at(st, stretch), :] = back
                dks[p, rows_at(st, keys_each), :] = grad_keys
                dvs[p, rows_at(st, keys_each), :] = grad_values

            return write

        per_stretch(r, one)
        out_product(tx.at[3], r, gcq, "cross_q", slabs)
        exchange(3, r).start()
        reduce_range(count + 2 * r + 1, count + 2 * r + 2)

    every(cross_back)

    def finish(r):
        exchange(3, r).wait_recv()

        def tile(rows):
            grad = gsecond[rows, :] + norm_back_rows(first[rows, :], gains[1:2, :], total_of(3, rows), 1)
            add_sum(6, grad)
            gfirst[rows, :] = grad
            fl[rows, :] = grad.astype(bf16)

        per_tile(r, tile)
        narrow(fl, r, at["self_out"], None, ga)
        reduce_range(3 * count + r, 3 * count + r + 1)

    every(finish)
    for p in range(slabs):
        head_sums[p] = jnp.sum(gcq[p].astype(f32), axis=0, keepdims=True)

    reduce_range(4 * count, steps)
    gather.finish()
    cross.finish()

    def settle(r):
        for phase in range(4):
            exchange(phase, r).wait_send()

    every(settle)


def chain(at, ids, att, tok, cot, bank, shard, gains, shifts, bias, out_bias, up_bias, w_front, banks, chunk, n_s, n_c):
    length, width = tok.shape
    slabs = att.shape[0]
    units = up_bias.shape[1] // TILE
    picks, stretches = ids.shape
    stretch, span = length // stretches, bank.shape[0] // banks
    keys_each = picks * span
    bf16, f32 = jnp.bfloat16, jnp.float32
    vmem, smem = pl.BlockSpec(memory_space=pltpu.VMEM), pl.BlockSpec(memory_space=pltpu.SMEM)
    shape = jax.ShapeDtypeStruct
    scratch = pltpu.VMEM
    row_slabs = shape((slabs, length, TILE), bf16)
    rows = shape((length, width), bf16)
    anywhere = pl.BlockSpec(memory_space=pl.ANY)
    chunks = 2 * units // n_c
    return pl.pallas_call(
        partial(chain_kernel, at, chunk, banks, n_s, n_c),
        out_shape=(
            rows, rows, rows,
            row_slabs, row_slabs, row_slabs,
            shape((slabs, stretches * keys_each, TILE), bf16), shape((slabs, stretches * keys_each, TILE), bf16),
            shape((length, width), f32), rows, shape((length, width), f32),
            shape((16, width), f32), shape((units // 2, 1, 2 * TILE), f32), shape((slabs, 1, TILE), f32),
            shape((chunks, width, TILE), bf16),
        ),
        in_specs=[smem] + [vmem] * 3 + [anywhere] * 2 + [vmem] * 5 + [anywhere],
        out_specs=(vmem,) * 15,
        scratch_shapes=[
            scratch((slabs, banks, span, TILE), bf16), scratch((slabs, banks, span, TILE), bf16),
            scratch((length, width), f32), scratch((length, width), f32),
            scratch((slabs, stretches, 2 * stretch, keys_each), f32),
            scratch((slabs, length, TILE), bf16), scratch((slabs, length, TILE), bf16),
            scratch((4, length, width), bf16), scratch((4, length, width), bf16),
            pltpu.SemaphoreType.DMA((4, length // chunk)), pltpu.SemaphoreType.DMA((4, length // chunk)),
            scratch((shard.shape[0], width, TILE), bf16), pltpu.SemaphoreType.DMA((2,)),
            scratch((length, width), bf16),
            scratch((units, length, TILE), bf16), scratch((units, length, TILE), bf16),
            scratch(bank.shape, bf16), pltpu.SemaphoreType.DMA,
            *gather_semaphores((shard.shape[0] - w_front.shape[0]) // n_c, n_s, n_c),
            *cross_scratch(chunks, width, n_s, n_c),
        ],
        compiler_params=pltpu.CompilerParams(collective_id=2, has_side_effects=True, vmem_limit_bytes=63 << 20),
        name="chain",
    )(ids, att, tok, cot, bank, shard, gains, shifts, bias, out_bias, up_bias, w_front)


def bank_kernel(span, at, ids, dks, dvs, w_all, mg, mine, send, head_sums, acc, w, ws):
    t = lax.axis_index("tp")
    f32, bf16 = jnp.float32, jnp.bfloat16
    slabs = dks.shape[0]
    picks, stretches = ids.shape
    acc[...] = jnp.zeros_like(acc)
    w_copy = pltpu.make_async_copy(w_all.at[pl.ds(at, 2 * slabs)], w, ws)
    w_copy.start()

    def add(i, carry):
        st, n = lax.div(i, picks), lax.rem(i, picks)
        rows = rows_at(ids[n, st], span)
        source = rows_at(i, span)
        for p in range(slabs):
            acc[p, rows, :] = acc[p, rows, :] + dks[p, source, :].astype(f32)
            acc[slabs + p, rows, :] = acc[slabs + p, rows, :] + dvs[p, source, :].astype(f32)
        return carry

    lax.fori_loop(0, stretches * picks, add, 0)
    half = mine.shape[1]
    w_copy.wait()
    total = jnp.zeros((1, slabs * TILE), f32)

    def one(i, sums):
        rows = rows_at(i, BLOCK)
        for p in range(2 * slabs):
            mg[p, rows, :] = acc[p, rows, :].astype(bf16)
        left = jnp.concatenate([mg[p, rows, :] for p in range(2 * slabs)], axis=1)
        for which, target in ((t, mine), (1 - t, send)):
            cols = pl.ds(pl.multiple_of(which * half, half), half)
            weight = jnp.concatenate([w[p, cols, :] for p in range(2 * slabs)], axis=1)
            target[rows, :] = dot_nt(left, weight).astype(target.dtype)
        return sums + jnp.sum(left[:, slabs * TILE :].astype(f32), axis=0, keepdims=True)

    total = lax.fori_loop(0, mine.shape[0] // BLOCK, one, total)
    for p in range(slabs):
        head_sums[p] = total[:, p * TILE : (p + 1) * TILE]


def bank_back(ids, dks, dvs, w, at, banks, span):
    slabs = dks.shape[0]
    rows, half = banks * span, w.shape[1] // 2
    bf16, f32 = jnp.bfloat16, jnp.float32
    vmem, smem = pl.BlockSpec(memory_space=pltpu.VMEM), pl.BlockSpec(memory_space=pltpu.SMEM)
    shape = jax.ShapeDtypeStruct
    return pl.pallas_call(
        partial(bank_kernel, span, at),
        out_shape=(
            shape((2 * slabs, rows, TILE), bf16), shape((rows, half), bf16),
            shape((rows, half), bf16), shape((slabs, 1, TILE), f32),
        ),
        in_specs=[smem, vmem, vmem, pl.BlockSpec(memory_space=pl.ANY)],
        out_specs=(vmem,) * 4,
        scratch_shapes=[
            pltpu.VMEM((2 * slabs, rows, TILE), f32), pltpu.VMEM((2 * slabs, w.shape[1], TILE), bf16),
            pltpu.SemaphoreType.DMA,
        ],
        compiler_params=pltpu.CompilerParams(vmem_limit_bytes=62 << 20),
        name="bank_back",
    )(ids, dks, dvs, w)


def tail_kernel(
    n_s, n_c, groups, early,
    q, k_far, v_far, up, att, lse, tok, gains, shifts, w_all, down_part, small_in, out_bias, gfirst, second, bank, bank_send, fl, n2, sl, mg, gcq, mx, hidden,
    gtok, result, res, res_hidden, small_out, bank_in,
    dk, dv, qm, um, lse_t, delta_t, dq_acc, dq, gk, gv, n1, core_in, x_in, tx, rx, rx_part, stage32, w,
    k, v, bank_here, totals, sm_mine, sm_core, sm_x, sm_z,
    cs, cr, xs, xr, ts, tr, ds_, ms, mr, ps, pr, es, ws, ns, nr, kvs, *engine
):
    f32, bf16 = jnp.float32, jnp.bfloat16
    place = Place(n_s, n_c)
    s, c, x, core, n_x = place.s, place.c, place.x, place.core, place.n_x
    sibling, peer = place.sibling, place.peer
    slabs, length, unused = q.shape
    width = tok.shape[1]
    per = length // BLOCK
    scale = HEAD_DIM ** (-0.5)
    place.greet()
    cross = Cross(place, totals, engine[:7])
    spread = Spread(place, totals, res, engine[7:14])
    extra = Spread(place, hidden, res_hidden, engine[14:])
    chunks = cross.chunks
    bank_copy = pltpu.make_async_copy(bank, bank_here, ds_)
    bank_copy.start()
    kv_copies = [pltpu.make_async_copy(far, here, kvs.at[i]) for i, (far, here) in enumerate(((k_far, k), (v_far, v)))]
    kv_copies[0].start()
    kv_copies[1].start()

    def send_hidden(kk, carry):
        extra.send(kk)
        return carry

    lax.fori_loop(0, extra.chunks, send_hidden, 0)
    part_copy = remote(down_part, rx_part, ps, pr, peer)
    neighbour_copy = remote(bank_send, bank_in, ns, nr, peer)
    neighbour_copy.start()
    w_copy = pltpu.make_async_copy(w_all.at[pl.ds(0, 3 * slabs)], w, ws)
    w_copy.start()

    def staged(source, r):
        return pltpu.make_async_copy(source.at[rows_at(r, BLOCK), :], stage32.at[r], es.at[r])

    for r in range(per):
        staged(gfirst, r).start()

    def owner_rows(index):
        return pl.ds(pl.multiple_of(index * length, length), length)

    def left_of(name):
        return {"self_in": n1, "memory": bank_here, "self_out": fl, "cross_q": n2, "cross_out": sl}[name]

    def slab_of(name, index):
        if name == "self_in":
            return (dq, gk, gv)[index // slabs][index % slabs]
        return {"memory": mg, "self_out": att, "cross_q": gcq, "cross_out": mx}[name][index]

    order = [(name, index) for name, count in groups for index in range(count)]

    def produce(kk):
        if any(order[kk * n_c + i] == ("memory", 0) for i in range(n_c)):
            bank_copy.wait()
        produce_group(cross, order, kk, left_of, slab_of)

    def loop(low, high, action):
        def run(i, carry):
            action(i)
            return carry

        lax.fori_loop(low, high, run, 0)

    def produce_some(i, low, high):
        for kk in range(low, high):
            pl.when(i == kk)(partial(produce, kk))

    def sum_and_send(kk):
        cross.stage_c(kk)
        spread.send(kk)


    low_all = half_masks((length, TILE))
    lse_t[...] = lse[...].T
    dq_acc[...] = jnp.zeros_like(dq_acc)

    def prepare(p, carry):
        for half in (0, 1):
            qm[p, half] = keep_half(q[p], low_all, half)
            um[p, half] = keep_half(up[p], low_all, half)
        prod = (up[p].astype(f32) * att[p].astype(f32)).T
        for half in (0, 1):
            delta_t[p, half] = jnp.sum(prod[half * HEAD_DIM : (half + 1) * HEAD_DIM, :], axis=0, keepdims=True)
        return carry

    loop(0, early, lambda i: produce_some(i, 0, early))
    kv_copies[0].wait()
    kv_copies[1].wait()
    lax.fori_loop(0, slabs, prepare, 0)

    def to_core(xo, part, p):
        theirs = owner_rows(xo * 2 + 1 - core)
        source = (dk if part == 0 else dv).at[p, theirs, :]
        return remote(source, core_in.at[xo, part, p], cs.at[xo, part, p], cr.at[xo, part, p], sibling)

    def to_owner(xo, part, p):
        d = x - xo
        return remote(
            core_in.at[xo, part, p], x_in.at[d - 1, part, p], xs.at[xo, part, p], xr.at[d - 1, part, p],
            {"ctx": xo * 2 + core},
        )

    def from_higher(d, part, p):
        here = x_in.at[d - 1, part, p]
        return remote(here, here, xs.at[0, part, p], xr.at[d - 1, part, p], sibling)

    def relay(xo, p):
        mine = owner_rows(xo * 2 + core)
        for part, source in ((0, dk), (1, dv)):
            to_core(xo, part, p).wait_recv()
            core_in[xo, part, p] = source[p, mine, :] + core_in[xo, part, p]
            to_owner(xo, part, p).start()

    points = (x + 1) * slabs

    def key_block(p, spot, size, begin):
        keys, values = k[p, spot, :], v[p, spot, :]
        low_keys = half_masks((size, TILE))
        dk_sum = dv_sum = jnp.zeros((size, TILE), f32)
        back = jnp.zeros((length - begin, TILE), f32)
        for half in (0, 1):
            q_half, u_half = qm[p, half, begin:, :], um[p, half, begin:, :]
            score = dot_nt(keys, q_half) * (scale * LOG2E)
            probs = jnp.exp2(score - lse_t[pl.ds(p * 2 + half, 1), begin:])
            grad = dot_nt(values, u_half)
            slope = (probs * (grad - delta_t[p, half, :, begin:])).astype(bf16)
            dv_sum = dv_sum + dot_nn(probs.astype(bf16), u_half)
            dk_sum = dk_sum + dot_nn(slope, q_half)
            back = back + dot_tn(slope, keep_half(keys, low_keys, half))
        dq_acc[p, begin:, :] = dq_acc[p, begin:, :] + back
        dk[p, spot, :] = (dk_sum * scale).astype(bf16)
        dv[p, spot, :] = dv_sum.astype(bf16)

    def chip(xo, carry):
        def one(p, inner):
            def whole(j, deeper):
                key_block(p, rows_at(j, length), length, 0)
                return deeper

            lax.fori_loop(xo * 2, lax.min(xo * 2 + 2, c), whole, 0)

            @pl.when(xo == x)
            def _():
                for begin in range(0, length, BLOCK):
                    key_block(p, pl.ds(pl.multiple_of(c * length + begin, BLOCK), BLOCK), BLOCK, begin)

            @pl.when((xo < x) | (core == 1))
            def _():
                to_core(xo, 0, p).start()
                to_core(xo, 1, p).start()

            pl.when((p > 0) & (xo < x))(lambda: relay(xo, p - 1))
            pl.when((p == 0) & (xo > 0))(lambda: relay(xo - 1, slabs - 1))
            point = xo * slabs + p

            pl.when(point == 0)(lambda: loop(0, early, cross.stage_b))
            pl.when(point == points - 1)(lambda: loop(0, early, sum_and_send))
            return inner

        lax.fori_loop(0, slabs, one, 0)

        return carry

    lax.fori_loop(0, x + 1, chip, 0)

    for p in range(slabs):
        dq[p] = (dq_acc[p] * scale).astype(bf16)

    loop(0, extra.chunks, extra.stage_d)

    def norm_tile(i, carry):
        at = rows_at(i, TILE)
        n1[at, :] = norm_rows(tok[at, :].astype(f32), gains[0:1, :], shifts[0:1, :])
        return carry

    lax.fori_loop(0, length // TILE, norm_tile, 0)
    loop(0, extra.chunks, extra.stage_e)
    own = owner_rows(c)

    @pl.when(core == 0)
    def _():
        for p in range(slabs):
            to_core(x, 0, p).wait_recv()
            to_core(x, 1, p).wait_recv()

    for d in range(1, n_x):

        @pl.when(x + d < n_x)
        def _():
            for p in range(slabs):
                from_higher(d, 0, p).wait_recv()
                from_higher(d, 1, p).wait_recv()

    for part, target in ((0, gk), (1, gv)):
        dq_acc[...] = (dk if part == 0 else dv)[:, own, :].astype(f32)

        @pl.when(core == 0)
        def _():
            dq_acc[...] = dq_acc[...] + core_in[x, part].astype(f32)

        for d in range(1, n_x):

            @pl.when(x + d < n_x)
            def _():
                dq_acc[...] = dq_acc[...] + x_in[d - 1, part].astype(f32)

        target[...] = dq_acc[...].astype(bf16)

    def exchange(r):
        at = rows_at(r, BLOCK)
        return remote(tx.at[at, :], rx.at[at, :], ts.at[r], tr.at[r], peer)

    w_copy.wait()

    def product(r, carry):
        at = rows_at(r, BLOCK)
        left = jnp.concatenate([ref[i, at, :] for ref in (dq, gk, gv) for i in range(slabs)], axis=1)

        def run(n, inner):
            cols = pl.ds(pl.multiple_of(n * 256, 256), 256)
            weight = jnp.concatenate([w[i, cols, :] for i in range(3 * slabs)], axis=1)
            tx[at, cols] = dot_nt(left, weight).astype(bf16)
            return inner

        lax.fori_loop(0, width // 256, run, 0)
        exchange(r).start()
        return carry

    lax.fori_loop(0, per, product, 0)

    part_copy.start()
    loop(early, chunks, lambda i: produce_some(i, early, chunks))
    loop(0, extra.chunks, extra.stage_f)
    loop(early, chunks, cross.stage_b)
    sm_mine[...] = small_in[...]
    for index, source in ((0, dq), (1, gv)):
        for p in range(slabs):
            lanes = slice((index * slabs + p) * TILE, (index * slabs + p + 1) * TILE)
            sm_mine[9:10, lanes] = jnp.sum(source[p].astype(f32), axis=0, keepdims=True)

    loop(early, chunks, sum_and_send)

    def last_rows(r, carry):
        exchange(r).wait_recv()
        staged(gfirst, r).wait()

        def tile(i, inner):
            at = pl.ds(pl.multiple_of(r * BLOCK + i * TILE, TILE), TILE)
            spot, rate = norm_parts(tok[at, :].astype(f32))
            upstream = tx[at, :].astype(f32) + rx[at, :].astype(f32)
            scaled = upstream * gains[0:1, :]
            sm_mine[0:1, :] = sm_mine[0:1, :] + jnp.sum(upstream * spot, axis=0, keepdims=True)
            sm_mine[3:4, :] = sm_mine[3:4, :] + jnp.sum(upstream, axis=0, keepdims=True)
            gtok[at, :] = stage32[r, rows_at(i, TILE), :] + rate * (
                scaled - jnp.mean(scaled, axis=-1, keepdims=True)
                - spot * jnp.mean(scaled * spot, axis=-1, keepdims=True)
            )
            return inner

        lax.fori_loop(0, BLOCK // TILE, tile, 0)
        staged(second, r).start()
        return carry

    lax.fori_loop(0, per, last_rows, 0)
    sm_send = remote(sm_mine, sm_core, ms.at[0], mr.at[0], sibling)

    def sm_x_copy(d):
        return remote(sm_x.at[x], sm_x.at[x], ms.at[d], mr.at[d], {"ctx": lax.rem(x + d, n_x) * 2 + core})

    def sm_x_in(d):
        here = sm_x.at[lax.rem(x - d + n_x, n_x)]
        return remote(here, here, ms.at[d], mr.at[d], sibling)

    def sm_z_copy(d):
        return remote(sm_z.at[s], sm_z.at[s], ms.at[n_x + d - 1], mr.at[n_x + d - 1], {"shard": lax.rem(s + d, n_s)})

    def sm_z_in(d):
        here = sm_z.at[lax.rem(s - d + n_s, n_s)]
        return remote(here, here, ms.at[n_x + d - 1], mr.at[n_x + d - 1], peer)

    sm_send.start()

    loop(0, early, spread.stage_d)
    sm_send.wait_recv()
    sm_x[x] = sm_mine[...] + sm_core[...]
    for d in range(1, n_x):
        sm_x_copy(d).start()
    loop(0, early, spread.stage_e)
    for d in range(1, n_x):
        sm_x_in(d).wait_recv()
    both = sm_x[0]
    for e in range(1, n_x):
        both = both + sm_x[e]
    sm_z[s] = both
    for d in range(1, n_s):
        sm_z_copy(d).start()
    loop(0, early, spread.stage_f)
    loop(early, chunks, spread.stage_d)
    loop(early, chunks, spread.stage_e)
    part_copy.wait_recv()

    def result_rows(r, carry):
        staged(second, r).wait()

        def tile(i, inner):
            at = pl.ds(pl.multiple_of(r * BLOCK + i * TILE, TILE), TILE)
            both = down_part[at, :].astype(f32) + rx_part[at, :].astype(f32)
            result[at, :] = (stage32[r, rows_at(i, TILE), :] + both + out_bias[2:3, :]).astype(bf16)
            return inner

        lax.fori_loop(0, BLOCK // TILE, tile, 0)
        return carry

    lax.fori_loop(0, per, result_rows, 0)

    for d in range(1, n_s):
        sm_z_in(d).wait_recv()
    both = sm_z[0]
    for e in range(1, n_s):
        both = both + sm_z[e]
    small_out[...] = both
    loop(early, chunks, spread.stage_f)
    part_copy.wait_send()
    neighbour_copy.wait()
    sm_send.wait_send()
    for d in range(1, n_x):
        sm_x_copy(d).wait_send()
    for d in range(1, n_s):
        sm_z_copy(d).wait_send()

    def settle(xo, carry):
        @pl.when((xo < x) | (core == 1))
        def _():
            for p in range(slabs):
                to_core(xo, 0, p).wait_send()
                to_core(xo, 1, p).wait_send()

        @pl.when(xo < x)
        def _():
            for p in range(slabs):
                to_owner(xo, 0, p).wait_send()
                to_owner(xo, 1, p).wait_send()

        return carry

    lax.fori_loop(0, x + 1, settle, 0)

    def settle_tp(r, carry):
        exchange(r).wait_send()
        return carry

    lax.fori_loop(0, per, settle_tp, 0)

    cross.finish()
    spread.finish()
    extra.finish()


def tail(groups, n_s, n_c, hidden, q, k, v, up, att, lse, tok, gains, shifts, w, part, small, out_bias, gfirst, second, bank, bank_send, *grad_inputs):
    slabs, length, unused = q.shape
    width = tok.shape[1]
    n_x = n_c // 2
    bf16, f32 = jnp.bfloat16, jnp.float32
    vmem, anywhere = pl.BlockSpec(memory_space=pltpu.VMEM), pl.BlockSpec(memory_space=pl.ANY)
    shape, scratch, dma = jax.ShapeDtypeStruct, pltpu.VMEM, pltpu.SemaphoreType.DMA
    pair = (2, slabs, length, TILE)
    total = sum(count for name, count in groups)
    chunks, rows = total // n_c, width // n_s
    early = (total - groups[-1][1]) // n_c
    return pl.pallas_call(
        partial(tail_kernel, n_s, n_c, groups, early),
        out_shape=(
            shape((length, width), f32), shape((length, width), bf16),
            shape((rows, total * TILE), bf16), shape((rows, hidden.shape[0] * n_c * TILE), bf16),
            shape(small.shape, f32), shape(bank_send.shape, bf16),
        ),
        in_specs=[vmem, anywhere, anywhere] + [vmem] * 6
        + [anywhere]
        + [vmem] * 3 + [anywhere] * 4 + [vmem] * (len(grad_inputs) + 1),
        out_specs=(vmem,) * 5 + (anywhere,),
        scratch_shapes=[
            scratch(k.shape, bf16), scratch(k.shape, bf16),
            scratch((slabs, 2, length, TILE), bf16), scratch((slabs, 2, length, TILE), bf16),
            scratch((TILE, length), f32), scratch((slabs, 2, 1, length), f32), scratch(q.shape, f32),
            scratch(q.shape, bf16), scratch(q.shape, bf16), scratch(q.shape, bf16),
            scratch((length, width), bf16),
            scratch((n_x,) + pair, bf16), scratch((n_x - 1,) + pair, bf16),
            scratch((length, width), bf16), scratch((length, width), bf16),
            scratch((length, width), bf16), scratch((length // BLOCK, BLOCK, width), f32),
            scratch((3 * slabs, width, TILE), bf16),
            scratch(k.shape, bf16), scratch(k.shape, bf16),
            scratch(bank.shape, bf16), scratch((chunks, width, TILE), bf16),
            scratch(small.shape, f32), scratch(small.shape, f32),
            scratch((n_x,) + small.shape, f32), scratch((n_s,) + small.shape, f32),
            dma((n_x, 2, slabs)), dma((n_x, 2, slabs)), dma((n_x - 1, 2, slabs)), dma((n_x - 1, 2, slabs)),
            dma((length // BLOCK,)), dma((length // BLOCK,)), dma,
            dma((n_x + n_s - 1,)), dma((n_x + n_s - 1,)),
            dma, dma, dma((length // BLOCK,)), dma, dma, dma, dma((2,)),
            *cross_scratch(chunks, width, n_s, n_c),
            *spread_scratch(chunks, width, n_s, n_c),
            *spread_scratch(hidden.shape[0], width, n_s, n_c),
        ],
        compiler_params=pltpu.CompilerParams(collective_id=3, has_side_effects=True, vmem_limit_bytes=64 << 20),
        name="tail",
    )(q, k, v, up, att, lse, tok, gains, shifts, w, part, small, out_bias, gfirst, second, bank, bank_send, *grad_inputs, hidden)


def final_kernel(
    slabs, units, res, hidden, mine, received, small,
    neigh, gains, shifts, head, outs, up_bias, self_in, self_out, cross_q, memory, cross_out, up, down,
):
    f32 = jnp.float32
    neigh[...] = mine[...].astype(f32) + received[...].astype(f32)
    local = slabs * TILE
    at = 0
    for j in range(2):
        memory[:, j, :] = res[:, (at + j * slabs) * TILE : (at + (j + 1) * slabs) * TILE].astype(f32)
    at += 2 * slabs
    self_out[...] = res[:, at * TILE : (at + slabs) * TILE].astype(f32)
    at += slabs
    cross_q[...] = res[:, at * TILE : (at + slabs) * TILE].astype(f32)
    at += slabs
    cross_out[...] = res[:, at * TILE : (at + slabs) * TILE].astype(f32)
    at += slabs
    for j in range(3):
        self_in[j] = res[:, (at + j * slabs) * TILE : (at + (j + 1) * slabs) * TILE].astype(f32)
    up[...] = hidden[:, : units * TILE].astype(f32)
    down[...] = hidden[:, units * TILE :].astype(f32)
    gains[...] = small[0:3, :]
    shifts[...] = small[3:6, :]
    outs[...] = small[6:9, :]
    width = small.shape[1]
    for j in range(4):
        head[j : j + 1, :] = small[9 + j // 2 : 10 + j // 2, (j % 2) * local : (j % 2 + 1) * local]
    for j in range(units * TILE // width):
        up_bias[:, j * width : (j + 1) * width] = small[11 + j : 12 + j, :]


def final(slabs, units, res, hidden, mine, received, small):
    f32 = jnp.float32
    shape = jax.ShapeDtypeStruct
    rows, local, width = res.shape[0], slabs * TILE, small.shape[1]
    out_shape = (
        shape(mine.shape, f32), shape((3, width), f32), shape((3, width), f32), shape((4, local), f32),
        shape((3, width), f32), shape((1, units * TILE), f32),
        shape((3, rows, local), f32), shape((rows, local), f32), shape((rows, local), f32),
        shape((rows, 2, local), f32), shape((rows, local), f32),
        shape((rows, units * TILE), f32), shape((rows, units * TILE), f32),
    )

    vmem = pl.BlockSpec(memory_space=pltpu.VMEM)
    return pl.pallas_call(
        partial(final_kernel, slabs, units),
        out_shape=out_shape,
        in_specs=[vmem] * 5,
        out_specs=(vmem,) * len(out_shape),
        compiler_params=pltpu.CompilerParams(vmem_limit_bytes=60 << 20),
        name="final",
    )(res, hidden, mine, received, small)


def slabbed(matrix):
    rows, columns = matrix.shape
    return matrix.reshape(rows, columns // TILE, TILE).transpose(1, 0, 2)


def shards(
    tokens,
    cotangent,
    neighbours,
    neighbour_ids,
    norm_gains,
    norm_shifts,
    head_bias,
    out_bias,
    up_bias,
    self_input,
    self_output,
    cross_query,
    cross_memory,
    cross_output,
    hidden_up,
    hidden_down,
):
    n_s, n_c = lax.axis_size("shard"), lax.axis_size("ctx")
    slice_rows = self_input.shape[0]
    shard = slabbed(
        jnp.concatenate(
            [
                self_input.reshape(slice_rows, -1),
                self_output.T,
                cross_memory.reshape(slice_rows, -1),
                cross_query,
                cross_output.T,
                hidden_up,
                hidden_down.T,
            ],
            axis=1,
        )
    )
    tok, cot = tokens[0], cotangent[0]
    length, width = tok.shape
    local = self_output.shape[0]
    slabs, units = local // TILE, hidden_up.shape[1] // TILE
    counts = (3 * slabs, slabs, 2 * slabs, slabs, slabs, units, units)
    names = ("self_in", "self_out", "memory", "cross_q", "cross_out", "up", "down")
    at, edge = {}, 0
    for name, count in zip(names, counts):
        at[name] = edge
        edge += count
    bank_shape = neighbours.shape[1:]
    bank = neighbours.reshape(bank_shape[0] * bank_shape[1], width)
    ids = neighbour_ids[0].T
    cut = at["up"]
    weights, q, k, v, att, lse = front(shard, tok, norm_gains, norm_shifts, head_bias, n_s, n_c, cut)
    n2, sl, fl, mx, gcq, ga, dks, dvs, gfirst, part, second, sums, up_sums, head_cross, hidden = chain(
        at, ids, att, tok, cot, bank, shard, norm_gains, norm_shifts, head_bias, out_bias, up_bias[None], weights,
        bank_shape[0], BLOCK, n_s, n_c,
    )
    mg, mine, send, head_memory = bank_back(
        ids, dks, dvs, weights, at["memory"], bank_shape[0], bank_shape[1]
    )
    small = jnp.concatenate(
        [
            sums[:9],
            jnp.zeros((1, width), jnp.float32),
            jnp.concatenate([head_cross, head_memory]).reshape(1, width),
            up_sums.reshape(-1, width),
        ]
    )
    small = jnp.pad(small, ((0, 16 - small.shape[0]), (0, 0)))
    lengths = dict(zip(names, counts))
    groups = [(name, lengths[name]) for name in ("memory", "self_out", "cross_q", "cross_out", "self_in")]
    grad_tokens, result, grads, hidden_grads, small, received = tail(
        groups, n_s, n_c, hidden, q, k, v, ga, att, lse, tok, norm_gains, norm_shifts, weights, part, small, out_bias, gfirst, second,
        bank, send, fl, n2, sl, mg, gcq, mx,
    )
    (
        neigh, gains, shifts, head, outs, bias_up, self_in, self_out, cross_q, memory, cross_out, up, down,
    ) = final(slabs, units, grads, hidden_grads, mine, received, small)
    return (
        result[None],
        grad_tokens[None],
        neigh.reshape((1,) + bank_shape[:2] + (width // 2,)),
        gains,
        shifts,
        head,
        outs,
        bias_up.reshape(-1),
        self_in.transpose(1, 0, 2),
        self_out.T,
        cross_q,
        memory,
        cross_out.T,
        up,
        down.T,
    )


def solution(mesh):
    placed = (
        P("shard", "ctx", None),
        P("shard", "ctx", None),
        P("shard", "ctx", None, None),
        P("shard", "ctx", None),
        P(),
        P(),
        P(None, "tp"),
        P(),
        P("tp"),
        P("shard", None, "tp"),
        P("tp", "shard"),
        P("shard", "tp"),
        P("shard", None, "tp"),
        P("tp", "shard"),
        P("shard", "tp"),
        P("tp", "shard"),
    )
    return jax.shard_map(
        shards,
        mesh=mesh,
        in_specs=placed,
        out_specs=(
            P("shard", "ctx", None),
            P("shard", "ctx", None),
            P("shard", "ctx", None, "tp"),
            P(),
            P(),
            P(None, "tp"),
            P(),
            P("tp"),
            P("shard", None, "tp"),
            P("tp", "shard"),
            P("shard", "tp"),
            P("shard", None, "tp"),
            P("tp", "shard"),
            P("shard", "tp"),
            P("tp", "shard"),
        ),
        check_vma=False,
    )
```

```python
from functools import partial

import jax
import jax.numpy as jnp
from jax import lax
from jax.experimental import pallas as pl
from jax.experimental.pallas import tpu as pltpu
from jax.sharding import PartitionSpec as P

HEAD_DIM = 64
BLOCK = 256


EPSILON = 1e-05
NEGATIVE = -1e30
HIGHEST = lax.Precision.HIGHEST


MESH = pl.DeviceIdType.MESH
LOG2E = 1.4426950408889634
TILE = 128


def aligned(index, size):
    return pl.multiple_of(index * size, size)


def rows_at(index, size):
    return pl.ds(pl.multiple_of(index * size, size), size)


def remote(src, dst, send, recv, where):
    return pltpu.make_async_remote_copy(
        src_ref=src, dst_ref=dst, send_sem=send, recv_sem=recv, device_id=where, device_id_type=MESH
    )


class Place:
    def __init__(self, n_s, n_c):
        self.n_s, self.n_c, self.n_x = n_s, n_c, n_c // 2
        self.s, self.c, self.t = lax.axis_index("shard"), lax.axis_index("ctx"), lax.axis_index("tp")
        self.x, self.core = lax.div(self.c, 2), lax.rem(self.c, 2)
        self.sibling_index = self.x * 2 + 1 - self.core
        self.sibling, self.peer = {"ctx": self.sibling_index}, {"tp": 1 - self.t}

    def along_x(self, d):
        return {"ctx": lax.rem(self.x + d, self.n_x) * 2 + self.core}

    def along_s(self, d):
        return {"shard": lax.rem(self.s + d, self.n_s)}

    def source_x(self, d):
        return lax.rem(self.x - d + self.n_x, self.n_x)

    def greet(self):
        barrier = pltpu.get_barrier_semaphore()
        partners = [self.along_x(d) for d in range(1, self.n_x)] + [self.along_s(d) for d in range(1, self.n_s)]
        partners += [self.sibling, self.peer]
        for where in partners:
            pl.semaphore_signal(barrier, inc=1, device_id=where, device_id_type=MESH)
        pl.semaphore_wait(barrier, len(partners))


def gather_semaphores(chunks, n_s, n_c):
    dma, n_x = pltpu.SemaphoreType.DMA, n_c // 2
    shapes = [(chunks, n_s - 1)] * 2 + [(chunks, n_s - 1, n_x - 1)] * 2 + [(chunks, n_s - 1, n_x)] * 2
    return [dma(shape) for shape in shapes] + [dma((1,))]


class Gather:
    def __init__(self, place, own, full, chunks, base, semaphores):
        self.place, self.own, self.full, self.chunks, self.base = place, own, full, chunks, base
        self.zs, self.zr, self.xs, self.xr, self.cs, self.cr, self.local = semaphores
        self.rows = own.shape[1]
        self.last = chunks + 1
        total = chunks * place.n_c
        self.own_copy = pltpu.make_async_copy(
            own.at[pl.ds(base, total)],
            full.at[pl.ds(base, total), pl.ds(aligned(place.s, self.rows), self.rows), :],
            self.local.at[0],
        )

    def block(self, origin, k, quarter):
        slab = self.base + k * self.place.n_c + quarter
        return self.full.at[slab, pl.ds(aligned(origin, self.rows), self.rows), :]

    def source(self, d):
        return lax.rem(self.place.s - d + self.place.n_s, self.place.n_s)

    def own_out(self, d, k):
        return remote(
            self.own.at[self.base + k * self.place.n_c + self.place.c], self.block(self.place.s, k, self.place.c),
            self.zs.at[k, d - 1], self.zr.at[k, d - 1], self.place.along_s(d),
        )

    def z_in(self, d, k):
        here = self.block(self.source(d), k, self.place.c)
        return remote(here, here, self.zs.at[k, d - 1], self.zr.at[k, d - 1], self.place.along_s(d))

    def x_move(self, d, k, e, incoming):
        quarter = self.place.source_x(e) * 2 + self.place.core if incoming else self.place.c
        here = self.block(self.source(d), k, quarter)
        return remote(here, here, self.xs.at[k, d - 1, e - 1], self.xr.at[k, d - 1, e - 1], self.place.along_x(e))

    def core_move(self, d, k, e, incoming):
        core = 1 - self.place.core if incoming else self.place.core
        here = self.block(self.source(d), k, self.place.source_x(e) * 2 + core)
        return remote(here, here, self.cs.at[k, d - 1, e], self.cr.at[k, d - 1, e], self.place.sibling)

    def each(self, low, high, body):
        def one(i, carry):
            body(i)
            return carry

        lax.fori_loop(low, high, one, 0)

    def start(self):
        self.own_copy.start()

        def send(k):
            for d in range(1, self.place.n_s):
                self.own_out(d, k).start()

        self.each(0, self.chunks, send)

    def advance(self, i):
        @pl.when(i < self.chunks)
        def _():
            for d in range(1, self.place.n_s):
                self.z_in(d, i).wait_recv()
                for e in range(1, self.place.n_x):
                    self.x_move(d, i, e, False).start()
                self.core_move(d, i, 0, False).start()

        @pl.when(i > 0)
        def _():
            for d in range(1, self.place.n_s):
                for e in range(1, self.place.n_x):
                    self.x_move(d, i - 1, e, True).wait_recv()
                    self.core_move(d, i - 1, e, False).start()

    def advance_range(self, low, high):
        self.each(low, high, self.advance)

    def complete_range(self, low, high):
        def one(k):
            for d in range(1, self.place.n_s):
                for e in range(self.place.n_x):
                    self.core_move(d, k, e, True).wait_recv()

        self.each(low, high, one)

    def finish(self):
        def one(k):
            for d in range(1, self.place.n_s):
                self.own_out(d, k).wait_send()
                for e in range(1, self.place.n_x):
                    self.x_move(d, k, e, False).wait_send()
                for e in range(self.place.n_x):
                    self.core_move(d, k, e, False).wait_send()

        self.each(0, self.chunks, one)


RING = 16


def cross_scratch(chunks, width, n_s, n_c):
    bf16, vmem, dma, n_x = jnp.bfloat16, pltpu.VMEM, pltpu.SemaphoreType.DMA, n_c // 2
    return [
        vmem((min(max(RING // n_c, 2), chunks), n_c, width, TILE), bf16),
        vmem((chunks, n_x, width, TILE), bf16),
        vmem((chunks, n_x - 1, width, TILE), bf16),
        dma((chunks, n_x)), dma((chunks, n_x)), dma((chunks, n_x - 1)), dma((chunks, n_x - 1)),
    ]


def spread_scratch(chunks, width, n_s, n_c):
    bf16, vmem, dma, n_x = jnp.bfloat16, pltpu.VMEM, pltpu.SemaphoreType.DMA, n_c // 2
    rows = width // n_s
    return [
        vmem((chunks, n_s - 1, rows, TILE), bf16),
        dma((chunks, n_s - 1)), dma((chunks, n_s - 1)),
        dma((chunks, n_x - 1)), dma((chunks, n_x - 1)), dma((chunks, n_x)), dma((chunks, n_x)),
    ]


class Cross:
    def __init__(self, place, total, refs):
        self.place, self.total = place, total
        self.gbuf, self.a_buf, self.b_buf, self.as_, self.ar, self.bs, self.br = refs
        self.chunks, self.ring = self.a_buf.shape[0], self.gbuf.shape[0]

    def a_out(self, kk, e):
        slot = lax.rem(kk, self.ring)
        source = self.gbuf.at[slot, e * 2 + 1 - self.place.core]
        return remote(source, self.a_buf.at[kk, e], self.as_.at[kk, e], self.ar.at[kk, e], self.place.sibling)

    def reserve(self, kk):
        if kk >= self.ring:
            for e in range(self.place.n_x):
                self.a_out(kk - self.ring, e).wait_send()
        return kk % self.ring

    def send(self, kk):
        for e in range(self.place.n_x):
            self.a_out(kk, e).start()

    def b_out(self, kk, d):
        to = lax.rem(self.place.x + d, self.place.n_x)
        return remote(
            self.a_buf.at[kk, to], self.b_buf.at[kk, d - 1], self.bs.at[kk, d - 1], self.br.at[kk, d - 1],
            self.place.along_x(d),
        )

    def stage_b(self, kk):
        x, core, slot = self.place.x, self.place.core, lax.rem(kk, self.ring)
        for d in range(1, self.place.n_x):
            e = lax.rem(x + d, self.place.n_x)
            self.a_out(kk, e).wait_recv()
            self.a_buf[kk, e] = self.gbuf[slot, e * 2 + core] + self.a_buf[kk, e]
            self.b_out(kk, d).start()
        self.a_out(kk, x).wait_recv()
        self.a_buf[kk, x] = self.gbuf[slot, self.place.c] + self.a_buf[kk, x]

    def stage_c(self, kk):
        total = self.a_buf[kk, self.place.x]
        for d in range(1, self.place.n_x):
            self.b_out(kk, d).wait_recv()
            total = total + self.b_buf[kk, d - 1]
        self.total[kk] = total

    def step(self, i, produce, low, high):
        for kk in range(low, high):
            pl.when(i == kk)(partial(produce, kk))
        for lag, stage in ((1, self.stage_b), (2, self.stage_c)):
            kk = i - lag
            pl.when((kk >= 0) & (kk < self.chunks))(partial(stage, kk))

    def finish(self):
        def one(kk, carry):
            @pl.when(kk >= max(self.chunks - self.ring, 0))
            def _():
                for e in range(self.place.n_x):
                    self.a_out(kk, e).wait_send()

            for d in range(1, self.place.n_x):
                self.b_out(kk, d).wait_send()
            return carry

        lax.fori_loop(0, self.chunks, one, 0)


class Spread:
    def __init__(self, place, total, res, refs):
        self.place, self.total, self.res = place, total, res
        self.z_in, self.zs, self.zr, self.fs, self.fr, self.hs, self.hr = refs
        self.chunks, self.rows = self.z_in.shape[0], self.z_in.shape[2]

    def shard_rows(self, index):
        return pl.ds(aligned(index, self.rows), self.rows)

    def z_copy(self, d, kk):
        theirs = self.shard_rows(lax.rem(self.place.s + d, self.place.n_s))
        return remote(
            self.total.at[kk, theirs, :], self.z_in.at[kk, d - 1], self.zs.at[kk, d - 1], self.zr.at[kk, d - 1],
            self.place.along_s(d),
        )

    def send(self, kk):
        for d in range(1, self.place.n_s):
            self.z_copy(d, kk).start()

    def block(self, kk, quarter):
        return self.res.at[:, pl.ds(pl.multiple_of((kk * self.place.n_c + quarter) * TILE, TILE), TILE)]

    def f_move(self, kk, d, incoming):
        here = self.block(kk, self.place.source_x(d) * 2 + self.place.core if incoming else self.place.c)
        return remote(here, here, self.fs.at[kk, d - 1], self.fr.at[kk, d - 1], self.place.along_x(d))

    def h_move(self, kk, d, incoming):
        core = 1 - self.place.core if incoming else self.place.core
        here = self.block(kk, self.place.source_x(d) * 2 + core)
        return remote(here, here, self.hs.at[kk, d], self.hr.at[kk, d], self.place.sibling)

    def stage_d(self, kk):
        total = self.total[kk, self.shard_rows(self.place.s), :].astype(jnp.float32)
        for d in range(1, self.place.n_s):
            self.z_copy(d, kk).wait_recv()
            total = total + self.z_in[kk, d - 1].astype(jnp.float32)
        lanes = pl.ds(pl.multiple_of((kk * self.place.n_c + self.place.c) * TILE, TILE), TILE)
        self.res[:, lanes] = total.astype(jnp.bfloat16)
        for d in range(1, self.place.n_x):
            self.f_move(kk, d, False).start()
        self.h_move(kk, 0, False).start()

    def stage_e(self, kk):
        for d in range(1, self.place.n_x):
            self.f_move(kk, d, True).wait_recv()
            self.h_move(kk, d, False).start()

    def stage_f(self, kk):
        for d in range(self.place.n_x):
            self.h_move(kk, d, True).wait_recv()

    def step(self, i):
        for lag, stage in ((0, self.stage_d), (1, self.stage_e), (2, self.stage_f)):
            kk = i - lag
            pl.when((kk >= 0) & (kk < self.chunks))(partial(stage, kk))

    def finish(self):
        def one(kk, carry):
            for d in range(1, self.place.n_x):
                self.f_move(kk, d, False).wait_send()
            for d in range(self.place.n_x):
                self.h_move(kk, d, False).wait_send()
            for d in range(1, self.place.n_s):
                self.z_copy(d, kk).wait_send()
            return carry

        lax.fori_loop(0, self.chunks, one, 0)


def produce_group(cross, order, kk, left_of, slab_of):
    slot, at, n_c = cross.reserve(kk), 0, cross.place.n_c
    while at < n_c:
        name, index = order[kk * n_c + at]
        count = 1
        while at + count < n_c and order[kk * n_c + at + count][0] == name:
            count += 1
        right = jnp.concatenate([slab_of(name, index + i) for i in range(count)], axis=1)
        product = dot_tn(left_of(name)[...], right).astype(jnp.bfloat16)
        for i in range(count):
            cross.gbuf[slot, at + i] = product[:, i * TILE : (i + 1) * TILE]
        at += count
    cross.send(kk)


def dot_nn(left, right):
    return lax.dot_general(left, right, (((1,), (0,)), ((), ())), preferred_element_type=jnp.float32)


def dot_nt(left, right):
    return lax.dot_general(left, right, (((1,), (1,)), ((), ())), preferred_element_type=jnp.float32)


def dot_tn(left, right):
    return lax.dot_general(left, right, (((0,), (0,)), ((), ())), preferred_element_type=jnp.float32)


def joined(ref, low, high):
    return jnp.concatenate([ref[index] for index in range(low, high)], axis=1)


def norm_parts(values):
    centre = values - jnp.mean(values, axis=-1, keepdims=True)
    spread = jnp.mean(centre * centre, axis=-1, keepdims=True)
    rate = lax.rsqrt(spread + EPSILON)
    return centre * rate, rate


def norm_rows(values, gain, shift):
    return (norm_parts(values)[0] * gain + shift).astype(jnp.bfloat16)


def half_masks(shape):
    lane = lax.broadcasted_iota(jnp.int32, shape, len(shape) - 1)
    return lane < HEAD_DIM


def keep_half(values, low, half):
    zero = jnp.zeros_like(values)
    return jnp.where(low, values, zero) if half == 0 else jnp.where(low, zero, values)


def fold(values, combine):
    result = values[:, :TILE]
    for at in range(TILE, values.shape[1], TILE):
        result = combine(result, values[:, at : at + TILE])
    return result


def attend(c, q, k, v, att, lse, scores, after):
    slabs, length, unused = q.shape
    scale = HEAD_DIM ** (-0.5) * LOG2E
    low = half_masks((length, TILE))
    lane = lax.broadcasted_iota(jnp.int32, (length, TILE), 1)
    steps = [(low_row, low_row + BLOCK) for low_row in range(0, length, BLOCK)]

    def one(p, carry):
        outs = []
        logs = lse[...]
        for half in (0, 1):
            part = keep_half(q[p], low, half)

            def first(j, peak):
                s = dot_nt(part, k[p, rows_at(j, length), :]) * scale
                scores[j] = s
                return jnp.maximum(peak, fold(s, jnp.maximum))

            peak = lax.fori_loop(0, c, first, jnp.full((length, TILE), NEGATIVE, jnp.float32))
            own_keys, own_values = k[p, rows_at(c, length), :], v[p, rows_at(c, length), :]
            tops = []
            for begin, end in steps:
                s = dot_nt(part[begin:end], own_keys[:end]) * scale
                scores[c, begin:end, :end] = s
                best = jnp.maximum(peak[begin:end], fold(s, jnp.maximum))
                tops.append(jnp.max(best, axis=1, keepdims=True))
            top = jnp.concatenate(tops, axis=0)

            def second(j, state):
                raised = jnp.exp2(scores[j] - top)
                mixed = dot_nn(raised.astype(jnp.bfloat16), v[p, rows_at(j, length), :])
                return state[0] + fold(raised, jnp.add), state[1] + mixed

            zero = jnp.zeros((length, TILE), jnp.float32)
            total, mixed = lax.fori_loop(0, c, second, (zero, zero))
            totals, mixes = [], []
            for (begin, end), best in zip(steps, tops):
                raised = jnp.exp2(scores[c, begin:end, :end] - best)
                totals.append(total[begin:end] + fold(raised, jnp.add))
                mixes.append(mixed[begin:end] + dot_nn(raised.astype(jnp.bfloat16), own_values[:end]))
            total = jnp.sum(jnp.concatenate(totals, axis=0), axis=1, keepdims=True)
            outs.append(jnp.concatenate(mixes, axis=0) / total)
            logs = jnp.where(lane == p * 2 + half, top + jnp.log2(total), logs)
            after(p * 2 + half)
        lse[...] = logs
        att[p] = jnp.where(low, outs[0], outs[1]).astype(jnp.bfloat16)
        return carry

    lse[...] = jnp.zeros_like(lse)
    lax.fori_loop(0, slabs, one, 0)


def front_kernel(
    n_s, n_c, chunks, shard, tok, gains, shifts, bias, w, q, k, v, att, lse,
    others, normed, scores, zs, zr, xs, xr, cs, cr, own_sem, txs, txr, tys, tyr, tcs, tcr,
):
    place = Place(n_s, n_c)
    c, x, core, n_x = place.c, place.x, place.core, place.n_x
    length, width = tok.shape
    slabs = q.shape[0]
    place.greet()
    gather = Gather(place, shard, w, chunks, 0, (zs, zr, xs, xr, cs, cr, own_sem))

    half = length // 2

    def token_half(index, which):
        return others.at[pl.ds(pl.multiple_of(index * length + which * half, half), half), :]

    def run(pair, method):
        copy, valid = pair
        pl.when(valid)(getattr(copy, method))

    def token_x(d):
        own_half = tok.at[pl.ds(pl.multiple_of(place.t * half, half), half), :]
        copy = remote(own_half, token_half(c, place.t), txs.at[d - 1], txr.at[d - 1], place.along_x(d))
        return copy, lax.rem(x + d, n_x) > x

    def token_in(d):
        here = token_half(place.source_x(d) * 2 + core, place.t)
        return remote(here, here, txs.at[d - 1], txr.at[d - 1], place.sibling), place.source_x(d) < x

    def token_peer(d, incoming):
        here = token_half(place.source_x(d) * 2 + core, 1 - place.t if incoming else place.t)
        return remote(here, here, tys.at[d - 1], tyr.at[d - 1], place.peer), place.source_x(d) < x

    def token_relay(d, which, incoming):
        here = token_half(place.source_x(d) * 2 + (1 - core if incoming else core), which)
        return remote(here, here, tcs.at[d, which], tcr.at[d, which], place.sibling), place.source_x(d) < x

    def token_own(which):
        own_half = tok.at[pl.ds(which * half, half), :]
        return remote(own_half, token_half(c, which), tcs.at[0, which], tcr.at[0, which], place.sibling), core == 0

    def token_own_in(which):
        here = token_half(place.sibling_index, which)
        return remote(here, here, tcs.at[0, which], tcr.at[0, which], place.sibling), core == 1

    for d in range(1, n_x):
        run(token_x(d), "start")
    for which in (0, 1):
        run(token_own(which), "start")
    gather.start()

    def norm_block(source, base, j):
        def tile(i, carry):
            rows = source[pl.ds(pl.multiple_of(base + i * TILE, TILE), TILE), :].astype(jnp.float32)
            normed[j, rows_at(i, TILE), :] = norm_rows(rows, gains[0:1, :], shifts[0:1, :])
            return carry

        lax.fori_loop(0, length // TILE, tile, 0)

    norm_block(tok, 0, c)
    needed = -(-3 * slabs // n_c)
    ready = min(needed + 1, gather.last)
    gather.advance_range(0, 1)
    for d in range(1, n_x):
        run(token_in(d), "wait_recv")
        run(token_peer(d, False), "start")
        for which in (0, 1):
            pl.when(place.t == which)(lambda: run(token_relay(d, which, False), "start"))
    gather.advance_range(1, 2)
    for d in range(1, n_x):
        run(token_peer(d, True), "wait_recv")
        for which in (0, 1):
            pl.when(place.t != which)(lambda: run(token_relay(d, which, False), "start"))
    gather.advance_range(2, ready)
    for which in (0, 1):
        for d in range(1, n_x):
            run(token_relay(d, which, True), "wait_recv")
        run(token_own_in(which), "wait_recv")

    def norm_other(j, carry):
        norm_block(others, j * length, j)
        return carry

    lax.fori_loop(0, c, norm_other, 0)
    gather.own_copy.wait()
    gather.complete_range(0, needed)

    def project(j, which, row_bias):
        result = dot_nn(normed[j], joined(w, which * slabs, (which + 1) * slabs))
        if row_bias is not None:
            result = result + row_bias
        return result.astype(jnp.bfloat16)

    def project_keys(j, carry):
        spot = rows_at(j, length)
        for which, target, row_bias in ((1, k, None), (2, v, bias[1:2, :])):
            result = project(j, which, row_bias)
            for p in range(slabs):
                target[p, spot, :] = result[:, p * TILE : (p + 1) * TILE]
        return carry

    lax.fori_loop(0, c + 1, project_keys, 0)
    queries = project(c, 0, bias[0:1, :])
    for p in range(slabs):
        q[p] = queries[:, p * TILE : (p + 1) * TILE]
    pieces = 2 * slabs

    def after(step):
        pl.when(ready + step < gather.last)(lambda: gather.advance(ready + step))

    attend(c, q, k, v, att, lse, scores, after)
    gather.advance_range(min(ready + pieces, gather.last), gather.last)
    gather.complete_range(needed, chunks)
    gather.finish()
    for d in range(1, n_x):
        run(token_x(d), "wait_send")
        run(token_peer(d, False), "wait_send")
        for which in (0, 1):
            run(token_relay(d, which, False), "wait_send")
    for which in (0, 1):
        run(token_own(which), "wait_send")


def front(shard, tok, gains, shifts, bias, n_s, n_c, cut):
    total, rows, unused = shard.shape
    length, width = tok.shape
    slabs = bias.shape[1] // TILE
    chunks, n_x = cut // n_c, n_c // 2
    dma, shape, scratch = pltpu.SemaphoreType.DMA, jax.ShapeDtypeStruct, pltpu.VMEM
    vmem = pl.BlockSpec(memory_space=pltpu.VMEM)
    bf16, f32 = jnp.bfloat16, jnp.float32
    return pl.pallas_call(
        partial(front_kernel, n_s, n_c, chunks),
        out_shape=(
            shape((cut, rows * n_s, TILE), bf16),
            shape((slabs, length, TILE), bf16),
            shape((slabs, length * n_c, TILE), bf16),
            shape((slabs, length * n_c, TILE), bf16),
            shape((slabs, length, TILE), bf16),
            shape((length, TILE), f32),
        ),
        in_specs=[vmem] * 5,
        out_specs=(vmem,) * 6,
        scratch_shapes=[
            scratch((length * n_c, width), bf16), scratch((n_c, length, width), bf16),
            scratch((n_c, length, length), f32),
            *gather_semaphores(chunks, n_s, n_c),
            dma((n_x - 1,)), dma((n_x - 1,)), dma((n_x - 1,)), dma((n_x - 1,)), dma((n_x, 2)), dma((n_x, 2)),
        ],
        compiler_params=pltpu.CompilerParams(collective_id=0, has_side_effects=True, vmem_limit_bytes=60 << 20),
        name="front",
    )(shard, tok, gains, shifts, bias)


WIDE = 4
ROWS = 256


def chain_kernel(
    at, chunk, banks, n_s, n_c, ids, att, tok, cot, bank_far, shard, gains, shifts, bias, out_bias, up_bias, w_front,
    n2, sl, fl, mx, gcq, ga, dks, dvs, gfirst, part, second, sums, up_sums, head_sums, total_out,
    mem_k, mem_v, first, gsecond, weights, gmix, cq, tx, rx, ss, rs, w, wsem, n3, act, gh, bank, bank_sem, *engines
):
    place = Place(n_s, n_c)
    peer = place.peer
    cut = w_front.shape[0]
    place.greet()
    gather = Gather(place, shard, w, (shard.shape[0] - cut) // n_c, cut, engines[:7])
    cross = Cross(place, total_out, engines[7:])
    edges = [at["self_out"], at["memory"], cut]

    def load(i):
        low, high = edges[i], edges[i + 1]
        return pltpu.make_async_copy(w_front.at[pl.ds(low, high - low)], w.at[pl.ds(low, high - low)], wsem.at[i])

    load(0).start()
    bank_copy = pltpu.make_async_copy(bank_far, bank, bank_sem)
    bank_copy.start()
    load(1).start()
    gather.start()
    f32, bf16 = jnp.float32, jnp.bfloat16
    length, width = tok.shape
    slabs = att.shape[0]
    units = act.shape[0]
    span = bank_far.shape[0] // banks
    picks, stretches = ids.shape
    stretch = length // stretches
    keys_each = picks * span
    scale = HEAD_DIM ** (-0.5)
    count = length // chunk
    tiles = chunk // ROWS
    low = half_masks((stretch, TILE))
    sums[...] = jnp.zeros_like(sums)
    up_sums[...] = jnp.zeros_like(up_sums)
    head_sums[...] = jnp.zeros_like(head_sums)

    def exchange(phase, r):
        rows = rows_at(r, chunk)
        return remote(tx.at[phase, rows, :], rx.at[phase, rows, :], ss.at[phase, r], rs.at[phase, r], peer)

    def every(stage):
        def run(r, carry):
            stage(r)
            return carry

        lax.fori_loop(0, count, run, 0)

    def per_tile(r, body):
        def run(i, carry):
            body(pl.ds(pl.multiple_of(r * chunk + i * ROWS, ROWS), ROWS))
            return carry

        lax.fori_loop(0, tiles, run, 0)

    def out_product(target, r, left, name, total):
        rows = rows_at(r, chunk)
        low_slab = at[name]
        step = 256

        def run(n, carry):
            cols = pl.ds(pl.multiple_of(n * step, step), step)
            weight = jnp.concatenate([w[low_slab + i, cols, :] for i in range(total)], axis=1)
            product = dot_nt(jnp.concatenate([left[i, rows, :] for i in range(total)], axis=1), weight)
            target[rows, cols] = product.astype(bf16)
            return carry

        lax.fori_loop(0, width // step, run, 0)

    def send_attended(r):
        out_product(tx.at[0], r, att, "self_out", slabs)
        exchange(0, r).start()

    load(0).wait()
    every(send_attended)
    load(1).wait()
    total = gather.last
    gather.advance_range(0, min(1, total))

    def memory(i, carry):
        rows = rows_at(i, 4 * span)
        for which, target, row_bias in ((0, mem_k, None), (1, mem_v, bias[3:4, :])):
            base = at["memory"] + which * slabs
            product = dot_nn(bank[rows, :], joined(w, base, base + slabs))
            if row_bias is not None:
                product = product + row_bias
            product = product.astype(bf16)
            for p in range(slabs):
                for e in range(4):
                    target[p, i * 4 + e] = product[e * span : (e + 1) * span, p * TILE : (p + 1) * TILE]
        return carry

    bank_copy.wait()
    lax.fori_loop(0, banks // 4, memory, 0)
    gather.advance_range(min(1, total), min(2, total))

    def narrow(source, r, base, row_bias, target):
        rows = rows_at(r, chunk)
        product = dot_nn(source[rows, :], joined(w, base, base + slabs))
        if row_bias is not None:
            product = product + row_bias
        product = product.astype(bf16)
        for p in range(slabs):
            target[p, rows, :] = product[:, p * TILE : (p + 1) * TILE]

    def picked(source, p, st):
        return jnp.concatenate(
            [source[p, ids[n, st]] for n in range(picks)], axis=0
        )

    def stacked(source, p, st):
        block = source[p, rows_at(st, stretch), :]
        return jnp.concatenate([keep_half(block, low, 0), keep_half(block, low, 1)], axis=0)

    def unstacked(both):
        return jnp.where(low, both[:stretch], both[stretch:])

    def total_of(phase, rows):
        return tx[phase, rows, :].astype(f32) + rx[phase, rows, :].astype(f32)

    def per_stretch(r, body):
        each = chunk // stretch

        def run(i, carry):
            writes = [body(p, r * each + i * WIDE + j) for j in range(WIDE) for p in range(slabs)]
            for write in writes:
                write()
            return carry

        lax.fori_loop(0, each // WIDE, run, 0)

    def cross_forward(r):
        exchange(0, r).wait_recv()

        def tile(rows):
            value = tok[rows, :].astype(f32) + total_of(0, rows) + out_bias[0:1, :]
            first[rows, :] = value
            n2[rows, :] = norm_rows(value, gains[1:2, :], shifts[1:2, :])

        per_tile(r, tile)
        narrow(n2, r, at["cross_q"], bias[2:3, :], cq)

        def one(p, st):
            keys, values = picked(mem_k, p, st), picked(mem_v, p, st)
            s = dot_nt(stacked(cq, p, st), keys) * (scale * LOG2E)
            raised = jnp.exp2(s - jnp.max(s, axis=1, keepdims=True))
            probs = raised / jnp.sum(raised, axis=1, keepdims=True)
            mixed = unstacked(dot_nn(probs.astype(bf16), values)).astype(bf16)

            def write():
                weights[p, st] = probs
                mx[p, rows_at(st, stretch), :] = mixed

            return write

        per_stretch(r, one)
        out_product(tx.at[1], r, mx, "cross_out", slabs)
        exchange(1, r).start()
        gather.advance_range(lax.min(2 + r, total), lax.min(3 + r, total))

    every(cross_forward)
    gather.advance_range(min(2 + count, total), total)
    gather.own_copy.wait()
    gather.complete_range(0, gather.chunks)
    curve = 0.7978845608028654
    cubic = 0.044715

    def feed(r):
        exchange(1, r).wait_recv()
        rows_all = rows_at(r, chunk)

        def tile(rows):
            value = first[rows, :] + total_of(1, rows) + out_bias[1:2, :]
            second[rows, :] = value
            n3[rows, :] = norm_rows(value, gains[2:3, :], shifts[2:3, :])

        per_tile(r, tile)

        def unit(j, carry):
            up = jnp.concatenate([w[at["up"] + 2 * j], w[at["up"] + 2 * j + 1]], axis=1)
            down = jnp.concatenate([w[at["down"] + 2 * j], w[at["down"] + 2 * j + 1]], axis=1)
            hidden = dot_nn(n3[rows_all, :], up) + up_bias[:, rows_at(j, 2 * TILE)]
            back = dot_nn(cot[rows_all, :], down)
            square = hidden * hidden
            bent = jnp.tanh(curve * hidden * (1.0 + cubic * square))
            half = 0.5 * (1.0 + bent)
            active = (hidden * half).astype(bf16)
            slope = half + 0.5 * hidden * (1.0 - bent * bent) * (curve * (1.0 + 3.0 * cubic * square))
            grad = (slope * back).astype(bf16)
            up_sums[j] = up_sums[j] + jnp.sum(grad.astype(f32), axis=0, keepdims=True)
            for i in range(2):
                lanes = slice(i * TILE, (i + 1) * TILE)
                act[2 * j + i, rows_all, :] = active[:, lanes]
                gh[2 * j + i, rows_all, :] = grad[:, lanes]
            return carry

        lax.fori_loop(0, units // 2, unit, 0)
        out_product(tx.at[2], r, gh, "up", units)
        exchange(2, r).start()

    every(feed)

    def result_product(r):
        out_product(part, r, act, "down", units)

    order = [(name, index) for name in ("up", "down") for index in range(units)]

    def left_of(name):
        return n3 if name == "up" else cot

    def slab_of(name, index):
        return (gh if name == "up" else act)[index]

    def produce(kk):
        produce_group(cross, order, kk, left_of, slab_of)

    steps = cross.chunks + 2

    def reduce_range(low, high):
        def one(i, carry):
            cross.step(i, produce, 0, cross.chunks)
            return carry

        lax.fori_loop(lax.min(low, steps), lax.min(high, steps), one, 0)

    def result_and_step(r):
        result_product(r)
        reduce_range(r, r + 1)

    every(result_and_step)

    def norm_back_rows(value, gain, upstream, row):
        spot, rate = norm_parts(value)
        scaled = upstream * gain
        sums[row : row + 1, :] = sums[row : row + 1, :] + jnp.sum(upstream * spot, axis=0, keepdims=True)
        sums[row + 3 : row + 4, :] = sums[row + 3 : row + 4, :] + jnp.sum(upstream, axis=0, keepdims=True)
        return rate * (
            scaled - jnp.mean(scaled, axis=-1, keepdims=True)
            - spot * jnp.mean(scaled * spot, axis=-1, keepdims=True)
        )

    def add_sum(row, values):
        sums[row : row + 1, :] = sums[row : row + 1, :] + jnp.sum(values, axis=0, keepdims=True)

    def cross_back(r):
        reduce_range(count + 2 * r, count + 2 * r + 1)
        exchange(2, r).wait_recv()

        def tile(rows):
            upstream = cot[rows, :].astype(f32)
            grad = upstream + norm_back_rows(second[rows, :], gains[2:3, :], total_of(2, rows), 2)
            add_sum(8, upstream)
            add_sum(7, grad)
            gsecond[rows, :] = grad
            sl[rows, :] = grad.astype(bf16)

        per_tile(r, tile)
        narrow(sl, r, at["cross_out"], None, gmix)

        def one(p, st):
            keys, values = picked(mem_k, p, st), picked(mem_v, p, st)
            grads, queries = stacked(gmix, p, st), stacked(cq, p, st)
            probs = weights[p, st]
            spread = dot_nt(grads, values)
            ds = (probs * (spread - jnp.sum(probs * spread, axis=1, keepdims=True))).astype(bf16)
            back = (unstacked(dot_nn(ds, keys)) * scale).astype(bf16)
            grad_keys = (dot_tn(ds, queries) * scale).astype(bf16)
            grad_values = dot_tn(probs.astype(bf16), grads).astype(bf16)

            def write():
                gcq[p, rows_at(st, stretch), :] = back
                dks[p, rows_at(st, keys_each), :] = grad_keys
                dvs[p, rows_at(st, keys_each), :] = grad_values

            return write

        per_stretch(r, one)
        out_product(tx.at[3], r, gcq, "cross_q", slabs)
        exchange(3, r).start()
        reduce_range(count + 2 * r + 1, count + 2 * r + 2)

    every(cross_back)

    def finish(r):
        exchange(3, r).wait_recv()

        def tile(rows):
            grad = gsecond[rows, :] + norm_back_rows(first[rows, :], gains[1:2, :], total_of(3, rows), 1)
            add_sum(6, grad)
            gfirst[rows, :] = grad
            fl[rows, :] = grad.astype(bf16)

        per_tile(r, tile)
        narrow(fl, r, at["self_out"], None, ga)
        reduce_range(3 * count + r, 3 * count + r + 1)

    every(finish)
    for p in range(slabs):
        head_sums[p] = jnp.sum(gcq[p].astype(f32), axis=0, keepdims=True)

    reduce_range(4 * count, steps)
    gather.finish()
    cross.finish()

    def settle(r):
        for phase in range(4):
            exchange(phase, r).wait_send()

    every(settle)


def chain(at, ids, att, tok, cot, bank, shard, gains, shifts, bias, out_bias, up_bias, w_front, banks, chunk, n_s, n_c):
    length, width = tok.shape
    slabs = att.shape[0]
    units = up_bias.shape[1] // TILE
    picks, stretches = ids.shape
    stretch, span = length // stretches, bank.shape[0] // banks
    keys_each = picks * span
    bf16, f32 = jnp.bfloat16, jnp.float32
    vmem, smem = pl.BlockSpec(memory_space=pltpu.VMEM), pl.BlockSpec(memory_space=pltpu.SMEM)
    shape = jax.ShapeDtypeStruct
    scratch = pltpu.VMEM
    row_slabs = shape((slabs, length, TILE), bf16)
    rows = shape((length, width), bf16)
    anywhere = pl.BlockSpec(memory_space=pl.ANY)
    chunks = 2 * units // n_c
    return pl.pallas_call(
        partial(chain_kernel, at, chunk, banks, n_s, n_c),
        out_shape=(
            rows, rows, rows,
            row_slabs, row_slabs, row_slabs,
            shape((slabs, stretches * keys_each, TILE), bf16), shape((slabs, stretches * keys_each, TILE), bf16),
            shape((length, width), f32), rows, shape((length, width), f32),
            shape((16, width), f32), shape((units // 2, 1, 2 * TILE), f32), shape((slabs, 1, TILE), f32),
            shape((chunks, width, TILE), bf16),
        ),
        in_specs=[smem] + [vmem] * 3 + [anywhere] * 2 + [vmem] * 5 + [anywhere],
        out_specs=(vmem,) * 15,
        scratch_shapes=[
            scratch((slabs, banks, span, TILE), bf16), scratch((slabs, banks, span, TILE), bf16),
            scratch((length, width), f32), scratch((length, width), f32),
            scratch((slabs, stretches, 2 * stretch, keys_each), f32),
            scratch((slabs, length, TILE), bf16), scratch((slabs, length, TILE), bf16),
            scratch((4, length, width), bf16), scratch((4, length, width), bf16),
            pltpu.SemaphoreType.DMA((4, length // chunk)), pltpu.SemaphoreType.DMA((4, length // chunk)),
            scratch((shard.shape[0], width, TILE), bf16), pltpu.SemaphoreType.DMA((2,)),
            scratch((length, width), bf16),
            scratch((units, length, TILE), bf16), scratch((units, length, TILE), bf16),
            scratch(bank.shape, bf16), pltpu.SemaphoreType.DMA,
            *gather_semaphores((shard.shape[0] - w_front.shape[0]) // n_c, n_s, n_c),
            *cross_scratch(chunks, width, n_s, n_c),
        ],
        compiler_params=pltpu.CompilerParams(collective_id=2, has_side_effects=True, vmem_limit_bytes=63 << 20),
        name="chain",
    )(ids, att, tok, cot, bank, shard, gains, shifts, bias, out_bias, up_bias, w_front)


def bank_kernel(span, at, ids, dks, dvs, w_all, mg, mine, send, head_sums, acc, w, ws):
    t = lax.axis_index("tp")
    f32, bf16 = jnp.float32, jnp.bfloat16
    slabs = dks.shape[0]
    picks, stretches = ids.shape
    acc[...] = jnp.zeros_like(acc)
    w_copy = pltpu.make_async_copy(w_all.at[pl.ds(at, 2 * slabs)], w, ws)
    w_copy.start()

    def add(i, carry):
        st, n = lax.div(i, picks), lax.rem(i, picks)
        rows = rows_at(ids[n, st], span)
        source = rows_at(i, span)
        for p in range(slabs):
            acc[p, rows, :] = acc[p, rows, :] + dks[p, source, :].astype(f32)
            acc[slabs + p, rows, :] = acc[slabs + p, rows, :] + dvs[p, source, :].astype(f32)
        return carry

    lax.fori_loop(0, stretches * picks, add, 0)
    half = mine.shape[1]
    w_copy.wait()
    total = jnp.zeros((1, slabs * TILE), f32)

    def one(i, sums):
        rows = rows_at(i, BLOCK)
        for p in range(2 * slabs):
            mg[p, rows, :] = acc[p, rows, :].astype(bf16)
        left = jnp.concatenate([mg[p, rows, :] for p in range(2 * slabs)], axis=1)
        for which, target in ((t, mine), (1 - t, send)):
            cols = pl.ds(pl.multiple_of(which * half, half), half)
            weight = jnp.concatenate([w[p, cols, :] for p in range(2 * slabs)], axis=1)
            target[rows, :] = dot_nt(left, weight).astype(target.dtype)
        return sums + jnp.sum(left[:, slabs * TILE :].astype(f32), axis=0, keepdims=True)

    total = lax.fori_loop(0, mine.shape[0] // BLOCK, one, total)
    for p in range(slabs):
        head_sums[p] = total[:, p * TILE : (p + 1) * TILE]


def bank_back(ids, dks, dvs, w, at, banks, span):
    slabs = dks.shape[0]
    rows, half = banks * span, w.shape[1] // 2
    bf16, f32 = jnp.bfloat16, jnp.float32
    vmem, smem = pl.BlockSpec(memory_space=pltpu.VMEM), pl.BlockSpec(memory_space=pltpu.SMEM)
    shape = jax.ShapeDtypeStruct
    return pl.pallas_call(
        partial(bank_kernel, span, at),
        out_shape=(
            shape((2 * slabs, rows, TILE), bf16), shape((rows, half), bf16),
            shape((rows, half), bf16), shape((slabs, 1, TILE), f32),
        ),
        in_specs=[smem, vmem, vmem, pl.BlockSpec(memory_space=pl.ANY)],
        out_specs=(vmem,) * 4,
        scratch_shapes=[
            pltpu.VMEM((2 * slabs, rows, TILE), f32), pltpu.VMEM((2 * slabs, w.shape[1], TILE), bf16),
            pltpu.SemaphoreType.DMA,
        ],
        compiler_params=pltpu.CompilerParams(vmem_limit_bytes=62 << 20),
        name="bank_back",
    )(ids, dks, dvs, w)


def tail_kernel(
    n_s, n_c, groups, early,
    q, k_far, v_far, up, att, lse, tok, gains, shifts, w_all, down_part, small_in, out_bias, gfirst, second, bank, bank_send, fl, n2, sl, mg, gcq, mx, hidden,
    gtok, result, res, res_hidden, small_out, bank_in,
    dk, dv, qm, um, lse_t, delta_t, dq_acc, dq, gk, gv, n1, core_in, x_in, tx, rx, rx_part, stage32, w,
    k, v, bank_here, totals, sm_mine, sm_core, sm_x, sm_z,
    cs, cr, xs, xr, ts, tr, ds_, ms, mr, ps, pr, es, ws, ns, nr, kvs, *engine
):
    f32, bf16 = jnp.float32, jnp.bfloat16
    place = Place(n_s, n_c)
    s, c, x, core, n_x = place.s, place.c, place.x, place.core, place.n_x
    sibling, peer = place.sibling, place.peer
    slabs, length, unused = q.shape
    width = tok.shape[1]
    per = length // BLOCK
    scale = HEAD_DIM ** (-0.5)
    place.greet()
    cross = Cross(place, totals, engine[:7])
    spread = Spread(place, totals, res, engine[7:14])
    extra = Spread(place, hidden, res_hidden, engine[14:])
    chunks = cross.chunks
    bank_copy = pltpu.make_async_copy(bank, bank_here, ds_)
    bank_copy.start()
    kv_copies = [pltpu.make_async_copy(far, here, kvs.at[i]) for i, (far, here) in enumerate(((k_far, k), (v_far, v)))]
    kv_copies[0].start()
    kv_copies[1].start()

    def send_hidden(kk, carry):
        extra.send(kk)
        return carry

    lax.fori_loop(0, extra.chunks, send_hidden, 0)
    part_copy = remote(down_part, rx_part, ps, pr, peer)
    neighbour_copy = remote(bank_send, bank_in, ns, nr, peer)
    neighbour_copy.start()
    w_copy = pltpu.make_async_copy(w_all.at[pl.ds(0, 3 * slabs)], w, ws)
    w_copy.start()

    def staged(source, r):
        return pltpu.make_async_copy(source.at[rows_at(r, BLOCK), :], stage32.at[r], es.at[r])

    for r in range(per):
        staged(gfirst, r).start()

    def owner_rows(index):
        return pl.ds(pl.multiple_of(index * length, length), length)

    def left_of(name):
        return {"self_in": n1, "memory": bank_here, "self_out": fl, "cross_q": n2, "cross_out": sl}[name]

    def slab_of(name, index):
        if name == "self_in":
            return (dq, gk, gv)[index // slabs][index % slabs]
        return {"memory": mg, "self_out": att, "cross_q": gcq, "cross_out": mx}[name][index]

    order = [(name, index) for name, count in groups for index in range(count)]

    def produce(kk):
        if any(order[kk * n_c + i] == ("memory", 0) for i in range(n_c)):
            bank_copy.wait()
        produce_group(cross, order, kk, left_of, slab_of)

    def loop(low, high, action):
        def run(i, carry):
            action(i)
            return carry

        lax.fori_loop(low, high, run, 0)

    def produce_some(i, low, high):
        for kk in range(low, high):
            pl.when(i == kk)(partial(produce, kk))

    def sum_and_send(kk):
        cross.stage_c(kk)
        spread.send(kk)


    low_all = half_masks((length, TILE))
    lse_t[...] = lse[...].T
    dq_acc[...] = jnp.zeros_like(dq_acc)

    def prepare(p, carry):
        for half in (0, 1):
            qm[p, half] = keep_half(q[p], low_all, half)
            um[p, half] = keep_half(up[p], low_all, half)
        prod = (up[p].astype(f32) * att[p].astype(f32)).T
        for half in (0, 1):
            delta_t[p, half] = jnp.sum(prod[half * HEAD_DIM : (half + 1) * HEAD_DIM, :], axis=0, keepdims=True)
        return carry

    loop(0, early, lambda i: produce_some(i, 0, early))
    kv_copies[0].wait()
    kv_copies[1].wait()
    lax.fori_loop(0, slabs, prepare, 0)

    def to_core(xo, part, p):
        theirs = owner_rows(xo * 2 + 1 - core)
        source = (dk if part == 0 else dv).at[p, theirs, :]
        return remote(source, core_in.at[xo, part, p], cs.at[xo, part, p], cr.at[xo, part, p], sibling)

    def to_owner(xo, part, p):
        d = x - xo
        return remote(
            core_in.at[xo, part, p], x_in.at[d - 1, part, p], xs.at[xo, part, p], xr.at[d - 1, part, p],
            {"ctx": xo * 2 + core},
        )

    def from_higher(d, part, p):
        here = x_in.at[d - 1, part, p]
        return remote(here, here, xs.at[0, part, p], xr.at[d - 1, part, p], sibling)

    def relay(xo, p):
        mine = owner_rows(xo * 2 + core)
        for part, source in ((0, dk), (1, dv)):
            to_core(xo, part, p).wait_recv()
            core_in[xo, part, p] = source[p, mine, :] + core_in[xo, part, p]
            to_owner(xo, part, p).start()

    points = (x + 1) * slabs

    def key_block(p, spot, size, begin):
        keys, values = k[p, spot, :], v[p, spot, :]
        low_keys = half_masks((size, TILE))
        dk_sum = dv_sum = jnp.zeros((size, TILE), f32)
        back = jnp.zeros((length - begin, TILE), f32)
        for half in (0, 1):
            q_half, u_half = qm[p, half, begin:, :], um[p, half, begin:, :]
            score = dot_nt(keys, q_half) * (scale * LOG2E)
            probs = jnp.exp2(score - lse_t[pl.ds(p * 2 + half, 1), begin:])
            grad = dot_nt(values, u_half)
            slope = (probs * (grad - delta_t[p, half, :, begin:])).astype(bf16)
            dv_sum = dv_sum + dot_nn(probs.astype(bf16), u_half)
            dk_sum = dk_sum + dot_nn(slope, q_half)
            back = back + dot_tn(slope, keep_half(keys, low_keys, half))
        dq_acc[p, begin:, :] = dq_acc[p, begin:, :] + back
        dk[p, spot, :] = (dk_sum * scale).astype(bf16)
        dv[p, spot, :] = dv_sum.astype(bf16)

    def chip(xo, carry):
        def one(p, inner):
            def whole(j, deeper):
                key_block(p, rows_at(j, length), length, 0)
                return deeper

            lax.fori_loop(xo * 2, lax.min(xo * 2 + 2, c), whole, 0)

            @pl.when(xo == x)
            def _():
                for begin in range(0, length, BLOCK):
                    key_block(p, pl.ds(pl.multiple_of(c * length + begin, BLOCK), BLOCK), BLOCK, begin)

            @pl.when((xo < x) | (core == 1))
            def _():
                to_core(xo, 0, p).start()
                to_core(xo, 1, p).start()

            pl.when((p > 0) & (xo < x))(lambda: relay(xo, p - 1))
            pl.when((p == 0) & (xo > 0))(lambda: relay(xo - 1, slabs - 1))
            point = xo * slabs + p

            pl.when(point == 0)(lambda: loop(0, early, cross.stage_b))
            return inner

        lax.fori_loop(0, slabs, one, 0)

        return carry

    lax.fori_loop(0, x + 1, chip, 0)

    for p in range(slabs):
        dq[p] = (dq_acc[p] * scale).astype(bf16)

    loop(0, extra.chunks, extra.stage_d)
    loop(0, early, sum_and_send)

    def norm_tile(i, carry):
        at = rows_at(i, TILE)
        n1[at, :] = norm_rows(tok[at, :].astype(f32), gains[0:1, :], shifts[0:1, :])
        return carry

    lax.fori_loop(0, length // TILE, norm_tile, 0)
    loop(0, extra.chunks, extra.stage_e)
    own = owner_rows(c)

    @pl.when(core == 0)
    def _():
        for p in range(slabs):
            to_core(x, 0, p).wait_recv()
            to_core(x, 1, p).wait_recv()

    for d in range(1, n_x):

        @pl.when(x + d < n_x)
        def _():
            for p in range(slabs):
                from_higher(d, 0, p).wait_recv()
                from_higher(d, 1, p).wait_recv()

    for part, target in ((0, gk), (1, gv)):
        dq_acc[...] = (dk if part == 0 else dv)[:, own, :].astype(f32)

        @pl.when(core == 0)
        def _():
            dq_acc[...] = dq_acc[...] + core_in[x, part].astype(f32)

        for d in range(1, n_x):

            @pl.when(x + d < n_x)
            def _():
                dq_acc[...] = dq_acc[...] + x_in[d - 1, part].astype(f32)

        target[...] = dq_acc[...].astype(bf16)

    def exchange(r):
        at = rows_at(r, BLOCK)
        return remote(tx.at[at, :], rx.at[at, :], ts.at[r], tr.at[r], peer)

    w_copy.wait()

    def product(r, carry):
        at = rows_at(r, BLOCK)
        left = jnp.concatenate([ref[i, at, :] for ref in (dq, gk, gv) for i in range(slabs)], axis=1)

        def run(n, inner):
            cols = pl.ds(pl.multiple_of(n * 256, 256), 256)
            weight = jnp.concatenate([w[i, cols, :] for i in range(3 * slabs)], axis=1)
            tx[at, cols] = dot_nt(left, weight).astype(bf16)
            return inner

        lax.fori_loop(0, width // 256, run, 0)
        exchange(r).start()
        return carry

    lax.fori_loop(0, per, product, 0)

    part_copy.start()
    loop(early, chunks, lambda i: produce_some(i, early, chunks))
    loop(0, extra.chunks, extra.stage_f)
    loop(early, chunks, cross.stage_b)
    sm_mine[...] = small_in[...]
    for index, source in ((0, dq), (1, gv)):
        for p in range(slabs):
            lanes = slice((index * slabs + p) * TILE, (index * slabs + p + 1) * TILE)
            sm_mine[9:10, lanes] = jnp.sum(source[p].astype(f32), axis=0, keepdims=True)

    loop(early, chunks, sum_and_send)

    def last_rows(r, carry):
        exchange(r).wait_recv()
        staged(gfirst, r).wait()

        def tile(i, inner):
            at = pl.ds(pl.multiple_of(r * BLOCK + i * TILE, TILE), TILE)
            spot, rate = norm_parts(tok[at, :].astype(f32))
            upstream = tx[at, :].astype(f32) + rx[at, :].astype(f32)
            scaled = upstream * gains[0:1, :]
            sm_mine[0:1, :] = sm_mine[0:1, :] + jnp.sum(upstream * spot, axis=0, keepdims=True)
            sm_mine[3:4, :] = sm_mine[3:4, :] + jnp.sum(upstream, axis=0, keepdims=True)
            gtok[at, :] = stage32[r, rows_at(i, TILE), :] + rate * (
                scaled - jnp.mean(scaled, axis=-1, keepdims=True)
                - spot * jnp.mean(scaled * spot, axis=-1, keepdims=True)
            )
            return inner

        lax.fori_loop(0, BLOCK // TILE, tile, 0)
        staged(second, r).start()
        return carry

    lax.fori_loop(0, per, last_rows, 0)
    sm_send = remote(sm_mine, sm_core, ms.at[0], mr.at[0], sibling)

    def sm_x_copy(d):
        return remote(sm_x.at[x], sm_x.at[x], ms.at[d], mr.at[d], {"ctx": lax.rem(x + d, n_x) * 2 + core})

    def sm_x_in(d):
        here = sm_x.at[lax.rem(x - d + n_x, n_x)]
        return remote(here, here, ms.at[d], mr.at[d], sibling)

    def sm_z_copy(d):
        return remote(sm_z.at[s], sm_z.at[s], ms.at[n_x + d - 1], mr.at[n_x + d - 1], {"shard": lax.rem(s + d, n_s)})

    def sm_z_in(d):
        here = sm_z.at[lax.rem(s - d + n_s, n_s)]
        return remote(here, here, ms.at[n_x + d - 1], mr.at[n_x + d - 1], peer)

    sm_send.start()

    loop(0, early, spread.stage_d)
    sm_send.wait_recv()
    sm_x[x] = sm_mine[...] + sm_core[...]
    for d in range(1, n_x):
        sm_x_copy(d).start()
    loop(0, early, spread.stage_e)
    for d in range(1, n_x):
        sm_x_in(d).wait_recv()
    both = sm_x[0]
    for e in range(1, n_x):
        both = both + sm_x[e]
    sm_z[s] = both
    for d in range(1, n_s):
        sm_z_copy(d).start()
    loop(0, early, spread.stage_f)
    loop(early, chunks, spread.stage_d)
    loop(early, chunks, spread.stage_e)
    part_copy.wait_recv()

    def result_rows(r, carry):
        staged(second, r).wait()

        def tile(i, inner):
            at = pl.ds(pl.multiple_of(r * BLOCK + i * TILE, TILE), TILE)
            both = down_part[at, :].astype(f32) + rx_part[at, :].astype(f32)
            result[at, :] = (stage32[r, rows_at(i, TILE), :] + both + out_bias[2:3, :]).astype(bf16)
            return inner

        lax.fori_loop(0, BLOCK // TILE, tile, 0)
        return carry

    lax.fori_loop(0, per, result_rows, 0)

    for d in range(1, n_s):
        sm_z_in(d).wait_recv()
    both = sm_z[0]
    for e in range(1, n_s):
        both = both + sm_z[e]
    small_out[...] = both
    loop(early, chunks, spread.stage_f)
    part_copy.wait_send()
    neighbour_copy.wait()
    sm_send.wait_send()
    for d in range(1, n_x):
        sm_x_copy(d).wait_send()
    for d in range(1, n_s):
        sm_z_copy(d).wait_send()

    def settle(xo, carry):
        @pl.when((xo < x) | (core == 1))
        def _():
            for p in range(slabs):
                to_core(xo, 0, p).wait_send()
                to_core(xo, 1, p).wait_send()

        @pl.when(xo < x)
        def _():
            for p in range(slabs):
                to_owner(xo, 0, p).wait_send()
                to_owner(xo, 1, p).wait_send()

        return carry

    lax.fori_loop(0, x + 1, settle, 0)

    def settle_tp(r, carry):
        exchange(r).wait_send()
        return carry

    lax.fori_loop(0, per, settle_tp, 0)

    cross.finish()
    spread.finish()
    extra.finish()


def tail(groups, n_s, n_c, hidden, q, k, v, up, att, lse, tok, gains, shifts, w, part, small, out_bias, gfirst, second, bank, bank_send, *grad_inputs):
    slabs, length, unused = q.shape
    width = tok.shape[1]
    n_x = n_c // 2
    bf16, f32 = jnp.bfloat16, jnp.float32
    vmem, anywhere = pl.BlockSpec(memory_space=pltpu.VMEM), pl.BlockSpec(memory_space=pl.ANY)
    shape, scratch, dma = jax.ShapeDtypeStruct, pltpu.VMEM, pltpu.SemaphoreType.DMA
    pair = (2, slabs, length, TILE)
    total = sum(count for name, count in groups)
    chunks, rows = total // n_c, width // n_s
    early = (total - groups[-1][1]) // n_c
    return pl.pallas_call(
        partial(tail_kernel, n_s, n_c, groups, early),
        out_shape=(
            shape((length, width), f32), shape((length, width), bf16),
            shape((rows, total * TILE), bf16), shape((rows, hidden.shape[0] * n_c * TILE), bf16),
            shape(small.shape, f32), shape(bank_send.shape, bf16),
        ),
        in_specs=[vmem, anywhere, anywhere] + [vmem] * 6
        + [anywhere]
        + [vmem] * 3 + [anywhere] * 4 + [vmem] * (len(grad_inputs) + 1),
        out_specs=(vmem,) * 5 + (anywhere,),
        scratch_shapes=[
            scratch(k.shape, bf16), scratch(k.shape, bf16),
            scratch((slabs, 2, length, TILE), bf16), scratch((slabs, 2, length, TILE), bf16),
            scratch((TILE, length), f32), scratch((slabs, 2, 1, length), f32), scratch(q.shape, f32),
            scratch(q.shape, bf16), scratch(q.shape, bf16), scratch(q.shape, bf16),
            scratch((length, width), bf16),
            scratch((n_x,) + pair, bf16), scratch((n_x - 1,) + pair, bf16),
            scratch((length, width), bf16), scratch((length, width), bf16),
            scratch((length, width), bf16), scratch((length // BLOCK, BLOCK, width), f32),
            scratch((3 * slabs, width, TILE), bf16),
            scratch(k.shape, bf16), scratch(k.shape, bf16),
            scratch(bank.shape, bf16), scratch((chunks, width, TILE), bf16),
            scratch(small.shape, f32), scratch(small.shape, f32),
            scratch((n_x,) + small.shape, f32), scratch((n_s,) + small.shape, f32),
            dma((n_x, 2, slabs)), dma((n_x, 2, slabs)), dma((n_x - 1, 2, slabs)), dma((n_x - 1, 2, slabs)),
            dma((length // BLOCK,)), dma((length // BLOCK,)), dma,
            dma((n_x + n_s - 1,)), dma((n_x + n_s - 1,)),
            dma, dma, dma((length // BLOCK,)), dma, dma, dma, dma((2,)),
            *cross_scratch(chunks, width, n_s, n_c),
            *spread_scratch(chunks, width, n_s, n_c),
            *spread_scratch(hidden.shape[0], width, n_s, n_c),
        ],
        compiler_params=pltpu.CompilerParams(collective_id=3, has_side_effects=True, vmem_limit_bytes=64 << 20),
        name="tail",
    )(q, k, v, up, att, lse, tok, gains, shifts, w, part, small, out_bias, gfirst, second, bank, bank_send, *grad_inputs, hidden)


def final_kernel(
    slabs, units, res, hidden, mine, received, small,
    neigh, gains, shifts, head, outs, up_bias, self_in, self_out, cross_q, memory, cross_out, up, down,
):
    f32 = jnp.float32
    neigh[...] = mine[...].astype(f32) + received[...].astype(f32)
    local = slabs * TILE
    at = 0
    for j in range(2):
        memory[:, j, :] = res[:, (at + j * slabs) * TILE : (at + (j + 1) * slabs) * TILE].astype(f32)
    at += 2 * slabs
    self_out[...] = res[:, at * TILE : (at + slabs) * TILE].astype(f32)
    at += slabs
    cross_q[...] = res[:, at * TILE : (at + slabs) * TILE].astype(f32)
    at += slabs
    cross_out[...] = res[:, at * TILE : (at + slabs) * TILE].astype(f32)
    at += slabs
    for j in range(3):
        self_in[j] = res[:, (at + j * slabs) * TILE : (at + (j + 1) * slabs) * TILE].astype(f32)
    up[...] = hidden[:, : units * TILE].astype(f32)
    down[...] = hidden[:, units * TILE :].astype(f32)
    gains[...] = small[0:3, :]
    shifts[...] = small[3:6, :]
    outs[...] = small[6:9, :]
    width = small.shape[1]
    for j in range(4):
        head[j : j + 1, :] = small[9 + j // 2 : 10 + j // 2, (j % 2) * local : (j % 2 + 1) * local]
    for j in range(units * TILE // width):
        up_bias[:, j * width : (j + 1) * width] = small[11 + j : 12 + j, :]


def final(slabs, units, res, hidden, mine, received, small):
    f32 = jnp.float32
    shape = jax.ShapeDtypeStruct
    rows, local, width = res.shape[0], slabs * TILE, small.shape[1]
    out_shape = (
        shape(mine.shape, f32), shape((3, width), f32), shape((3, width), f32), shape((4, local), f32),
        shape((3, width), f32), shape((1, units * TILE), f32),
        shape((3, rows, local), f32), shape((rows, local), f32), shape((rows, local), f32),
        shape((rows, 2, local), f32), shape((rows, local), f32),
        shape((rows, units * TILE), f32), shape((rows, units * TILE), f32),
    )

    vmem = pl.BlockSpec(memory_space=pltpu.VMEM)
    return pl.pallas_call(
        partial(final_kernel, slabs, units),
        out_shape=out_shape,
        in_specs=[vmem] * 5,
        out_specs=(vmem,) * len(out_shape),
        compiler_params=pltpu.CompilerParams(vmem_limit_bytes=60 << 20),
        name="final",
    )(res, hidden, mine, received, small)


def slabbed(matrix):
    rows, columns = matrix.shape
    return matrix.reshape(rows, columns // TILE, TILE).transpose(1, 0, 2)


def shards(
    tokens,
    cotangent,
    neighbours,
    neighbour_ids,
    norm_gains,
    norm_shifts,
    head_bias,
    out_bias,
    up_bias,
    self_input,
    self_output,
    cross_query,
    cross_memory,
    cross_output,
    hidden_up,
    hidden_down,
):
    n_s, n_c = lax.axis_size("shard"), lax.axis_size("ctx")
    slice_rows = self_input.shape[0]
    shard = slabbed(
        jnp.concatenate(
            [
                self_input.reshape(slice_rows, -1),
                self_output.T,
                cross_memory.reshape(slice_rows, -1),
                cross_query,
                cross_output.T,
                hidden_up,
                hidden_down.T,
            ],
            axis=1,
        )
    )
    tok, cot = tokens[0], cotangent[0]
    length, width = tok.shape
    local = self_output.shape[0]
    slabs, units = local // TILE, hidden_up.shape[1] // TILE
    counts = (3 * slabs, slabs, 2 * slabs, slabs, slabs, units, units)
    names = ("self_in", "self_out", "memory", "cross_q", "cross_out", "up", "down")
    at, edge = {}, 0
    for name, count in zip(names, counts):
        at[name] = edge
        edge += count
    bank_shape = neighbours.shape[1:]
    bank = neighbours.reshape(bank_shape[0] * bank_shape[1], width)
    ids = neighbour_ids[0].T
    cut = at["up"]
    weights, q, k, v, att, lse = front(shard, tok, norm_gains, norm_shifts, head_bias, n_s, n_c, cut)
    n2, sl, fl, mx, gcq, ga, dks, dvs, gfirst, part, second, sums, up_sums, head_cross, hidden = chain(
        at, ids, att, tok, cot, bank, shard, norm_gains, norm_shifts, head_bias, out_bias, up_bias[None], weights,
        bank_shape[0], BLOCK, n_s, n_c,
    )
    mg, mine, send, head_memory = bank_back(
        ids, dks, dvs, weights, at["memory"], bank_shape[0], bank_shape[1]
    )
    small = jnp.concatenate(
        [
            sums[:9],
            jnp.zeros((1, width), jnp.float32),
            jnp.concatenate([head_cross, head_memory]).reshape(1, width),
            up_sums.reshape(-1, width),
        ]
    )
    small = jnp.pad(small, ((0, 16 - small.shape[0]), (0, 0)))
    lengths = dict(zip(names, counts))
    groups = [(name, lengths[name]) for name in ("memory", "self_out", "cross_q", "cross_out", "self_in")]
    grad_tokens, result, grads, hidden_grads, small, received = tail(
        groups, n_s, n_c, hidden, q, k, v, ga, att, lse, tok, norm_gains, norm_shifts, weights, part, small, out_bias, gfirst, second,
        bank, send, fl, n2, sl, mg, gcq, mx,
    )
    (
        neigh, gains, shifts, head, outs, bias_up, self_in, self_out, cross_q, memory, cross_out, up, down,
    ) = final(slabs, units, grads, hidden_grads, mine, received, small)
    return (
        result[None],
        grad_tokens[None],
        neigh.reshape((1,) + bank_shape[:2] + (width // 2,)),
        gains,
        shifts,
        head,
        outs,
        bias_up.reshape(-1),
        self_in.transpose(1, 0, 2),
        self_out.T,
        cross_q,
        memory,
        cross_out.T,
        up,
        down.T,
    )


def solution(mesh):
    placed = (
        P("shard", "ctx", None),
        P("shard", "ctx", None),
        P("shard", "ctx", None, None),
        P("shard", "ctx", None),
        P(),
        P(),
        P(None, "tp"),
        P(),
        P("tp"),
        P("shard", None, "tp"),
        P("tp", "shard"),
        P("shard", "tp"),
        P("shard", None, "tp"),
        P("tp", "shard"),
        P("shard", "tp"),
        P("tp", "shard"),
    )
    return jax.shard_map(
        shards,
        mesh=mesh,
        in_specs=placed,
        out_specs=(
            P("shard", "ctx", None),
            P("shard", "ctx", None),
            P("shard", "ctx", None, "tp"),
            P(),
            P(),
            P(None, "tp"),
            P(),
            P("tp"),
            P("shard", None, "tp"),
            P("tp", "shard"),
            P("shard", "tp"),
            P("shard", None, "tp"),
            P("tp", "shard"),
            P("shard", "tp"),
            P("tp", "shard"),
        ),
        check_vma=False,
    )
```
